256 devices in a mesh: seq: 32 (over y_hi, z, core), head: 8 (over y_lo, x).
Axes of the slice: x: 4, y: 4 (y_hi: 2, y_lo: 2; y = y_hi * 2 + y_lo), z: 8, core: 2. Of those that a mesh axis runs over, the one named last changes fastest.
Arguments:
- queries: bfloat16 [4096, 8192], P('seq', 'head'), may hold values from -190 to 190
- key_vectors: bfloat16 [4096, 1024], P('seq', 'head'), may hold values from -6.1 to 6.1
- value_vectors: bfloat16 [4096, 1024], P('seq', 'head'), may hold values from -54 to 54
- log_gate: float32 [64, 4096], P('head', 'seq'), may hold values from -1 to 0, as said below
- query_map: float32 [64, 128, 128], P('head'), may hold values from -0.5 to 0.5
- key_map: float32 [64, 128, 128], P('head'), may hold values from -0.5 to 0.5
- level_weight: float32 [64, 13], P('head'), may hold values from 0.25 to 2
- norm_gain: float32 [8192], P('head'), may hold values from 0.5 to 1.5
Outputs:
- grad_query_map: float32 [64, 128, 128], P('head')
- grad_key_map: float32 [64, 128, 128], P('head')
- grad_level_weight: float32 [64, 13], P('head')
- grad_norm_gain: float32 [8192], P('head')
The draws below stay inside these ranges and needn't reach their ends.
Inputs may be any that keep to these rules, and one draw needn't show every extreme that they name: `log_gate`: every entry is negative.
All inputs are finite; a program needn't handle non-finite values.
Results may differ from the reference program's by a relative error of at most 0.0015.
Values may be sent and summed in bfloat16 or wider, within the bound.
A program may use at most 128 MiB of HBM per device.

```python
import math
import jax
import jax.numpy as jnp
from jax import lax

HD = 128
GROUP = 8
TOK_DEV = 128
KV_HEADS = 8
QUERY_HEAD_COUNT = 64
TOKENS = 4096
LEVELS = 13


def drawn_pair(key):
    base = jax.random.fold_in(key, 17)
    first, second = jax.random.split(base, 2)
    key_rows = jax.random.truncated_normal(first, -6.0, 6.0, (TOKENS, KV_HEADS, HD), jnp.float32)
    query_rows = jax.random.truncated_normal(second, -6.0, 6.0, (TOKENS, KV_HEADS, GROUP, HD), jnp.float32)
    return (query_rows.reshape(TOKENS, KV_HEADS * GROUP * HD), key_rows.reshape(TOKENS, KV_HEADS * HD))


def draw_queries(key, part):
    return drawn_pair(key)[0].astype(jnp.bfloat16)


def draw_key_vectors(key, part):
    return drawn_pair(key)[1].astype(jnp.bfloat16)


def draw_value_vectors(key, part):
    base = jax.random.fold_in(key, 23)
    value_rows = jax.random.truncated_normal(base, -6.0, 6.0, (TOKENS, KV_HEADS, HD), jnp.float32)
    ramp = jnp.arange(KV_HEADS).astype(jnp.float32) / max(KV_HEADS - 1, 1)
    head_scale = 1.0 + 2.0 * ramp
    return (value_rows * head_scale[None, :, None]).reshape(TOKENS, KV_HEADS * HD).astype(jnp.bfloat16)


def draw_log_gate(key, part):
    base = jax.random.fold_in(key, 31)
    component_listing = jax.random.split(base, 7)
    head_draw = jax.random.uniform(component_listing[0], (QUERY_HEAD_COUNT,), jnp.float32)
    fast_share = 0.5
    is_fast = head_draw < fast_share
    fast_rate = jnp.exp(jax.random.uniform(component_listing[1], (QUERY_HEAD_COUNT,), jnp.float32, math.log(1.0 / 50.0), math.log(1.0 / 30.0)))
    slow_rate = jnp.exp(jax.random.uniform(component_listing[2], (QUERY_HEAD_COUNT,), jnp.float32, math.log(0.2), math.log(0.6))) / TOKENS
    head_frequency = jnp.where(is_fast, fast_rate, slow_rate)
    extent_multiplier = jnp.exp(jax.random.uniform(component_listing[3], (QUERY_HEAD_COUNT, TOKENS // TOK_DEV), jnp.float32, math.log(0.5), math.log(2.0)))
    extent_multiplier = jnp.repeat(extent_multiplier, TOK_DEV, axis=1)
    jaggedness = jax.random.uniform(component_listing[4], (QUERY_HEAD_COUNT, TOKENS), jnp.float32, 0.5, 1.5)
    spots = jax.random.randint(component_listing[5], (3,), 0, TOKENS)
    cluster_depth = jax.random.uniform(component_listing[6], (3, QUERY_HEAD_COUNT), jnp.float32, 0.22, 0.4)
    positions = jnp.arange(TOKENS)
    match_total = (positions[None, :] == spots[:, None]).astype(jnp.float32)
    clusters_drawn = jnp.einsum('mv,ml->vl', cluster_depth, match_total)
    return -(head_frequency[:, None] * extent_multiplier * jaggedness) - clusters_drawn


def levels(rng, extent, cuts, low, high):
    loudness = 1.0
    for dim, shards_of in cuts:
        heights = jax.random.uniform(jax.random.fold_in(jax.random.fold_in(rng, 6), dim), (shards_of,), jnp.float32, low / len(cuts), high / len(cuts))
        loudness = loudness * jnp.repeat(jnp.exp(heights), extent[dim] // shards_of).reshape((-1,) + (1,) * (len(extent) - 1 - dim))
    return loudness


def gaussian(own_key, extent, deviation, bound, cuts=(), held_as=jnp.bfloat16):
    factor_of = levels(own_key, extent, cuts, -0.22, 0.18) if cuts else 1.0
    result = jax.random.normal(own_key, extent, jnp.float32) * deviation * factor_of
    return jnp.minimum(jnp.maximum(result, -bound), bound).astype(held_as)


def setup_inputs(seed: int = 0) -> dict:
    keys = jax.random.split(jax.random.key(seed), 9)
    return {
        "queries": draw_queries(jax.random.fold_in(keys[8], 71), 0),
        "key_vectors": draw_key_vectors(jax.random.fold_in(keys[8], 71), 0),
        "value_vectors": draw_value_vectors(jax.random.fold_in(keys[8], 71), 0),
        "log_gate": draw_log_gate(jax.random.fold_in(keys[8], 71), 0),
        "query_map": gaussian(keys[4], (QUERY_HEAD_COUNT, HD, HD), HD ** -0.5, 0.5, ((0, 8),), jnp.float32),
        "key_map": gaussian(keys[5], (QUERY_HEAD_COUNT, HD, HD), HD ** -0.5, 0.5, ((0, 8),), jnp.float32),
        "level_weight": jnp.clip(jnp.exp(math.log(2.0) - 2.0794415 * jax.random.uniform(keys[6], (QUERY_HEAD_COUNT, LEVELS), jnp.float32) ** levels(keys[6], (QUERY_HEAD_COUNT, LEVELS), ((0, 8),), -0.2, 0.2)), 0.25, 2.0),
        "norm_gain": jnp.clip(1.0 + 0.1 * jax.random.normal(keys[7], (QUERY_HEAD_COUNT * HD,), jnp.float32), 0.5, 1.5),
    }


HIGHEST = lax.Precision.HIGHEST
EPSILON = 1e-05

def bit_length(numbers, bit_count):
    digits = jnp.zeros_like(numbers)
    for bit_power in range(bit_count):
        digits = digits + (numbers >= 1 << bit_power).astype(jnp.int32)
    return digits

def teacher(query_rows, key_rows, value_rows):
    score_scale = HD ** (-0.5)
    positions = jnp.arange(TOKENS, dtype=jnp.int32)
    keys_float = key_rows.astype(jnp.float32)
    values_float = value_rows.astype(jnp.float32)

    def block_out(block_id):
        block_rows = lax.dynamic_slice_in_dim(query_rows, block_id * TOK_DEV, TOK_DEV, 0).astype(jnp.float32)
        scores = jnp.einsum('rgd,kd->grk', block_rows, keys_float, precision=HIGHEST) * score_scale
        own_pos = block_id * TOK_DEV + jnp.arange(TOK_DEV, dtype=jnp.int32)
        scores = jnp.where(positions[None, None, :] <= own_pos[None, :, None], scores, -jnp.inf)
        row_peak = lax.optimization_barrier(jnp.max(scores, axis=2, keepdims=True))
        weights = jnp.exp(scores - row_peak)
        rounded = lax.optimization_barrier(weights.astype(jnp.bfloat16)).astype(jnp.float32)
        weighted = jnp.einsum('grk,kd->grd', rounded, values_float, precision=HIGHEST)
        return weighted / lax.optimization_barrier(jnp.sum(weights, axis=2))[..., None]
    block_outs = lax.map(block_out, jnp.arange(TOKENS // TOK_DEV, dtype=jnp.int32))
    return block_outs.transpose(1, 0, 2, 3).reshape(GROUP, TOKENS, HD)

def student(query_maps, key_maps, level_rows, query_rows, key_rows, value_rows, gate_rows):
    span_total = TOKENS // TOK_DEV
    low_bits = TOK_DEV.bit_length() - 1
    query_float = query_rows.astype(jnp.float32)
    keys_float = key_rows.astype(jnp.float32)
    values_float = value_rows.astype(jnp.float32)
    query_proj = jnp.einsum('tgd,gde->gte', query_float, query_maps, precision=HIGHEST).reshape(GROUP, span_total, TOK_DEV, HD)
    key_proj = jnp.einsum('td,gde->gte', keys_float, key_maps, precision=HIGHEST).reshape(GROUP, span_total, TOK_DEV, HD)
    values_spans = values_float.reshape(span_total, TOK_DEV, HD)
    keys_spans = keys_float.reshape(span_total, TOK_DEV, HD)
    cumulative = jnp.cumsum(gate_rows, axis=1).reshape(GROUP, span_total, TOK_DEV)
    position = jnp.arange(TOK_DEV, dtype=jnp.int32)
    causal = position[None, :] <= position[:, None]
    level_ids = jnp.arange(LEVELS, dtype=jnp.int32)
    local_level = bit_length(jnp.bitwise_xor(position[:, None], position[None, :]), LEVELS)
    local_pick = (local_level[None] == level_ids[:, None, None]).astype(jnp.float32)
    level_mask = jnp.einsum('gl,lrs->grs', level_rows, local_pick, precision=HIGHEST)
    decay_in = jnp.exp(jnp.where(causal[None, None], cumulative[..., :, None] - cumulative[..., None, :], -jnp.inf))
    scores = jnp.einsum('gcre,gcse->gcrs', query_proj, key_proj, precision=HIGHEST)
    local_part = jnp.einsum('gcrs,csd->gcrd', scores * decay_in * level_mask[:, None], values_spans, precision=HIGHEST)
    ending = cumulative[:, :, -1]
    before = jnp.concatenate([jnp.zeros((GROUP, 1), ending.dtype), ending[:, :-1]], axis=1)
    raw_state = jnp.einsum('gcs,csa,csb->gcab', jnp.exp(ending[..., None] - cumulative), keys_spans, values_spans, precision=HIGHEST)
    span_ids = jnp.arange(span_total, dtype=jnp.int32)
    span_level = low_bits + bit_length(jnp.bitwise_xor(span_ids[:, None], span_ids[None, :]), LEVELS)
    span_pick = (span_level[None] == level_ids[:, None, None]).astype(jnp.float32)
    earlier = span_ids[None, :] < span_ids[:, None]
    link_decay = jnp.exp(jnp.where(earlier[None], before[:, :, None] - ending[:, None, :], -jnp.inf))
    coupling = link_decay * jnp.einsum('gl,lcx->gcx', level_rows, span_pick, precision=HIGHEST)
    combined = jnp.einsum('gcx,gxab->gcab', coupling, raw_state, precision=HIGHEST)
    key_state = jnp.einsum('gba,gcbf->gcaf', key_maps, combined, precision=HIGHEST)
    entry_decay = jnp.exp(cumulative - before[..., None])
    far_part = entry_decay[..., None] * jnp.einsum('gcre,gcef->gcrf', query_proj, key_state, precision=HIGHEST)
    return (local_part + far_part).reshape(GROUP, TOKENS, HD)

def reference(queries, key_vectors, value_vectors, log_gate, query_map, key_map, level_weight, norm_gain):
    query_rows = queries.reshape(TOKENS, KV_HEADS, GROUP, HD).transpose(1, 0, 2, 3)
    key_rows = key_vectors.reshape(TOKENS, KV_HEADS, HD).transpose(1, 0, 2)
    value_rows = value_vectors.reshape(TOKENS, KV_HEADS, HD).transpose(1, 0, 2)
    gate_rows = log_gate.reshape(KV_HEADS, GROUP, TOKENS)
    target = lax.map(lambda head_items: teacher(*head_items), (query_rows, key_rows, value_rows))
    checked = jax.checkpoint(student)

    def distill_loss(parameters):
        query_maps, key_maps, level_rows, gain_rows = parameters
        head_outs = lax.map(lambda head_items: checked(*head_items), (query_maps.reshape(KV_HEADS, GROUP, HD, HD), key_maps.reshape(KV_HEADS, GROUP, HD, HD), level_rows.reshape(KV_HEADS, GROUP, LEVELS), query_rows, key_rows, value_rows, gate_rows))
        square_sum = lax.optimization_barrier(jnp.sum(head_outs * head_outs, axis=(0, 1, 3)))
        inverse = lax.rsqrt(square_sum / (QUERY_HEAD_COUNT * HD) + EPSILON)
        normed = head_outs * inverse[None, None, :, None]
        student_out = normed * gain_rows.reshape(KV_HEADS, GROUP, 1, HD)
        mismatch = student_out - target
        return jnp.sum(mismatch * mismatch) / (2.0 * TOKENS)
    grad_query, grad_key, grad_levels, grad_gain = jax.grad(distill_loss)((query_map, key_map, level_weight, norm_gain))
    return (grad_query, grad_key, grad_levels, grad_gain)
```

```python
import functools

import jax
import jax.numpy as jnp
from jax import lax
from jax.experimental import pallas as pl
from jax.experimental.pallas import tpu as pltpu
from jax.sharding import PartitionSpec as P

F32 = jnp.float32
BF = jnp.bfloat16
HIGHEST = lax.Precision.HIGHEST
MESH = pl.DeviceIdType.MESH
NEGATIVE = -1e30
EPSILON = 1e-05
HD = 128
TOK = 128
HEADS = 8
SPANS = 32
LEVELS = 13
LOW = 7
CROSS = 5
TOKENS = TOK * SPANS
WIDTH = 64 * HD
SMALL = 24
CHUNK = HD + SMALL
LOG2E = 1.4426950408889634
SCALE = HD**-0.5 * LOG2E
LIMIT = 58 << 20


def pieces(a):
    high = a.astype(BF)
    return high, (a - high.astype(F32)).astype(BF)


def dg(a, b, ca, cb, precision=None):
    return lax.dot_general(
        a, b, (((ca,), (cb,)), ((), ())), preferred_element_type=F32, precision=precision
    )


def halves(o):
    n = o.shape[1] // 2
    return o[:, :n] + o[:, n:]


def mm(a, b, ca, cb):
    bh, bl = pieces(b)
    left = jnp.concatenate(pieces(a), axis=ca)
    right = jnp.concatenate(
        [jnp.concatenate([bh, bh], axis=cb), jnp.concatenate([bl, bl], axis=cb)], axis=1 - cb
    )
    return halves(dg(left, right, ca, cb))


def mm_left_exact(a, b, ca, cb):
    return halves(dg(a, jnp.concatenate(pieces(b), axis=1 - cb), ca, cb))


def mm_right_exact(a, b, ca, cb):
    return dg(jnp.concatenate(pieces(a), axis=ca), jnp.concatenate([b, b], axis=cb), ca, cb)


def iota(shape, dim):
    return lax.broadcasted_iota(jnp.int32, shape, dim)


def local_levels():
    x = jnp.bitwise_xor(iota((TOK, TOK), 0), iota((TOK, TOK), 1))
    level = jnp.zeros_like(x)
    for bit in range(LOW):
        level = level + (x >= 1 << bit).astype(jnp.int32)
    return level


def rows(h):
    return slice(h * TOK, (h + 1) * TOK)


def make_cumulative(g_all, lc):
    upper = (iota((TOK, TOK), 0) <= iota((TOK, TOK), 1)).astype(F32)
    lc[...] = dg(g_all[...].reshape(SPANS * HEADS, TOK), upper, 1, 0, HIGHEST)


def column_cumulative(gates):
    lower = (iota((TOK, TOK), 1) <= iota((TOK, TOK), 0)).astype(F32)
    return dg(lower, gates, 1, 1, HIGHEST)


def teacher(c, qs, kv, peak, score, total, tgt):
    last = c // 2
    peak[...] = jnp.full_like(peak, NEGATIVE)

    def scored(p, masked):
        keys = kv[0, pl.ds(2 * p, 2)].reshape(2 * TOK, HD)
        for h in range(HEADS):
            s = dg(qs[rows(h)], keys, 1, 1)
            if masked:
                at = 2 * TOK * p + iota((TOK, 2 * TOK), 1)
                s = jnp.where(at <= c * TOK + iota((TOK, 2 * TOK), 0), s, NEGATIVE)
            score[p, rows(h)] = s
            peak[rows(h)] = jnp.maximum(peak[rows(h)], jnp.maximum(s[:, :TOK], s[:, TOK:]))

    def step(p, carry):
        scored(p, False)
        return carry

    lax.fori_loop(0, last, step, 0)
    scored(last, True)
    for h in range(HEADS):
        peak[rows(h)] = jnp.broadcast_to(
            jnp.max(peak[rows(h)], axis=1, keepdims=True), (TOK, TOK)
        )
    total[...] = jnp.zeros_like(total)
    tgt[...] = jnp.zeros_like(tgt)

    def weighed(p, carry):
        values = kv[1, pl.ds(2 * p, 2)].reshape(2 * TOK, HD)
        for h in range(HEADS):
            s = score[p, rows(h)]
            top = peak[rows(h)]
            w0 = jnp.exp2((s[:, :TOK] - top) * SCALE)
            w1 = jnp.exp2((s[:, TOK:] - top) * SCALE)
            total[rows(h)] += w0 + w1
            w = jnp.concatenate([w0.astype(BF), w1.astype(BF)], axis=1)
            tgt[h] += dg(w, values, 1, 0)
        return carry

    lax.fori_loop(0, last + 1, weighed, 0)
    for h in range(HEADS):
        tgt[h] = tgt[h] / jnp.sum(total[rows(h)], axis=1, keepdims=True)


def level_sums(c, kv, lc, ls):
    last = c // 2
    odd = c - 2 * last

    def decayed(x, since):
        own = lc[pl.ds(pl.multiple_of(x * HEADS, HEADS), HEADS)]
        since = since + own[:, TOK - 1 :]
        return since, jnp.exp(since - own)

    before = jnp.maximum(c - 1, 0)
    since, weight = decayed(before, jnp.zeros((HEADS, 1), F32))
    since = jnp.where(odd == 1, since, 0.0)
    weight = jnp.where(odd == 1, weight, 0.0)
    keys = kv[0, before].astype(F32).T
    values = kv[1, before]
    for h in range(HEADS):
        ls[0, h] = mm_right_exact(keys * weight[h : h + 1], values, 1, 0)
    for j in range(1, CROSS):
        size = 1 << (j - 1)
        count = (last // size) % 2 * size
        base = last // (2 * size) * (2 * size)
        for h in range(HEADS):
            ls[j, h] = jnp.zeros((HD, HD), F32)

        def step(i, since, j=j, count=count, base=base):
            p = base + count - 1 - i
            since, later = decayed(2 * p + 1, since)
            since, earlier = decayed(2 * p, since)
            weight = jnp.concatenate([earlier, later], axis=1)
            keys = kv[0, pl.ds(2 * p, 2)].reshape(2 * TOK, HD).astype(F32).T
            values = kv[1, pl.ds(2 * p, 2)].reshape(2 * TOK, HD)
            for h in range(HEADS):
                ls[j, h] += mm_right_exact(keys * weight[h : h + 1], values, 1, 0)
            return since

        since = lax.fori_loop(0, count, step, since)


def student(c, qs, kv, g_all, wq, wk, lw, gain, lc, ls, tgt, qp, kp, ks, comb, mix, sd, raw, sums):
    key = kv[0, c]
    value = kv[1, c]
    row_cum = lc[pl.ds(pl.multiple_of(c * HEADS, HEADS), HEADS)]
    col_cum = column_cumulative(g_all[c])
    causal = iota((TOK, TOK), 1) <= iota((TOK, TOK), 0)
    level = local_levels()
    for h in range(HEADS):
        qp[h] = mm_left_exact(qs[rows(h)], wq[h], 1, 0)
        kp[h] = mm_left_exact(key, wk[h], 1, 0)
    for h in range(HEADS):
        combined = lw[h, LOW + 1] * ls[0, h]
        for j in range(1, CROSS):
            combined = combined + lw[h, LOW + 1 + j] * ls[j, h]
        comb[h] = combined
        ks[h] = mm(wk[h], combined, 0, 0)
    for h in range(HEADS):
        decay = jnp.exp(
            jnp.where(causal, col_cum[:, h : h + 1] - row_cum[h : h + 1], NEGATIVE)
        )
        mask = jnp.full((TOK, TOK), lw[h, 0], F32)
        for j in range(1, LOW + 1):
            mask = jnp.where(level == j, lw[h, j], mask)
        scores = mm(qp[h], kp[h], 1, 1)
        sd[h] = scores * decay
        mix[h] = decay * mask
    for h in range(HEADS):
        local = mm_right_exact(sd[h] * mask_of(level, lw, h), value, 1, 0)
        far = jnp.exp(col_cum[:, h : h + 1]) * mm(qp[h], ks[h], 1, 0)
        raw[h] = local + far
    square = jnp.zeros((TOK, HD), F32)
    scaled = jnp.zeros((TOK, HD), F32)
    against = jnp.zeros((TOK, HD), F32)
    for h in range(HEADS):
        g = gain[h : h + 1]
        square = square + raw[h] * raw[h]
        scaled = scaled + (raw[h] * g) * (raw[h] * g)
        against = against + tgt[h] * g * raw[h]
    one = jnp.ones((8, HD), F32)
    tile = [dg(one, x, 1, 1, HIGHEST) for x in (square, scaled, against)]
    sums[...] = jnp.concatenate([t[:1] for t in tile] + [tile[0][:5]], axis=0)


def mask_of(level, lw, h):
    mask = jnp.full((TOK, TOK), lw[h, 0], F32)
    for j in range(1, LOW + 1):
        mask = jnp.where(level == j, lw[h, j], mask)
    return mask


def backward(c, qs, kv, g_all, wk, gain, all_sums, ls, tgt, qp, kp, ks, comb, mix, sd, raw, res, out):
    key = kv[0, c]
    value = kv[1, c]
    entry = jnp.exp(column_cumulative(g_all[c]))
    eye = (iota((TOK, TOK), 0) == iota((TOK, TOK), 1)).astype(F32)
    level = local_levels()
    column = dg(eye, all_sums, 1, 1, HIGHEST)
    inverse = lax.rsqrt(column[:, 0:1] / WIDTH + EPSILON)
    inner = (inverse * column[:, 1:2] - column[:, 2:3]) / TOKENS
    back = inverse * inverse * inverse * inner / WIDTH
    gain_rows = []
    for h in range(HEADS):
        g = gain[h : h + 1]
        normed = raw[h] * inverse
        mismatch = (normed * g - tgt[h]) * (1.0 / TOKENS)
        gain_rows.append(jnp.sum(mismatch * normed, axis=0, keepdims=True))
        res[h] = inverse * (mismatch * g) - raw[h] * back
    lane = iota((16, TOK), 1)
    level_tile = jnp.zeros((16, TOK), F32)
    for h in range(HEADS):
        m = 2 * (h % 4)
        side = h // 4
        e = entry[:, h : h + 1]
        d_mix = mm_right_exact(res[h], value, 1, 1)
        d_scores = d_mix * mix[h]
        through = d_mix * sd[h]
        d_state = mm(e * qp[h], res[h], 0, 0)
        d_comb = mm(wk[h], d_state, 1, 0)
        d_query = mm(d_scores, kp[h], 1, 0) + e * mm(res[h], ks[h], 1, 1)
        d_key = mm(d_scores, qp[h], 0, 0)
        out[side, m, :HD] = mm_left_exact(qs[rows(h)], d_query, 0, 0)
        out[side, m + 1, :HD] = mm(comb[h], d_state, 1, 1) + mm_left_exact(key, d_key, 0, 0)
        lines = [
            jnp.sum(jnp.where(level == j, through, 0.0), axis=0, keepdims=True)
            for j in range(LOW + 1)
        ]
        lines += [jnp.sum(ls[j, h] * d_comb, axis=0, keepdims=True) for j in range(CROSS)]
        lines.append(jnp.zeros((16 - LEVELS, TOK), F32))
        summed = jnp.sum(jnp.concatenate(lines, axis=0), axis=1, keepdims=True)
        level_tile = jnp.where(lane == h, summed, level_tile)
    small = jnp.concatenate([level_tile] + gain_rows, axis=0)
    for side in range(2):
        for m in range(HEADS):
            out[side, m, HD:] = small


def place():
    c = lax.axis_index("seq")
    return c, c // 16, c // 2 % 8, c % 2


def at(y, z, k):
    return y * 16 + z * 2 + k


def greet(axis, partners):
    barrier = pltpu.get_barrier_semaphore()
    for partner in partners:
        pl.semaphore_signal(barrier, inc=1, device_id={axis: partner}, device_id_type=MESH)
    pl.semaphore_wait(barrier, len(partners))


def gather_kernel(k_ref, v_ref, g_ref, kv, gates, send, recv):
    c, y, z, k = place()
    up, down = at(y, (z + 1) % 8, k), at(y, (z + 7) % 8, k)
    twin, across = at(y, z, 1 - k), at(1 - y, z, k)
    greet("seq", (up, down, twin, across))
    kv[0, c] = k_ref[...]
    kv[1, c] = v_ref[...]
    gates[c] = g_ref[...]

    @pl.when(k == 0)
    def _():
        kv[0, c + 1] = jnp.zeros((TOK, HD), BF)
        kv[1, c + 1] = jnp.zeros((TOK, HD), BF)

    def copies(slot, way, target):
        return [
            pltpu.make_async_remote_copy(
                src_ref=src,
                dst_ref=src,
                send_sem=send.at[i, way, slot],
                recv_sem=recv.at[i, slot],
                device_id={"seq": target},
                device_id_type=MESH,
            )
            for i, src in enumerate((gates.at[slot], kv.at[:, slot]))
        ]

    ways = {"twin": (0, twin), "across": (1, across), "up": (2, up), "down": (3, down)}
    sent = []

    def push(slot, way, when):
        number, target = ways[way]

        @pl.when(when)
        def _():
            for copy in copies(slot, number, target):
                copy.start()

        sent.append((slot, way, when))

    def arrived(slot, when):
        @pl.when(when)
        def _():
            for copy in copies(slot, 0, twin):
                copy.wait_recv()

    always = y >= 0
    second = y == 1
    own = at(y, z, k)
    push(own, "across", y == 0)
    push(own, "up", z <= 6)
    push(own, "down", z <= 2)
    push(own, "twin", k == 0)
    first = at(0, z, k)
    arrived(first, second)
    push(first, "up", second)
    push(first, "down", second)
    push(first, "twin", second)
    for r in range(1, 5):
        zs = (z + 8 - r) % 8
        here = z >= r
        slot = at(y, zs, k)
        arrived(slot, here)
        if r < 4:
            push(slot, "up", here & (z <= 6))
        push(slot, "twin", here)
        slot = at(0, zs, k)
        arrived(slot, second)
        if r < 4:
            push(slot, "up", second)
        push(slot, "twin", second)
        if r < 4:
            zs = (z + r) % 8
            here = zs <= 2
            slot = at(y, zs, k)
            arrived(slot, here)
            if r < 3:
                push(slot, "down", here)
            push(slot, "twin", here & (z > zs))
            slot = at(0, zs, k)
            arrived(slot, second)
            if r < 3:
                push(slot, "down", second)
            push(slot, "twin", second)
    arrived(at(y, z, 1 - k), k == 1)
    arrived(at(0, z, 1 - k), second)
    for r in range(1, 8):
        zs = (z + r) % 8
        arrived(at(y, zs, 1 - k), zs < z)
        arrived(at(0, zs, 1 - k), second)
    for slot, way, when in sent:
        number, target = ways[way]

        @pl.when(when)
        def _(slot=slot, number=number, target=target):
            for copy in copies(slot, number, target):
                copy.wait_send()


def exchange_kernel(sums_ref, out, box, send, recv):
    me = lax.axis_index("head")
    peers = [(me + d) % HEADS for d in range(1, HEADS)]
    greet("head", peers)
    box[me] = sums_ref[...]
    copies = [
        pltpu.make_async_remote_copy(
            src_ref=box.at[me],
            dst_ref=box.at[me],
            send_sem=send.at[d],
            recv_sem=recv.at[me],
            device_id={"head": peer},
            device_id_type=MESH,
        )
        for d, peer in enumerate(peers)
    ]
    for copy in copies:
        copy.start()
    for d, peer in enumerate(peers):
        pltpu.make_async_remote_copy(
            src_ref=box.at[peer],
            dst_ref=box.at[peer],
            send_sem=send.at[d],
            recv_sem=recv.at[peer],
            device_id={"head": peer},
            device_id_type=MESH,
        ).wait_recv()
    total = box[0]
    for i in range(1, HEADS):
        total = total + box[i]
    out[...] = total
    for copy in copies:
        copy.wait_send()


def reduce_kernel(
    g_ref, out, small, levels, gains, part, pair, box, total, far,
    s1, r1, s2, r2, s3, r3, s4, r4, s5, r5,
):
    c, y, z, k = place()
    twin, across = at(y, z, 1 - k), at(1 - y, z, k)
    peers = [at(y, (z + d) % 8, k) for d in range(1, 8)]
    greet("seq", [twin, across] + peers)

    def remote(src, dst, send, recv, target):
        return pltpu.make_async_remote_copy(
            src_ref=src, dst_ref=dst, send_sem=send, recv_sem=recv,
            device_id={"seq": target}, device_id_type=MESH,
        )

    order = [(z + d) % 8 for d in range(1, 9)]
    for m in order:
        remote(g_ref.at[1 - k, m], pair.at[m], s1.at[m], r1.at[m], twin).start()
    for d, m in enumerate(order):
        remote(g_ref.at[1 - k, m], pair.at[m], s1.at[m], r1.at[m], twin).wait_recv()
        if d < 7:
            part[m] = g_ref[k, m] + pair[m]
            remote(part.at[m], box.at[z], s2.at[m], r2.at[z], peers[d]).start()
        else:
            box[m] = g_ref[k, m] + pair[m]
    for d in range(7):
        m = order[d]
        remote(part.at[m], box.at[m], s2.at[m], r2.at[m], peers[d]).wait_recv()
    whole = box[0]
    for i in range(1, 8):
        whole = whole + box[i]
    total[...] = whole
    swap = remote(total, far, s3, r3, across)
    swap.start()
    swap.wait_recv()
    final = total[...] + far[...]
    out[k, z] = final[:HD]
    small[...] = final[HD:]
    spread = [
        remote(out.at[k, z], out.at[k, z], s4.at[d], r4.at[z], peers[d]) for d in range(7)
    ]
    for copy in spread:
        copy.start()
    back = [remote(out.at[k, z], out.at[k, z], s5.at[z], r5.at[z], twin)]
    back[0].start()
    for d in (0, 6, 1, 5, 2, 4, 3):
        m = order[d]
        remote(out.at[k, m], out.at[k, m], s4.at[d], r4.at[m], peers[d]).wait_recv()
        back.append(remote(out.at[k, m], out.at[k, m], s5.at[m], r5.at[m], twin))
        back[-1].start()
    tile = jnp.concatenate([final[HD : HD + 16], jnp.zeros((TOK - 16, TOK), F32)], axis=0).T
    levels[...] = tile[:HEADS, :LEVELS]
    gains[...] = final[HD + 16 :]
    for m in range(8):
        remote(out.at[1 - k, m], out.at[1 - k, m], s5.at[m], r5.at[m], twin).wait_recv()
    for m in order:
        remote(g_ref.at[1 - k, m], pair.at[m], s1.at[m], r1.at[m], twin).wait_send()
    for d in range(7):
        m = order[d]
        remote(part.at[m], box.at[z], s2.at[m], r2.at[z], peers[d]).wait_send()
    swap.wait_send()
    for copy in spread + back:
        copy.wait_send()


VM = pl.BlockSpec(memory_space=pltpu.VMEM)
SM = pl.BlockSpec(memory_space=pltpu.SMEM)
DMA = pltpu.SemaphoreType.DMA


def shaped(shape, dtype=F32):
    return jax.ShapeDtypeStruct(shape, dtype)


def gathered(key_vectors, value_vectors, log_gate):
    return pl.pallas_call(
        gather_kernel,
        out_shape=(shaped((2, SPANS, TOK, HD), BF), shaped((SPANS, HEADS, TOK))),
        in_specs=[VM] * 3,
        out_specs=(VM, VM),
        scratch_shapes=[DMA((2, 4, SPANS)), DMA((2, SPANS))],
        compiler_params=pltpu.CompilerParams(
            collective_id=0, has_side_effects=True, vmem_limit_bytes=LIMIT
        ),
        name="gather",
    )(key_vectors, value_vectors, log_gate)


def exchanged(sums):
    return pl.pallas_call(
        exchange_kernel,
        out_shape=shaped((8, TOK)),
        in_specs=[VM],
        out_specs=VM,
        scratch_shapes=[pltpu.VMEM((HEADS, 8, TOK), F32), DMA((HEADS,)), DMA((HEADS,))],
        compiler_params=pltpu.CompilerParams(collective_id=1, has_side_effects=True),
        name="exchange",
    )(sums)


def reduced(parts):
    out, _, levels, gains = pl.pallas_call(
        reduce_kernel,
        out_shape=(
            shaped((2, 8, HD, HD)),
            shaped((SMALL, TOK)),
            shaped((HEADS, LEVELS)),
            shaped((HEADS, HD)),
        ),
        in_specs=[VM],
        out_specs=(VM,) * 4,
        scratch_shapes=[pltpu.VMEM((8, CHUNK, HD), F32)] * 3
        + [pltpu.VMEM((CHUNK, HD), F32)] * 2
        + [DMA((8,))] * 4
        + [DMA, DMA]
        + [DMA((8,))] * 4,
        compiler_params=pltpu.CompilerParams(
            collective_id=2, has_side_effects=True, vmem_limit_bytes=LIMIT
        ),
        name="reduce",
    )(parts)
    return out.reshape(HEADS, 2, HD, HD), levels, gains


def forward_kernel(
    q, kv, g_all, wq, wk, lw, gain,
    qs, ls, tgt, qp, kp, ks, comb, mix, sd, raw, sums,
    lc, peak, score, total,
):
    c = lax.axis_index("seq")
    for h in range(HEADS):
        qs[rows(h)] = q[:, rows(h)]
    make_cumulative(g_all, lc)
    teacher(c, qs, kv, peak, score, total, tgt)
    level_sums(c, kv, lc, ls)
    student(
        c, qs, kv, g_all, wq, wk, lw, gain, lc, ls, tgt, qp, kp, ks, comb, mix, sd, raw, sums
    )


def backward_kernel(
    qs, kv, g_all, wk, gain, all_sums, ls, tgt, qp, kp, ks, comb, mix, sd, raw, out, res
):
    c = lax.axis_index("seq")
    backward(
        c, qs, kv, g_all, wk, gain, all_sums[...], ls, tgt, qp, kp, ks, comb, mix, sd, raw, res, out
    )


def square():
    return shaped((HEADS, TOK, HD))


def on_device(comm, queries, key_vectors, value_vectors, log_gate, query_map, key_map, lw, norm_gain):
    gather, exchange, reduce = comm
    gain = norm_gain.reshape(HEADS, HD)
    kv, gates = gather(key_vectors, value_vectors, log_gate)
    qs, ls, tgt, qp, kp, ks, comb, mix, sd, raw, sums = pl.pallas_call(
        forward_kernel,
        out_shape=(
            shaped((HEADS * TOK, HD), BF),
            shaped((CROSS, HEADS, HD, HD)),
            *(square() for _ in range(8)),
            shaped((8, TOK)),
        ),
        in_specs=[VM] * 5 + [SM, VM],
        out_specs=(VM,) * 11,
        scratch_shapes=[
            pltpu.VMEM((SPANS * HEADS, TOK), F32),
            pltpu.VMEM((HEADS * TOK, TOK), F32),
            pltpu.VMEM((SPANS // 2, HEADS * TOK, 2 * TOK), F32),
            pltpu.VMEM((HEADS * TOK, TOK), F32),
        ],
        compiler_params=pltpu.CompilerParams(vmem_limit_bytes=LIMIT),
        name="forward",
    )(queries, kv, gates, query_map, key_map, lw, gain)
    all_sums = exchange(sums)
    parts = pl.pallas_call(
        backward_kernel,
        out_shape=shaped((2, 8, CHUNK, HD)),
        in_specs=[VM] * 15,
        out_specs=VM,
        scratch_shapes=[pltpu.VMEM((HEADS, TOK, HD), F32)],
        compiler_params=pltpu.CompilerParams(vmem_limit_bytes=LIMIT),
        name="backward",
    )(qs, kv, gates, key_map, gain, all_sums, ls, tgt, qp, kp, ks, comb, mix, sd, raw)
    grads, levels, gains = reduce(parts)
    return grads[:, 0], grads[:, 1], levels, gains.reshape(-1)


COMM = (gathered, exchanged, reduced)


def solution(mesh, comm=COMM):
    return jax.shard_map(
        functools.partial(on_device, comm),
        mesh=mesh,
        in_specs=(
            P("seq", "head"),
            P("seq", "head"),
            P("seq", "head"),
            P("head", "seq"),
            P("head", None, None),
            P("head", None, None),
            P("head", None),
            P("head"),
        ),
        out_specs=(P("head", None, None), P("head", None, None), P("head", None), P("head")),
        check_vma=False,
    )
```

```python
import jax
import jax.numpy as jnp
from jax import lax
from jax.experimental import pallas as pl
from jax.experimental.pallas import tpu as pltpu
from jax.sharding import PartitionSpec as P

F32 = jnp.float32
BF = jnp.bfloat16
HIGHEST = lax.Precision.HIGHEST
MESH = pl.DeviceIdType.MESH
NEGATIVE = -1e30
EPSILON = 1e-05
HD = 128
TOK = 128
HEADS = 8
SPANS = 32
LEVELS = 13
LOW = 7
CROSS = 5
TOKENS = TOK * SPANS
WIDTH = 64 * HD
SMALL = 24
HALF = HD // 2
LOG2E = 1.4426950408889634
SCALE = HD**-0.5 * LOG2E
LIMIT = 58 << 20


def pieces(a):
    high = a.astype(BF)
    return high, (a - high.astype(F32)).astype(BF)


def dg(a, b, ca, cb, precision=None):
    return lax.dot_general(
        a, b, (((ca,), (cb,)), ((), ())), preferred_element_type=F32, precision=precision
    )


def halves(o):
    n = o.shape[1] // 2
    return o[:, :n] + o[:, n:]


def mm(a, b, ca, cb):
    bh, bl = pieces(b)
    left = jnp.concatenate(pieces(a), axis=ca)
    right = jnp.concatenate(
        [jnp.concatenate([bh, bh], axis=cb), jnp.concatenate([bl, bl], axis=cb)], axis=1 - cb
    )
    return halves(dg(left, right, ca, cb))


def mm_left_exact(a, b, ca, cb):
    return halves(dg(a, jnp.concatenate(pieces(b), axis=1 - cb), ca, cb))


def mm_right_exact(a, b, ca, cb):
    return dg(jnp.concatenate(pieces(a), axis=ca), jnp.concatenate([b, b], axis=cb), ca, cb)


def iota(shape, dim):
    return lax.broadcasted_iota(jnp.int32, shape, dim)


def local_levels():
    x = jnp.bitwise_xor(iota((TOK, TOK), 0), iota((TOK, TOK), 1))
    level = jnp.zeros_like(x)
    for bit in range(LOW):
        level = level + (x >= 1 << bit).astype(jnp.int32)
    return level


def rows(h):
    return slice(h * TOK, (h + 1) * TOK)


def column_cumulative(gates):
    lower = (iota((TOK, TOK), 1) <= iota((TOK, TOK), 0)).astype(F32)
    return dg(lower, gates, 1, 1, HIGHEST)


def pair_of(kv, which, p):
    return kv[which, pl.ds(2 * p, 2)].reshape(2 * TOK, HD)


def scored(c, p, masked, qs, kv, peak, score):
    keys = pair_of(kv, 0, p)
    for h in range(HEADS):
        s = dg(qs[rows(h)], keys, 1, 1)
        if masked:
            place_of = 2 * TOK * p + iota((TOK, 2 * TOK), 1)
            s = jnp.where(place_of <= c * TOK + iota((TOK, 2 * TOK), 0), s, NEGATIVE)
        score[p, rows(h)] = s
        top = jnp.maximum(s[:, :TOK], s[:, TOK:])
        peak[rows(h)] = top if masked else jnp.maximum(peak[rows(h)], top)


def weighed(p, h, values, score, peak, total, tgt):
    s = score[p, rows(h)]
    top = peak[rows(h)]
    w0 = jnp.exp2((s[:, :TOK] - top) * SCALE)
    w1 = jnp.exp2((s[:, TOK:] - top) * SCALE)
    total[rows(h)] += w0 + w1
    tgt[h] += dg(jnp.concatenate([w0.astype(BF), w1.astype(BF)], axis=1), values, 1, 0)


def level_weights(c, gates, lc, weights):
    upper = (iota((TOK, TOK), 0) <= iota((TOK, TOK), 1)).astype(F32)
    lc[...] = dg(gates[...].reshape(SPANS * HEADS, TOK), upper, 1, 0, HIGHEST)

    def step(i, since):
        x = c - 1 - i
        own = lc[pl.ds(pl.multiple_of(x * HEADS, HEADS), HEADS)]
        since = since + own[:, TOK - 1 :]
        weights[x] = jnp.exp(since - own)
        return since

    lax.fori_loop(0, c, step, jnp.zeros((HEADS, 1), F32))


def student_inside(qs, kv, c, gate, wq, wk, lw, qp, kp, mix, sd):
    key = kv[0, c]
    upper = (iota((TOK, TOK), 0) <= iota((TOK, TOK), 1)).astype(F32)
    row_cum = dg(gate, upper, 1, 0, HIGHEST)
    col_cum = column_cumulative(gate)
    causal = iota((TOK, TOK), 1) <= iota((TOK, TOK), 0)
    level = local_levels()
    for h in range(HEADS):
        qp[h] = mm_left_exact(qs[rows(h)], wq[h], 1, 0)
        kp[h] = mm_left_exact(key, wk[h], 1, 0)
    for h in range(HEADS):
        decay = jnp.exp(
            jnp.where(causal, col_cum[:, h : h + 1] - row_cum[h : h + 1], NEGATIVE)
        )
        mask = jnp.full((TOK, TOK), lw[h, 0], F32)
        for j in range(1, LOW + 1):
            mask = jnp.where(level == j, lw[h, j], mask)
        sd[h] = mm(qp[h], kp[h], 1, 1) * decay
        mix[h] = decay * mask


def student_whole(entry, kv, c, wk, lw, gain, ls, tgt, qp, ks, comb, raw, local):
    for h in range(HEADS):
        combined = lw[h, LOW + 1] * ls[0, h]
        for j in range(1, CROSS):
            combined = combined + lw[h, LOW + 1 + j] * ls[j, h]
        comb[h] = combined
        ks[h] = mm(wk[h], combined, 0, 0)
    square = jnp.zeros((TOK, HD), F32)
    scaled = jnp.zeros((TOK, HD), F32)
    against = jnp.zeros((TOK, HD), F32)
    for h in range(HEADS):
        r = local[h] + entry[:, h : h + 1] * mm(qp[h], ks[h], 1, 0)
        raw[h] = r
        rg = r * gain[h : h + 1]
        square = square + r * r
        scaled = scaled + rg * rg
        against = against + tgt[h] * rg
    one = jnp.ones((8, HD), F32)
    tile = [dg(one, x, 1, 1, HIGHEST) for x in (square, scaled, against)]
    return jnp.concatenate([t[:1] for t in tile] + [tile[0][:5]], axis=0)


def backward_inside(
    all_sums, entry, kv, c, wk, gain, ls, tgt, qp, kp, ks, comb, mix, sd, raw, res, dstate, dquery, dkey
):
    value = kv[1, c]
    eye = (iota((TOK, TOK), 0) == iota((TOK, TOK), 1)).astype(F32)
    level = local_levels()
    column = dg(eye, all_sums, 1, 1, HIGHEST)
    inverse = lax.rsqrt(column[:, 0:1] / WIDTH + EPSILON)
    inner = (inverse * column[:, 1:2] - column[:, 2:3]) / TOKENS
    back = inverse * inverse * inverse * inner / WIDTH
    gain_rows = []
    for h in range(HEADS):
        g = gain[h : h + 1]
        normed = raw[h] * inverse
        mismatch = (normed * g - tgt[h]) * (1.0 / TOKENS)
        gain_rows.append(jnp.sum(mismatch * normed, axis=0, keepdims=True))
        res[h] = inverse * (mismatch * g) - raw[h] * back
    lane = iota((16, TOK), 1)
    level_tile = jnp.zeros((16, TOK), F32)
    for h in range(HEADS):
        e = entry[:, h : h + 1]
        d_mix = mm_right_exact(res[h], value, 1, 1)
        d_scores = d_mix * mix[h]
        through = d_mix * sd[h]
        dstate[h] = mm(e * qp[h], res[h], 0, 0)
        d_comb = mm(wk[h], dstate[h], 1, 0)
        dquery[h] = mm(d_scores, kp[h], 1, 0) + e * mm(res[h], ks[h], 1, 1)
        dkey[h] = mm(d_scores, qp[h], 0, 0)
        lines = [
            jnp.sum(jnp.where(level == j, through, 0.0), axis=0, keepdims=True)
            for j in range(LOW + 1)
        ]
        lines += [jnp.sum(ls[j, h] * d_comb, axis=0, keepdims=True) for j in range(CROSS)]
        lines.append(jnp.zeros((16 - LEVELS, TOK), F32))
        summed = jnp.sum(jnp.concatenate(lines, axis=0), axis=1, keepdims=True)
        level_tile = jnp.where(lane == h, summed, level_tile)
    return jnp.concatenate([level_tile] + gain_rows, axis=0)


def at(y, z, k):
    return y * 16 + z * 2 + k


def remote(axis, src, dst, send, recv, target):
    return pltpu.make_async_remote_copy(
        src_ref=src, dst_ref=dst, send_sem=send, recv_sem=recv,
        device_id={axis: target}, device_id_type=MESH,
    )


TWIN, ACROSS, UP, DOWN = range(4)


def whole_kernel(
    q_hbm, k_ref, v_ref, g_ref, wq_hbm, wk_hbm, lw, gain,
    out, levels, gains,
    qs, wq, wk, kv, gates, score, peak, total, tgt, lc, weights, ls, qp, kp, ks, comb, mix, sd, raw, res, local,
    dstate, dquery, dkey, grads, pair, part, from_up, from_down, mine, far,
    sums_box, small_part, small_pair, small_box, small_total, small_far,
    load, send, recv, sums_send, sums_recv, pair_send, pair_recv, ring_send, ring_recv, far_send, far_recv,
    out_send, out_recv, small_send, small_recv,
):
    c = lax.axis_index("seq")
    y, z, k = c // 16, c // 2 % 8, c % 2
    own_pair = c // 2
    targets = (at(y, z, 1 - k), at(1 - y, z, k), at(y, (z + 1) % 8, k), at(y, (z + 7) % 8, k))
    twin, across, up, down = targets
    z_peers = [at(y, (z + d) % 8, k) for d in range(1, 8)]
    me = lax.axis_index("head")
    head_peers = [(me + d) % HEADS for d in range(1, HEADS)]

    loads = [
        pltpu.make_async_copy(q_hbm.at[:, rows(h)], qs.at[rows(h)], load.at[h])
        for h in range(HEADS)
    ]
    loads.append(pltpu.make_async_copy(wq_hbm, wq, load.at[8]))
    loads.append(pltpu.make_async_copy(wk_hbm, wk, load.at[9]))
    for copy in loads:
        copy.start()
    kv[0, c] = k_ref[...]
    kv[1, c] = v_ref[...]
    gates[c] = g_ref[...]

    @pl.when(k == 0)
    def _():
        kv[0, c + 1] = jnp.zeros((TOK, HD), BF)
        kv[1, c + 1] = jnp.zeros((TOK, HD), BF)

    barrier = pltpu.get_barrier_semaphore()
    for partner in [twin, across] + z_peers:
        pl.semaphore_signal(barrier, inc=1, device_id={"seq": partner}, device_id_type=MESH)
    for partner in head_peers:
        pl.semaphore_signal(barrier, inc=1, device_id={"head": partner}, device_id_type=MESH)
    pl.semaphore_wait(barrier, 16)

    def copies(phase, slot, way):
        refs = ((0, gates.at[slot]), (1, kv.at[0, slot])) if phase == 0 else ((2, kv.at[1, slot]),)
        return [
            remote("seq", ref, ref, send.at[i, way, slot], recv.at[i, slot], targets[way])
            for i, ref in refs
        ]

    def push(phase, slot, way, when):
        @pl.when(when)
        def _():
            for copy in copies(phase, slot, way):
                copy.start()

    def pushed(phase, slot, way, when):
        @pl.when(when)
        def _():
            for copy in copies(phase, slot, way):
                copy.wait_send()

    def arrived(phase, slot, when):
        @pl.when(when)
        def _():
            for copy in copies(phase, slot, TWIN):
                copy.wait_recv()

    second = y == 1

    def first_moves(phase, act):
        own = at(y, z, k)
        act(phase, own, ACROSS, y == 0)
        act(phase, own, UP, z <= 6)
        act(phase, own, DOWN, z <= 2)
        act(phase, own, TWIN, k == 0)

    def across_moves(phase, act, wait):
        slot = at(0, z, k)
        wait(phase, slot, second)
        act(phase, slot, UP, second)
        act(phase, slot, DOWN, second)
        act(phase, slot, TWIN, second)

    def round_moves(phase, r, act, wait):
        zs = (z + 8 - r) % 8
        slot, here = at(y, zs, k), z >= r
        wait(phase, slot, here)
        act(phase, slot, UP, here & (z <= 6) & (r < 4))
        act(phase, slot, TWIN, here)
        slot = at(0, zs, k)
        wait(phase, slot, second)
        act(phase, slot, UP, second & (r < 4))
        act(phase, slot, TWIN, second)
        zs = (z + r) % 8
        slot, here = at(y, zs, k), (zs <= 2) & (r < 4)
        wait(phase, slot, here)
        act(phase, slot, DOWN, here & (r < 3))
        act(phase, slot, TWIN, here & (z > zs))
        slot, here = at(0, zs, k), second & (r < 4)
        wait(phase, slot, here)
        act(phase, slot, DOWN, here & (r < 3))
        act(phase, slot, TWIN, here)

    def no_wait(phase, slot, when):
        pass

    def pairs(phase, r, use):
        def one(kind, carry):
            other = kind % 2
            above = kind // 2
            zs = (z + 8 + r * (2 * above - 1)) % 8
            mine_ok = (other == 0) & (r >= 1) & (zs < z) & ((above == 0) & (z >= r) | (above == 1) & (r < 4) & (zs <= 2))
            other_ok = (other == 1) & second & ((above == 0) | (r >= 1) & (r < 4))
            ys = y * (1 - other)

            @pl.when(mine_ok | other_ok)
            def _():
                for copy in copies(phase, at(ys, zs, 1 - k), TWIN):
                    copy.wait_recv()
                use(ys * 8 + zs)

            return carry

        lax.fori_loop(0, 4, one, 0)

    first_moves(0, push)
    first_moves(1, push)
    for copy in loads:
        copy.wait()
    across_moves(0, push, arrived)
    arrived(0, at(y, z, 0), k == 1)
    scored(c, own_pair, True, qs, kv, peak, score)

    def key_round(r, carry):
        @pl.when(r <= 4)
        def _():
            round_moves(0, r, push, arrived)

        @pl.when(r == 1)
        def _():
            student_inside(qs, kv, c, g_ref[...], wq, wk, lw, qp, kp, mix, sd)

        pairs(0, r - 1, lambda p: scored(c, p, False, qs, kv, peak, score))
        return carry

    lax.fori_loop(1, 6, key_round, 0)
    across_moves(1, push, arrived)
    level_weights(c, gates, lc, weights)
    for h in range(HEADS):
        peak[rows(h)] = jnp.broadcast_to(
            jnp.max(peak[rows(h)], axis=1, keepdims=True), (TOK, TOK)
        )
    total[...] = jnp.zeros_like(total)
    tgt[...] = jnp.zeros_like(tgt)
    ls[...] = jnp.zeros_like(ls)
    arrived(1, at(y, z, 0), k == 1)

    @pl.when(k == 1)
    def _():
        keys = kv[0, c - 1].astype(F32).T
        for h in range(HEADS):
            ls[0, h] = mm_right_exact(keys * weights[c - 1, h : h + 1], kv[1, c - 1], 1, 0)

    for h in range(HEADS):
        weighed(own_pair, h, pair_of(kv, 1, own_pair), score, peak, total, tgt)
        local[h] = mm_right_exact(sd[h] * mix_ratio(lw, h), kv[1, c], 1, 0)

    def use_values(p):
        values = pair_of(kv, 1, p)
        keys = pair_of(kv, 0, p).astype(F32).T
        weight = jnp.concatenate([weights[2 * p], weights[2 * p + 1]], axis=1)
        j = jnp.int32(0)
        for b in range(4):
            j = j + (own_pair // (1 << b) != p // (1 << b)).astype(jnp.int32)
        for h in range(HEADS):
            weighed(p, h, values, score, peak, total, tgt)
            ls[j, h] += mm_right_exact(keys * weight[h : h + 1], values, 1, 0)

    def value_round(r, carry):
        @pl.when(r <= 4)
        def _():
            round_moves(1, r, push, arrived)

        pairs(1, r - 1, use_values)
        return carry

    lax.fori_loop(1, 6, value_round, 0)
    for h in range(HEADS):
        tgt[h] = tgt[h] / jnp.sum(total[rows(h)], axis=1, keepdims=True)
    entry = jnp.exp(column_cumulative(g_ref[...]))
    sums_box[me] = student_whole(entry, kv, c, wk, lw, gain, ls, tgt, qp, ks, comb, raw, local)

    outgoing = [
        remote("head", sums_box.at[me], sums_box.at[me], sums_send.at[d], sums_recv.at[me], peer)
        for d, peer in enumerate(head_peers)
    ]
    for copy in outgoing:
        copy.start()
    for d, peer in enumerate(head_peers):
        remote(
            "head", sums_box.at[peer], sums_box.at[peer], sums_send.at[d], sums_recv.at[peer], peer
        ).wait_recv()
    all_sums = sums_box[0]
    for i in range(1, HEADS):
        all_sums = all_sums + sums_box[i]
    small_part[...] = backward_inside(
        all_sums, entry, kv, c, wk, gain, ls, tgt, qp, kp, ks, comb, mix, sd, raw, res, dstate, dquery, dkey
    )

    small_twin = remote("seq", small_part, small_pair, small_send.at[0], small_recv.at[8], twin)
    small_twin.start()
    key = kv[0, c]
    order = [(z + d) % 8 for d in (4, 3, 5, 2, 6, 1, 7, 0)]

    def to_twin(h):
        return remote("seq", grads.at[1 - k, h], pair.at[h], pair_send.at[h], pair_recv.at[h], twin)

    for h in order:
        q_rows = qs[pl.ds(pl.multiple_of(h * TOK, TOK), TOK)]
        grads[0, h] = mm_left_exact(q_rows, dquery[h], 0, 0)
        grads[1, h] = mm(comb[h], dstate[h], 1, 1) + mm_left_exact(key, dkey[h], 0, 0)
        to_twin(h).start()
    small_twin.wait_recv()
    small_box[z] = small_part[...] + small_pair[...]
    small_out = [
        remote("seq", small_box.at[z], small_box.at[z], small_send.at[d], small_recv.at[z], peer)
        for d, peer in enumerate(z_peers, 1)
    ]
    for copy in small_out:
        copy.start()

    def half(a):
        return pl.ds(a * HALF, HALF)

    def hop(way, i, h, a):
        box = from_up if way == DOWN else from_down
        return remote(
            "seq", part.at[h, half(a)], box.at[i, half(a)], ring_send.at[way - 2, i, a],
            ring_recv.at[way - 2, i, a], targets[way],
        )

    def summed(way, i, h):
        to_twin(h).wait_recv()
        for a in range(2):
            held = grads[k, h, half(a)] + pair[h, half(a)]
            if i:
                hop(way, i - 1, h, a).wait_recv()
                held = held + (from_up if way == DOWN else from_down)[i - 1, half(a)]
            part[h, half(a)] = held
            hop(way, i, h, a).start()

    hops = []
    for i in range(4):
        summed(DOWN, i, (z + 4 + i) % 8)
        hops.append((DOWN, i, (z + 4 + i) % 8))
        if i < 3:
            summed(UP, i, (z + 3 - i) % 8)
            hops.append((UP, i, (z + 3 - i) % 8))
    to_twin(z).wait_recv()

    def swap(a):
        return remote(
            "seq", mine.at[half(a)], far.at[half(a)], far_send.at[a], far_recv.at[a], across
        )

    for a in range(2):
        hop(UP, 2, z, a).wait_recv()
        held = grads[k, z, half(a)] + pair[z, half(a)] + from_down[2, half(a)]
        hop(DOWN, 3, z, a).wait_recv()
        mine[half(a)] = held + from_up[3, half(a)]
        swap(a).start()
    for d, h in enumerate([(z + d) % 8 for d in range(1, 8)], 1):
        remote(
            "seq", small_box.at[h], small_box.at[h], small_send.at[d], small_recv.at[h], z_peers[d - 1]
        ).wait_recv()
    held = small_box[0]
    for i in range(1, 8):
        held = held + small_box[i]
    small_total[...] = held
    small_swap = remote("seq", small_total, small_far, small_send.at[8], small_recv.at[9], across)
    small_swap.start()

    def spread(way, h, a):
        ref = out.at[k, h, half(a)]
        return remote("seq", ref, ref, out_send.at[way, h, a], out_recv.at[0, h, a], targets[way])

    def to_out_twin(h, a):
        ref = out.at[k, h, half(a)]
        return remote("seq", ref, ref, out_send.at[0, h, a], out_recv.at[1, h, a], twin)

    pending = []

    def go(copy):
        copy.start()
        pending.append(copy)

    for a in range(2):
        swap(a).wait_recv()
        out[k, z, half(a)] = mine[half(a)] + far[half(a)]
        go(spread(UP, z, a))
        go(spread(DOWN, z, a))
        go(to_out_twin(z, a))
    small_swap.wait_recv()
    final = small_total[...] + small_far[...]
    tile = jnp.concatenate([final[:16], jnp.zeros((TOK - 16, TOK), F32)], axis=0).T
    levels[...] = tile[:HEADS, :LEVELS]
    gains[...] = final[16:]
    for r in range(1, 5):
        for a in range(2):
            h = (z + 8 - r) % 8
            spread(UP, h, a).wait_recv()
            if r < 4:
                go(spread(UP, h, a))
            go(to_out_twin(h, a))
            if r < 4:
                h = (z + r) % 8
                spread(DOWN, h, a).wait_recv()
                if r < 3:
                    go(spread(DOWN, h, a))
                go(to_out_twin(h, a))
    for h in range(8):
        for a in range(2):
            ref = out.at[1 - k, h, half(a)]
            remote("seq", ref, ref, out_send.at[0, h, a], out_recv.at[1, h, a], twin).wait_recv()

    for phase in range(2):
        first_moves(phase, pushed)
        across_moves(phase, pushed, no_wait)

        def sent(r, carry, phase=phase):
            round_moves(phase, r, pushed, no_wait)
            return carry

        lax.fori_loop(1, 5, sent, 0)
    for copy in outgoing + [small_twin] + small_out + [small_swap] + pending:
        copy.wait_send()
    for h in order:
        to_twin(h).wait_send()
    for way, i, h in hops:
        for a in range(2):
            hop(way, i, h, a).wait_send()
    for a in range(2):
        swap(a).wait_send()


def mix_ratio(lw, h):
    level = local_levels()
    mask = jnp.full((TOK, TOK), lw[h, 0], F32)
    for j in range(1, LOW + 1):
        mask = jnp.where(level == j, lw[h, j], mask)
    return mask


VM = pl.BlockSpec(memory_space=pltpu.VMEM)
SM = pl.BlockSpec(memory_space=pltpu.SMEM)
ANY = pl.BlockSpec(memory_space=pl.ANY)
DMA = pltpu.SemaphoreType.DMA


def shaped(shape, dtype=F32):
    return jax.ShapeDtypeStruct(shape, dtype)


def on_device(queries, key_vectors, value_vectors, log_gate, query_map, key_map, lw, norm_gain):
    matrix = pltpu.VMEM((HEADS, TOK, HD), F32)
    small = pltpu.VMEM((SMALL, TOK), F32)
    one = pltpu.VMEM((TOK, HD), F32)
    out, levels, gains = pl.pallas_call(
        whole_kernel,
        out_shape=(shaped((2, HEADS, HD, HD)), shaped((HEADS, LEVELS)), shaped((HEADS, HD))),
        in_specs=[ANY, VM, VM, VM, ANY, ANY, SM, VM],
        out_specs=(VM,) * 3,
        scratch_shapes=[
            pltpu.VMEM((HEADS * TOK, HD), BF),
            matrix,
            matrix,
            pltpu.VMEM((2, SPANS, TOK, HD), BF),
            pltpu.VMEM((SPANS, HEADS, TOK), F32),
            pltpu.VMEM((SPANS // 2, HEADS * TOK, 2 * TOK), F32),
            pltpu.VMEM((HEADS * TOK, TOK), F32),
            pltpu.VMEM((HEADS * TOK, TOK), F32),
            matrix,
            pltpu.VMEM((SPANS * HEADS, TOK), F32),
            pltpu.VMEM((SPANS, HEADS, TOK), F32),
            pltpu.VMEM((CROSS, HEADS, HD, HD), F32),
            *[matrix] * 12,
            pltpu.VMEM((2, HEADS, HD, HD), F32),
            matrix,
            matrix,
            pltpu.VMEM((4, HD, HD), F32),
            pltpu.VMEM((3, HD, HD), F32),
            one,
            one,
            pltpu.VMEM((HEADS, 8, TOK), F32),
            small,
            small,
            pltpu.VMEM((8, SMALL, TOK), F32),
            small,
            small,
            DMA((10,)),
            DMA((3, 4, SPANS)),
            DMA((3, SPANS)),
            DMA((7,)),
            DMA((HEADS,)),
            DMA((8,)),
            DMA((8,)),
            DMA((2, 4, 2)),
            DMA((2, 4, 2)),
            DMA((2,)),
            DMA((2,)),
            DMA((4, 8, 2)),
            DMA((2, 8, 2)),
            DMA((9,)),
            DMA((10,)),
        ],
        compiler_params=pltpu.CompilerParams(
            collective_id=0, has_side_effects=True, vmem_limit_bytes=LIMIT
        ),
        name="distill",
    )(
        queries, key_vectors, value_vectors, log_gate, query_map, key_map, lw,
        norm_gain.reshape(HEADS, HD),
    )
    return out[0], out[1], levels, gains.reshape(-1)


def solution(mesh):
    return jax.shard_map(
        on_device,
        mesh=mesh,
        in_specs=(
            P("seq", "head"),
            P("seq", "head"),
            P("seq", "head"),
            P("head", "seq"),
            P("head", None, None),
            P("head", None, None),
            P("head", None),
            P("head"),
        ),
        out_specs=(P("head", None, None), P("head", None, None), P("head", None), P("head")),
        check_vma=False,
    )
```

```python
import jax
import jax.numpy as jnp
from jax import lax
from jax.experimental import pallas as pl
from jax.experimental.pallas import tpu as pltpu
from jax.sharding import PartitionSpec as P

F32 = jnp.float32
BF = jnp.bfloat16
HIGHEST = lax.Precision.HIGHEST
MESH = pl.DeviceIdType.MESH
NEGATIVE = -1e30
EPSILON = 1e-05
HD = 128
TOK = 128
HEADS = 8
SPANS = 32
LEVELS = 13
LOW = 7
CROSS = 5
TOKENS = TOK * SPANS
WIDTH = 64 * HD
SMALL = 24
GATE_ROWS = 32
VALUE_ROWS = 128 + GATE_ROWS
PIECE = 64 + 8
HALF = HD // 2
LOG2E = 1.4426950408889634
SCALE = HD**-0.5 * LOG2E
LIMIT = 58 << 20


def pieces(a):
    high = a.astype(BF)
    return high, (a - high.astype(F32)).astype(BF)


def dg(a, b, ca, cb, precision=None):
    return lax.dot_general(
        a, b, (((ca,), (cb,)), ((), ())), preferred_element_type=F32, precision=precision
    )


def halves(o):
    n = o.shape[1] // 2
    return o[:, :n] + o[:, n:]


def mm(a, b, ca, cb):
    bh, bl = pieces(b)
    left = jnp.concatenate(pieces(a), axis=ca)
    right = jnp.concatenate(
        [jnp.concatenate([bh, bh], axis=cb), jnp.concatenate([bl, bl], axis=cb)], axis=1 - cb
    )
    return halves(dg(left, right, ca, cb))


def mm_left_exact(a, b, ca, cb):
    return halves(dg(a, jnp.concatenate(pieces(b), axis=1 - cb), ca, cb))


def mm_right_exact(a, b, ca, cb):
    return dg(jnp.concatenate(pieces(a), axis=ca), jnp.concatenate([b, b], axis=cb), ca, cb)


def iota(shape, dim):
    return lax.broadcasted_iota(jnp.int32, shape, dim)


def local_levels():
    x = jnp.bitwise_xor(iota((TOK, TOK), 0), iota((TOK, TOK), 1))
    level = jnp.zeros_like(x)
    for bit in range(LOW):
        level = level + (x >= 1 << bit).astype(jnp.int32)
    return level


def rows(h):
    return slice(h * TOK, (h + 1) * TOK)


def column_cumulative(gates):
    lower = (iota((TOK, TOK), 1) <= iota((TOK, TOK), 0)).astype(F32)
    return dg(lower, gates, 1, 1, HIGHEST)


def pair_of(ref, p):
    return jnp.concatenate([ref[2 * p, :TOK], ref[2 * p + 1, :TOK]], axis=0)


def scored(c, p, masked, qs, keys_all, peak, score):
    keys = pair_of(keys_all, p)
    for h in range(HEADS):
        s = dg(qs[rows(h)], keys, 1, 1)
        if masked:
            place_of = 2 * TOK * p + iota((TOK, 2 * TOK), 1)
            s = jnp.where(place_of <= c * TOK + iota((TOK, 2 * TOK), 0), s, NEGATIVE)
        score[p, rows(h)] = s
        top = jnp.maximum(s[:, :TOK], s[:, TOK:])
        peak[rows(h)] = top if masked else jnp.maximum(peak[rows(h)], top)


def weighed(p, h, values, score, peak, total, tgt):
    s = score[p, rows(h)]
    top = peak[rows(h)]
    w0 = jnp.exp2((s[:, :TOK] - top) * SCALE)
    w1 = jnp.exp2((s[:, TOK:] - top) * SCALE)
    total[rows(h)] += w0 + w1
    tgt[h] += dg(jnp.concatenate([w0.astype(BF), w1.astype(BF)], axis=1), values, 1, 0)


def level_weights(c, vals, lc, weights):
    upper = (iota((TOK, TOK), 0) <= iota((TOK, TOK), 1)).astype(BF)
    lc[...] = dg(vals[:, TOK:].reshape(SPANS * GATE_ROWS, TOK), upper, 1, 0)

    def step(i, since):
        x = c - 1 - i
        three = lc[pl.ds(pl.multiple_of(x * GATE_ROWS, GATE_ROWS), 3 * HEADS)]
        own = three[:HEADS] + three[HEADS : 2 * HEADS] + three[2 * HEADS :]
        since = since + own[:, TOK - 1 :]
        weights[x] = jnp.exp(since - own)
        return since

    lax.fori_loop(0, c, step, jnp.zeros((HEADS, 1), F32))


def gate_pieces(gate):
    high = gate.astype(BF).astype(F32)
    middle = (gate - high).astype(BF).astype(F32)
    low = gate - high - middle
    return jnp.concatenate([high, middle, low, jnp.zeros_like(gate)], axis=0).astype(BF)


def student_inside(qs, key, gate, wq, wk, lw, qp, kp, mix, sd):
    upper = (iota((TOK, TOK), 0) <= iota((TOK, TOK), 1)).astype(F32)
    row_cum = dg(gate, upper, 1, 0, HIGHEST)
    col_cum = column_cumulative(gate)
    causal = iota((TOK, TOK), 1) <= iota((TOK, TOK), 0)
    level = local_levels()
    for h in range(HEADS):
        qp[h] = mm_left_exact(qs[rows(h)], wq[h], 1, 0)
        kp[h] = mm_left_exact(key, wk[h], 1, 0)
    for h in range(HEADS):
        decay = jnp.exp(
            jnp.where(causal, col_cum[:, h : h + 1] - row_cum[h : h + 1], NEGATIVE)
        )
        mask = jnp.full((TOK, TOK), lw[h, 0], F32)
        for j in range(1, LOW + 1):
            mask = jnp.where(level == j, lw[h, j], mask)
        sd[h] = mm(qp[h], kp[h], 1, 1) * decay
        mix[h] = decay * mask


def student_whole(entry, wk, lw, gain, ls, tgt, qp, ks, comb, raw, local):
    for h in range(HEADS):
        combined = lw[h, LOW + 1] * ls[0, h]
        for j in range(1, CROSS):
            combined = combined + lw[h, LOW + 1 + j] * ls[j, h]
        comb[h] = combined
        ks[h] = mm(wk[h], combined, 0, 0)
    square = jnp.zeros((TOK, HD), F32)
    scaled = jnp.zeros((TOK, HD), F32)
    against = jnp.zeros((TOK, HD), F32)
    for h in range(HEADS):
        r = local[h] + entry[:, h : h + 1] * mm(qp[h], ks[h], 1, 0)
        raw[h] = r
        rg = r * gain[h : h + 1]
        square = square + r * r
        scaled = scaled + rg * rg
        against = against + tgt[h] * rg
    one = jnp.ones((8, HD), F32)
    tile = [dg(one, x, 1, 1, HIGHEST) for x in (square, scaled, against)]
    return jnp.concatenate([t[:1] for t in tile] + [tile[0][:5]], axis=0)


def backward_inside(
    all_sums, entry, value, wk, gain, ls, tgt, qp, kp, ks, mix, sd, raw, res, dstate, dquery, dkey
):
    eye = (iota((TOK, TOK), 0) == iota((TOK, TOK), 1)).astype(F32)
    level = local_levels()
    column = dg(eye, all_sums, 1, 1, HIGHEST)
    inverse = lax.rsqrt(column[:, 0:1] / WIDTH + EPSILON)
    inner = (inverse * column[:, 1:2] - column[:, 2:3]) / TOKENS
    back = inverse * inverse * inverse * inner / WIDTH
    gain_rows = []
    for h in range(HEADS):
        g = gain[h : h + 1]
        normed = raw[h] * inverse
        mismatch = (normed * g - tgt[h]) * (1.0 / TOKENS)
        gain_rows.append(jnp.sum(mismatch * normed, axis=0, keepdims=True))
        res[h] = inverse * (mismatch * g) - raw[h] * back
    lane = iota((16, TOK), 1)
    level_tile = jnp.zeros((16, TOK), F32)
    for h in range(HEADS):
        e = entry[:, h : h + 1]
        d_mix = mm_right_exact(res[h], value, 1, 1)
        d_scores = d_mix * mix[h]
        through = d_mix * sd[h]
        dstate[h] = mm(e * qp[h], res[h], 0, 0)
        d_comb = mm(wk[h], dstate[h], 1, 0)
        dquery[h] = mm(d_scores, kp[h], 1, 0) + e * mm(res[h], ks[h], 1, 1)
        dkey[h] = mm(d_scores, qp[h], 0, 0)
        lines = [
            jnp.sum(jnp.where(level == j, through, 0.0), axis=0, keepdims=True)
            for j in range(LOW + 1)
        ]
        lines += [jnp.sum(ls[j, h] * d_comb, axis=0, keepdims=True) for j in range(CROSS)]
        lines.append(jnp.zeros((16 - LEVELS, TOK), F32))
        summed = jnp.sum(jnp.concatenate(lines, axis=0), axis=1, keepdims=True)
        level_tile = jnp.where(lane == h, summed, level_tile)
    return jnp.concatenate([level_tile] + gain_rows, axis=0)


def at(y, z, k):
    return y * 16 + z * 2 + k


def remote(axis, src, dst, send, recv, target):
    return pltpu.make_async_remote_copy(
        src_ref=src, dst_ref=dst, send_sem=send, recv_sem=recv,
        device_id={axis: target}, device_id_type=MESH,
    )


def whole_kernel(
    q_hbm, k_ref, v_ref, g_ref, wq_hbm, wk_hbm, lw, gain,
    out, levels, gains,
    qs, wq, wk, keys_all, vals, score, peak, total, tgt, lc, weights, ls, qp, kp, ks, comb, mix, sd, raw, res, local,
    dstate, dquery, dkey, grads, pair, part, box, done, sums_box, small_part, small_pair, small_sum,
    load, own_send, relay_send, twin_send, recv, sums_send, sums_recv, pair_send, pair_recv,
    part_send, part_recv, done_send, done_recv, small_sem,
):
    c = lax.axis_index("seq")
    y, z, k = c // 16, c // 2 % 8, c % 2
    own_pair = c // 2
    second = y == 1
    twin, across = at(y, z, 1 - k), at(1 - y, z, k)
    far_first = (4, 3, 5, 2, 6, 1, 7)
    me = lax.axis_index("head")
    head_peers = [(me + d) % HEADS for d in range(1, HEADS)]

    barrier = pltpu.get_barrier_semaphore()
    for d in range(8):
        for other in range(2):
            if d or other:
                target = at((y + other) % 2, (z + d) % 8, k)
                pl.semaphore_signal(barrier, inc=1, device_id={"seq": target}, device_id_type=MESH)
    pl.semaphore_signal(barrier, inc=1, device_id={"seq": twin}, device_id_type=MESH)
    for peer in head_peers:
        pl.semaphore_signal(barrier, inc=1, device_id={"head": peer}, device_id_type=MESH)

    loads = [
        pltpu.make_async_copy(q_hbm.at[:, rows(h)], qs.at[rows(h)], load.at[h])
        for h in range(HEADS)
    ]
    loads.append(pltpu.make_async_copy(wq_hbm, wq, load.at[8]))
    loads.append(pltpu.make_async_copy(wk_hbm, wk, load.at[9]))
    for copy in loads:
        copy.start()
    keys_all[c] = k_ref[...]
    vals[c, :TOK] = v_ref[...]
    vals[c, TOK:] = gate_pieces(g_ref[...])

    @pl.when(k == 0)
    def _():
        keys_all[c + 1] = jnp.zeros((TOK, HD), BF)
        vals[c + 1] = jnp.zeros((VALUE_ROWS, HD), BF)

    for copy in loads:
        copy.wait()
    pl.semaphore_wait(barrier, 23)

    def block(phase, slot):
        return keys_all.at[slot] if phase == 0 else vals.at[slot]

    def copy_of(phase, slot, sem, target):
        ref = block(phase, slot)
        return remote("seq", ref, ref, sem, recv.at[phase, slot], target)

    def to_twin(phase, slot):
        return copy_of(phase, slot, twin_send.at[phase, slot], twin)

    def to_across(phase):
        return copy_of(phase, c, own_send.at[phase, 0], across)

    def to_row(phase, d):
        return copy_of(phase, c, own_send.at[phase, d], at(y, (z + d) % 8, k))

    def relayed(phase, d):
        return copy_of(phase, at(0, z, k), relay_send.at[phase, d], at(y, (z + d) % 8, k))

    def act(when, copy, wait=False):
        @pl.when(when)
        def _():
            if wait:
                copy.wait_send()
            else:
                copy.start()

    def own_moves(phase, wait=False):
        act(y == 0, to_across(phase), wait)
        act(k == 0, to_twin(phase, c), wait)
        for d in far_first:
            act(z + d < 8, to_row(phase, d), wait)

    def arrived(phase, slot):
        to_twin(phase, slot).wait_recv()

    def relay(phase):
        @pl.when(second)
        def _():
            slot = at(0, z, k)
            arrived(phase, slot)
            for d in far_first:
                relayed(phase, d).start()
            to_twin(phase, slot).start()

    def chip_of(i):
        d = jnp.where(i % 2 == 1, (i + 1) // 2, 8 - i // 2)
        return (z + 8 - d) % 8

    def forward(phase, i):
        zs = chip_of(i)

        @pl.when(zs < z)
        def _():
            slot = at(y, zs, k)
            arrived(phase, slot)
            to_twin(phase, slot).start()

        @pl.when(second)
        def _():
            slot = at(0, zs, k)
            arrived(phase, slot)
            to_twin(phase, slot).start()

    def pairs(phase, i, use):
        zs = jnp.where(i == 0, z, chip_of(i))

        def one(other, carry):
            @pl.when((other == 0) & (zs < z) | (other == 1) & second)
            def _():
                ys = y * (1 - other)
                arrived(phase, at(ys, zs, 1 - k))
                use(ys * 8 + zs)

            return carry

        lax.fori_loop(0, 2, one, 0)

    own_moves(0)
    own_moves(1)
    student_inside(qs, k_ref[...], g_ref[...], wq, wk, lw, qp, kp, mix, sd)
    relay(0)
    relay(1)

    @pl.when(k == 1)
    def _():
        arrived(0, c - 1)

    scored(c, own_pair, True, qs, keys_all, peak, score)

    def key_step(i, carry):
        @pl.when(i < 8)
        def _():
            forward(0, i)

        pairs(0, i - 1, lambda p: scored(c, p, False, qs, keys_all, peak, score))
        return carry

    lax.fori_loop(1, 9, key_step, 0)

    def value_forward(i, carry):
        forward(1, i)
        return carry

    lax.fori_loop(1, 8, value_forward, 0)
    for h in range(HEADS):
        peak[rows(h)] = jnp.broadcast_to(
            jnp.max(peak[rows(h)], axis=1, keepdims=True), (TOK, TOK)
        )
    total[...] = jnp.zeros_like(total)
    tgt[...] = jnp.zeros_like(tgt)
    ls[...] = jnp.zeros_like(ls)

    @pl.when(k == 1)
    def _():
        arrived(1, c - 1)

    level = local_levels()
    for h in range(HEADS):
        weighed(own_pair, h, pair_of(vals, own_pair), score, peak, total, tgt)
        mask = jnp.full((TOK, TOK), lw[h, 0], F32)
        for j in range(1, LOW + 1):
            mask = jnp.where(level == j, lw[h, j], mask)
        local[h] = mm_right_exact(sd[h] * mask, v_ref[...], 1, 0)

    def all_here(i, carry):
        zs = jnp.where(i == 0, z, chip_of(i))

        @pl.when(zs < z)
        def _():
            arrived(1, at(y, zs, 1 - k))

        @pl.when(second)
        def _():
            arrived(1, at(0, zs, 1 - k))

        return carry

    lax.fori_loop(0, 8, all_here, 0)
    level_weights(c, vals, lc, weights)

    @pl.when(k == 1)
    def _():
        keys = keys_all[c - 1].astype(F32).T
        for h in range(HEADS):
            ls[0, h] = mm_right_exact(keys * weights[c - 1, h : h + 1], vals[c - 1, :TOK], 1, 0)

    def use_values(p, carry):
        values = pair_of(vals, p)
        keys = pair_of(keys_all, p).astype(F32).T
        weight = jnp.concatenate([weights[2 * p], weights[2 * p + 1]], axis=1)
        j = jnp.int32(0)
        for b in range(4):
            j = j + (own_pair // (1 << b) != p // (1 << b)).astype(jnp.int32)
        for h in range(HEADS):
            weighed(p, h, values, score, peak, total, tgt)
            ls[j, h] += mm_right_exact(keys * weight[h : h + 1], values, 1, 0)
        return carry

    lax.fori_loop(0, own_pair, use_values, 0)
    for h in range(HEADS):
        tgt[h] = tgt[h] / jnp.sum(total[rows(h)], axis=1, keepdims=True)
    entry = jnp.exp(column_cumulative(g_ref[...]))
    sums_box[me] = student_whole(entry, wk, lw, gain, ls, tgt, qp, ks, comb, raw, local)

    outgoing = [
        remote("head", sums_box.at[me], sums_box.at[me], sums_send.at[d], sums_recv.at[me], peer)
        for d, peer in enumerate(head_peers)
    ]
    for copy in outgoing:
        copy.start()
    for d, peer in enumerate(head_peers):
        remote(
            "head", sums_box.at[peer], sums_box.at[peer], sums_send.at[d], sums_recv.at[peer], peer
        ).wait_recv()
    all_sums = sums_box[0]
    for i in range(1, HEADS):
        all_sums = all_sums + sums_box[i]
    small_part[...] = backward_inside(
        all_sums, entry, v_ref[...], wk, gain, ls, tgt, qp, kp, ks, mix, sd, raw, res, dstate, dquery, dkey
    )

    small_twin = remote("seq", small_part, small_pair, small_sem.at[0], small_sem.at[1], twin)
    small_twin.start()
    order = [(z + d) % 8 for d in far_first + (0,)]

    def twin_part(h):
        return remote("seq", grads.at[1 - k, h], pair.at[h], pair_send.at[h], pair_recv.at[h], twin)

    for h in order:
        q_rows = qs[pl.ds(pl.multiple_of(h * TOK, TOK), TOK)]
        grads[0, h] = mm_left_exact(q_rows, dquery[h], 0, 0)
        grads[1, h] = mm(comb[h], dstate[h], 1, 1) + mm_left_exact(k_ref[...], dkey[h], 0, 0)
        twin_part(h).start()
    small_twin.wait_recv()
    small_sum[...] = small_part[...] + small_pair[...]
    here = y * 8 + z

    def piece_to(h, a):
        return remote(
            "seq", part.at[h, a], box.at[here], part_send.at[h, a], part_recv.at[here], at(a, h, k)
        )

    for h in order:
        twin_part(h).wait_recv()
        tile = h % 3
        for a in range(2):
            part[h, a, :HALF] = grads[k, h, a * HALF : (a + 1) * HALF] + pair[h, a * HALF : (a + 1) * HALF]
            part[h, a, HALF:] = small_sum[pl.ds(pl.multiple_of(tile * 8, 8), 8)]
            act((h != z) | (a != y), piece_to(h, a))
    box[here] = part[z, y]
    for h in order:
        for a in range(2):
            source = a * 8 + h

            @pl.when((h != z) | (a != y))
            def _(source=source, h=h, a=a):
                remote(
                    "seq", part.at[h, a], box.at[source], part_send.at[h, a], part_recv.at[source], at(a, h, k)
                ).wait_recv()

    whole = box[0]
    for i in range(1, 16):
        whole = whole + box[i]
    done[k, z, y] = whole

    def sum_to(h, a):
        ref = done.at[k, z, y]
        return remote("seq", ref, ref, done_send.at[0, h, a], done_recv.at[0, z, y], at(a, h, k))

    def sum_from(h, a):
        ref = done.at[k, h, a]
        return remote("seq", ref, ref, done_send.at[0, h, a], done_recv.at[0, h, a], at(a, h, k))

    def sum_twin(core, h, a):
        ref = done.at[core, h, a]
        return remote("seq", ref, ref, done_send.at[1, h, a], done_recv.at[1, h, a], twin)

    for h in order:
        for a in range(2):
            act((h != z) | (a != y), sum_to(h, a))
    sum_twin(k, z, y).start()
    for h in [(z + d) % 8 for d in (0, 1, 7, 2, 6, 3, 5, 4)]:
        for a in range(2):

            @pl.when((h != z) | (a != y))
            def _(h=h, a=a):
                sum_from(h, a).wait_recv()
                sum_twin(k, h, a).start()

    for a in range(2):
        out[k, :, a * HALF : (a + 1) * HALF] = done[k, :, a, :HALF]
    tile = jnp.concatenate(
        [done[k, t, 0, HALF:] for t in range(2)] + [jnp.zeros((TOK - 16, TOK), F32)], axis=0
    ).T
    levels[...] = tile[:HEADS, :LEVELS]
    gains[...] = done[k, 2, 0, HALF:]
    for h in range(8):
        for a in range(2):
            sum_twin(1 - k, h, a).wait_recv()
    for a in range(2):
        out[1 - k, :, a * HALF : (a + 1) * HALF] = done[1 - k, :, a, :HALF]

    for phase in range(2):
        own_moves(phase, True)

        @pl.when(second)
        def _(phase=phase):
            for d in far_first:
                relayed(phase, d).wait_send()
            to_twin(phase, at(0, z, k)).wait_send()

        def sent(i, carry, phase=phase):
            zs = chip_of(i)
            act(zs < z, to_twin(phase, at(y, zs, k)), True)
            act(second, to_twin(phase, at(0, zs, k)), True)
            return carry

        lax.fori_loop(1, 8, sent, 0)
    for copy in outgoing + [small_twin]:
        copy.wait_send()
    for h in order:
        twin_part(h).wait_send()
        for a in range(2):
            act((h != z) | (a != y), piece_to(h, a), True)
            act((h != z) | (a != y), sum_to(h, a), True)
            sum_twin(k, h, a).wait_send()


VM = pl.BlockSpec(memory_space=pltpu.VMEM)
SM = pl.BlockSpec(memory_space=pltpu.SMEM)
ANY = pl.BlockSpec(memory_space=pl.ANY)
DMA = pltpu.SemaphoreType.DMA


def shaped(shape, dtype=F32):
    return jax.ShapeDtypeStruct(shape, dtype)


def on_device(queries, key_vectors, value_vectors, log_gate, query_map, key_map, lw, norm_gain):
    matrix = pltpu.VMEM((HEADS, TOK, HD), F32)
    small = pltpu.VMEM((SMALL, TOK), F32)
    out, levels, gains = pl.pallas_call(
        whole_kernel,
        out_shape=(shaped((2, HEADS, HD, HD)), shaped((HEADS, LEVELS)), shaped((HEADS, HD))),
        in_specs=[ANY, VM, VM, VM, ANY, ANY, SM, VM],
        out_specs=(VM,) * 3,
        scratch_shapes=[
            pltpu.VMEM((HEADS * TOK, HD), BF),
            matrix,
            matrix,
            pltpu.VMEM((SPANS, TOK, HD), BF),
            pltpu.VMEM((SPANS, VALUE_ROWS, HD), BF),
            pltpu.VMEM((SPANS // 2, HEADS * TOK, 2 * TOK), F32),
            pltpu.VMEM((HEADS * TOK, TOK), F32),
            pltpu.VMEM((HEADS * TOK, TOK), F32),
            matrix,
            pltpu.VMEM((SPANS * GATE_ROWS, TOK), F32),
            pltpu.VMEM((SPANS, HEADS, TOK), F32),
            pltpu.VMEM((CROSS, HEADS, HD, HD), F32),
            *[matrix] * 12,
            pltpu.VMEM((2, HEADS, HD, HD), F32),
            matrix,
            pltpu.VMEM((HEADS, 2, PIECE, HD), F32),
            pltpu.VMEM((16, PIECE, HD), F32),
            pltpu.VMEM((2, HEADS, 2, PIECE, HD), F32),
            pltpu.VMEM((HEADS, 8, TOK), F32),
            small,
            small,
            small,
            DMA((10,)),
            DMA((2, 8)),
            DMA((2, 8)),
            DMA((2, SPANS)),
            DMA((2, SPANS)),
            DMA((7,)),
            DMA((HEADS,)),
            DMA((8,)),
            DMA((8,)),
            DMA((8, 2)),
            DMA((16,)),
            DMA((2, 8, 2)),
            DMA((2, 8, 2)),
            DMA((2,)),
        ],
        compiler_params=pltpu.CompilerParams(
            collective_id=0, has_side_effects=True, vmem_limit_bytes=LIMIT
        ),
        name="distill",
    )(
        queries, key_vectors, value_vectors, log_gate, query_map, key_map, lw,
        norm_gain.reshape(HEADS, HD),
    )
    return out[0], out[1], levels, gains.reshape(-1)


def solution(mesh):
    return jax.shard_map(
        on_device,
        mesh=mesh,
        in_specs=(
            P("seq", "head"),
            P("seq", "head"),
            P("seq", "head"),
            P("head", "seq"),
            P("head", None, None),
            P("head", None, None),
            P("head", None),
            P("head"),
        ),
        out_specs=(P("head", None, None), P("head", None, None), P("head", None), P("head")),
        check_vma=False,
    )
```

```python
import jax
import jax.numpy as jnp
from jax import lax
from jax.experimental import pallas as pl
from jax.experimental.pallas import tpu as pltpu
from jax.sharding import PartitionSpec as P

F32 = jnp.float32
BF = jnp.bfloat16
HIGHEST = lax.Precision.HIGHEST
MESH = pl.DeviceIdType.MESH
NEGATIVE = -1e30
EPSILON = 1e-05
HD = 128
TOK = 128
HEADS = 8
SPANS = 32
LEVELS = 13
LOW = 7
CROSS = 5
TOKENS = TOK * SPANS
WIDTH = 64 * HD
SMALL = 24
GATE_ROWS = 32
KEY_ROWS = 128 + GATE_ROWS
PIECE = 64 + 8
HALF = HD // 2
LOG2E = 1.4426950408889634
SCALE = HD**-0.5 * LOG2E
LIMIT = 58 << 20


def pieces(a):
    high = a.astype(BF)
    return high, (a - high.astype(F32)).astype(BF)


def dg(a, b, ca, cb, precision=None):
    return lax.dot_general(
        a, b, (((ca,), (cb,)), ((), ())), preferred_element_type=F32, precision=precision
    )


def halves(o):
    n = o.shape[1] // 2
    return o[:, :n] + o[:, n:]


def mm(a, b, ca, cb):
    bh, bl = pieces(b)
    left = jnp.concatenate(pieces(a), axis=ca)
    right = jnp.concatenate(
        [jnp.concatenate([bh, bh], axis=cb), jnp.concatenate([bl, bl], axis=cb)], axis=1 - cb
    )
    return halves(dg(left, right, ca, cb))


def mm_left_exact(a, b, ca, cb):
    return halves(dg(a, jnp.concatenate(pieces(b), axis=1 - cb), ca, cb))


def mm_right_exact(a, b, ca, cb):
    return dg(jnp.concatenate(pieces(a), axis=ca), jnp.concatenate([b, b], axis=cb), ca, cb)


def iota(shape, dim):
    return lax.broadcasted_iota(jnp.int32, shape, dim)


def local_levels():
    x = jnp.bitwise_xor(iota((TOK, TOK), 0), iota((TOK, TOK), 1))
    level = jnp.zeros_like(x)
    for bit in range(LOW):
        level = level + (x >= 1 << bit).astype(jnp.int32)
    return level


def rows(h):
    return slice(h * TOK, (h + 1) * TOK)


def column_cumulative(gates):
    lower = (iota((TOK, TOK), 1) <= iota((TOK, TOK), 0)).astype(F32)
    return dg(lower, gates, 1, 1, HIGHEST)


def pair_of(ref, p):
    return jnp.concatenate([ref[2 * p, :TOK], ref[2 * p + 1, :TOK]], axis=0)


def scored(c, p, masked, qs, keys_all, peak, score):
    keys = pair_of(keys_all, p)
    for h in range(HEADS):
        s = dg(qs[rows(h)], keys, 1, 1)
        if masked:
            place_of = 2 * TOK * p + iota((TOK, 2 * TOK), 1)
            s = jnp.where(place_of <= c * TOK + iota((TOK, 2 * TOK), 0), s, NEGATIVE)
        score[p, rows(h)] = s
        top = jnp.maximum(s[:, :TOK], s[:, TOK:])
        peak[rows(h)] = top if masked else jnp.maximum(peak[rows(h)], top)


def weighed(p, h, values, score, peak, total, tgt):
    s = score[p, rows(h)]
    top = peak[rows(h)]
    w0 = jnp.exp2((s[:, :TOK] - top) * SCALE)
    w1 = jnp.exp2((s[:, TOK:] - top) * SCALE)
    total[rows(h)] += w0 + w1
    tgt[h] += dg(jnp.concatenate([w0.astype(BF), w1.astype(BF)], axis=1), values, 1, 0)


def level_weights(c, keys_all, lc, weights):
    upper = (iota((TOK, TOK), 0) <= iota((TOK, TOK), 1)).astype(BF)
    lc[...] = dg(keys_all[:, TOK:].reshape(SPANS * GATE_ROWS, TOK), upper, 1, 0)

    def step(i, since):
        x = c - 1 - i
        three = lc[pl.ds(pl.multiple_of(x * GATE_ROWS, GATE_ROWS), 3 * HEADS)]
        own = three[:HEADS] + three[HEADS : 2 * HEADS] + three[2 * HEADS :]
        since = since + own[:, TOK - 1 :]
        weights[x] = jnp.exp(since - own)
        return since

    lax.fori_loop(0, c, step, jnp.zeros((HEADS, 1), F32))


def gate_pieces(gate):
    high = gate.astype(BF).astype(F32)
    middle = (gate - high).astype(BF).astype(F32)
    low = gate - high - middle
    return jnp.concatenate([high, middle, low, jnp.zeros_like(gate)], axis=0).astype(BF)


def student_inside(qs, key, gate, wq, wk, lw, qp, kp, mix, sd):
    upper = (iota((TOK, TOK), 0) <= iota((TOK, TOK), 1)).astype(F32)
    row_cum = dg(gate, upper, 1, 0, HIGHEST)
    col_cum = column_cumulative(gate)
    causal = iota((TOK, TOK), 1) <= iota((TOK, TOK), 0)
    level = local_levels()
    for h in range(HEADS):
        qp[h] = mm_left_exact(qs[rows(h)], wq[h], 1, 0)
        kp[h] = mm_left_exact(key, wk[h], 1, 0)
    for h in range(HEADS):
        decay = jnp.exp(
            jnp.where(causal, col_cum[:, h : h + 1] - row_cum[h : h + 1], NEGATIVE)
        )
        mask = jnp.full((TOK, TOK), lw[h, 0], F32)
        for j in range(1, LOW + 1):
            mask = jnp.where(level == j, lw[h, j], mask)
        sd[h] = mm(qp[h], kp[h], 1, 1) * decay
        mix[h] = decay * mask


def student_whole(entry, wk, lw, gain, ls, tgt, qp, ks, comb, raw, local):
    for h in range(HEADS):
        combined = lw[h, LOW + 1] * ls[0, h]
        for j in range(1, CROSS):
            combined = combined + lw[h, LOW + 1 + j] * ls[j, h]
        comb[h] = combined
        ks[h] = mm(wk[h], combined, 0, 0)
    square = jnp.zeros((TOK, HD), F32)
    scaled = jnp.zeros((TOK, HD), F32)
    against = jnp.zeros((TOK, HD), F32)
    for h in range(HEADS):
        r = local[h] + entry[:, h : h + 1] * mm(qp[h], ks[h], 1, 0)
        raw[h] = r
        rg = r * gain[h : h + 1]
        square = square + r * r
        scaled = scaled + rg * rg
        against = against + tgt[h] * rg
    one = jnp.ones((8, HD), F32)
    tile = [dg(one, x, 1, 1, HIGHEST) for x in (square, scaled, against)]
    return jnp.concatenate([t[:1] for t in tile] + [tile[0][:5]], axis=0)


def backward_inside(
    all_sums, entry, value, wk, gain, ls, tgt, qp, kp, ks, mix, sd, raw, res, dstate, dquery, dkey
):
    eye = (iota((TOK, TOK), 0) == iota((TOK, TOK), 1)).astype(F32)
    level = local_levels()
    column = dg(eye, all_sums, 1, 1, HIGHEST)
    inverse = lax.rsqrt(column[:, 0:1] / WIDTH + EPSILON)
    inner = (inverse * column[:, 1:2] - column[:, 2:3]) / TOKENS
    back = inverse * inverse * inverse * inner / WIDTH
    gain_rows = []
    for h in range(HEADS):
        g = gain[h : h + 1]
        normed = raw[h] * inverse
        mismatch = (normed * g - tgt[h]) * (1.0 / TOKENS)
        gain_rows.append(jnp.sum(mismatch * normed, axis=0, keepdims=True))
        res[h] = inverse * (mismatch * g) - raw[h] * back
    lane = iota((16, TOK), 1)
    level_tile = jnp.zeros((16, TOK), F32)
    for h in range(HEADS):
        e = entry[:, h : h + 1]
        d_mix = mm_right_exact(res[h], value, 1, 1)
        d_scores = d_mix * mix[h]
        through = d_mix * sd[h]
        dstate[h] = mm(e * qp[h], res[h], 0, 0)
        d_comb = mm(wk[h], dstate[h], 1, 0)
        dquery[h] = mm(d_scores, kp[h], 1, 0) + e * mm(res[h], ks[h], 1, 1)
        dkey[h] = mm(d_scores, qp[h], 0, 0)
        lines = [
            jnp.sum(jnp.where(level == j, through, 0.0), axis=0, keepdims=True)
            for j in range(LOW + 1)
        ]
        lines += [jnp.sum(ls[j, h] * d_comb, axis=0, keepdims=True) for j in range(CROSS)]
        lines.append(jnp.zeros((16 - LEVELS, TOK), F32))
        summed = jnp.sum(jnp.concatenate(lines, axis=0), axis=1, keepdims=True)
        level_tile = jnp.where(lane == h, summed, level_tile)
    return jnp.concatenate([level_tile] + gain_rows, axis=0)


def at(y, z, k):
    return y * 16 + z * 2 + k


def remote(axis, src, dst, send, recv, target):
    return pltpu.make_async_remote_copy(
        src_ref=src, dst_ref=dst, send_sem=send, recv_sem=recv,
        device_id={axis: target}, device_id_type=MESH,
    )


def whole_kernel(
    q_hbm, k_ref, v_ref, g_ref, wq_hbm, wk_hbm, lw, gain,
    done,
    qs, wq, wk, keys_all, vals, score, peak, total, tgt, lc, weights, ls, qp, kp, ks, comb, mix, sd, raw, res, local,
    dstate, dquery, dkey, grads, pair, part, box, sums_box, small_part, small_pair, small_sum,
    load, own_send, across_send, relay_send, twin_send, recv, sums_send, sums_recv, pair_send, pair_recv,
    part_send, part_recv, done_send, done_recv, small_sem,
):
    c = lax.axis_index("seq")
    y, z, k = c // 16, c // 2 % 8, c % 2
    own_pair = c // 2
    second = y == 1
    twin, across = at(y, z, 1 - k), at(1 - y, z, k)
    far_first = (4, 3, 5, 2, 6, 1, 7)
    me = lax.axis_index("head")
    head_peers = [(me + d) % HEADS for d in range(1, HEADS)]

    barrier = pltpu.get_barrier_semaphore()
    for d in range(8):
        for other in range(2):
            if d or other:
                target = at((y + other) % 2, (z + d) % 8, k)
                pl.semaphore_signal(barrier, inc=1, device_id={"seq": target}, device_id_type=MESH)
    pl.semaphore_signal(barrier, inc=1, device_id={"seq": twin}, device_id_type=MESH)
    for peer in head_peers:
        pl.semaphore_signal(barrier, inc=1, device_id={"head": peer}, device_id_type=MESH)

    loads = [
        pltpu.make_async_copy(q_hbm.at[:, rows(h)], qs.at[rows(h)], load.at[h])
        for h in range(HEADS)
    ]
    loads.append(pltpu.make_async_copy(wq_hbm, wq, load.at[8]))
    loads.append(pltpu.make_async_copy(wk_hbm, wk, load.at[9]))
    for copy in loads:
        copy.start()
    keys_all[c, :TOK] = k_ref[...]
    keys_all[c, TOK:] = gate_pieces(g_ref[...])
    vals[c] = v_ref[...]

    @pl.when(k == 0)
    def _():
        keys_all[c + 1] = jnp.zeros((KEY_ROWS, HD), BF)
        vals[c + 1] = jnp.zeros((TOK, HD), BF)

    for copy in loads:
        copy.wait()
    student_inside(qs, k_ref[...], g_ref[...], wq, wk, lw, qp, kp, mix, sd)
    pl.semaphore_wait(barrier, 23)

    def block(phase, slot):
        return keys_all.at[slot] if phase == 0 else vals.at[slot]

    def copy_of(phase, slot, sem, target):
        ref = block(phase, slot)
        return remote("seq", ref, ref, sem, recv.at[phase, slot], target)

    def to_twin(phase, slot):
        return copy_of(phase, slot, twin_send.at[phase, slot], twin)

    def to_across(phase, zs):
        return copy_of(phase, at(0, zs, k), across_send.at[phase, zs], across)

    def to_row(phase, d):
        return copy_of(phase, c, own_send.at[phase, d], at(y, (z + d) % 8, k))

    def relayed(phase, d):
        return copy_of(phase, at(0, z, k), relay_send.at[phase, d], at(y, (z + d) % 8, k))

    def act(when, copy, wait=False):
        @pl.when(when)
        def _():
            if wait:
                copy.wait_send()
            else:
                copy.start()

    row_first = (y == 0) & (k == 0)

    def own_moves(phase, wait=False):
        act(y == 0, to_across(phase, z), wait)
        act(k == 0, to_twin(phase, c), wait)
        for d in far_first:
            act((z + d < 8) | row_first, to_row(phase, d), wait)

    def arrived(phase, slot):
        to_twin(phase, slot).wait_recv()

    def relay(phase):
        @pl.when(second)
        def _():
            slot = at(0, z, k)
            arrived(phase, slot)
            for d in far_first:
                act(k == 1, relayed(phase, d))
            to_twin(phase, slot).start()

    def chip_of(i):
        d = jnp.where(i % 2 == 1, (i + 1) // 2, 8 - i // 2)
        return (z + 8 - d) % 8

    def forward(phase, i):
        zs = chip_of(i)

        @pl.when((zs < z) | row_first)
        def _():
            slot = at(y, zs, k)
            arrived(phase, slot)
            act(row_first, to_across(phase, zs))
            act(zs < z, to_twin(phase, slot))

        @pl.when(second)
        def _():
            slot = at(0, zs, k)
            arrived(phase, slot)
            to_twin(phase, slot).start()

    def pairs(phase, i, use):
        zs = jnp.where(i == 0, z, chip_of(i))

        def one(other, carry):
            @pl.when((other == 0) & (zs < z) | (other == 1) & second)
            def _():
                ys = y * (1 - other)
                arrived(phase, at(ys, zs, 1 - k))
                use(ys * 8 + zs)

            return carry

        lax.fori_loop(0, 2, one, 0)

    own_moves(0)

    @pl.when(k == 1)
    def _():
        arrived(0, c - 1)

    scored(c, own_pair, True, qs, keys_all, peak, score)
    relay(0)
    own_moves(1)
    relay(1)

    def key_step(i, carry):
        @pl.when(i < 8)
        def _():
            forward(0, i)

        pairs(0, i - 1, lambda p: scored(c, p, False, qs, keys_all, peak, score))
        return carry

    lax.fori_loop(1, 9, key_step, 0)
    for h in range(HEADS):
        peak[rows(h)] = jnp.broadcast_to(
            jnp.max(peak[rows(h)], axis=1, keepdims=True), (TOK, TOK)
        )
    total[...] = jnp.zeros_like(total)
    tgt[...] = jnp.zeros_like(tgt)
    ls[...] = jnp.zeros_like(ls)
    level_weights(c, keys_all, lc, weights)

    @pl.when(k == 1)
    def _():
        arrived(1, c - 1)
        keys = keys_all[c - 1, :TOK].astype(F32).T
        for h in range(HEADS):
            ls[0, h] = mm_right_exact(keys * weights[c - 1, h : h + 1], vals[c - 1], 1, 0)

    level = local_levels()
    for h in range(HEADS):
        weighed(own_pair, h, pair_of(vals, own_pair), score, peak, total, tgt)
        mask = jnp.full((TOK, TOK), lw[h, 0], F32)
        for j in range(1, LOW + 1):
            mask = jnp.where(level == j, lw[h, j], mask)
        local[h] = mm_right_exact(sd[h] * mask, v_ref[...], 1, 0)

    def use_values(p):
        values = pair_of(vals, p)
        keys = pair_of(keys_all, p).astype(F32).T
        weight = jnp.concatenate([weights[2 * p], weights[2 * p + 1]], axis=1)
        j = jnp.int32(0)
        for b in range(4):
            j = j + (own_pair // (1 << b) != p // (1 << b)).astype(jnp.int32)
        for h in range(HEADS):
            weighed(p, h, values, score, peak, total, tgt)
            ls[j, h] += mm_right_exact(keys * weight[h : h + 1], values, 1, 0)

    def value_step(i, carry):
        @pl.when(i < 8)
        def _():
            forward(1, i)

        pairs(1, i - 1, use_values)
        return carry

    lax.fori_loop(1, 9, value_step, 0)
    for h in range(HEADS):
        tgt[h] = tgt[h] / jnp.sum(total[rows(h)], axis=1, keepdims=True)
    entry = jnp.exp(column_cumulative(g_ref[...]))
    sums_box[me] = student_whole(entry, wk, lw, gain, ls, tgt, qp, ks, comb, raw, local)

    outgoing = [
        remote("head", sums_box.at[me], sums_box.at[me], sums_send.at[d], sums_recv.at[me], peer)
        for d, peer in enumerate(head_peers)
    ]
    for copy in outgoing:
        copy.start()
    for d, peer in enumerate(head_peers):
        remote(
            "head", sums_box.at[peer], sums_box.at[peer], sums_send.at[d], sums_recv.at[peer], peer
        ).wait_recv()
    all_sums = sums_box[0]
    for i in range(1, HEADS):
        all_sums = all_sums + sums_box[i]
    small_part[...] = backward_inside(
        all_sums, entry, v_ref[...], wk, gain, ls, tgt, qp, kp, ks, mix, sd, raw, res, dstate, dquery, dkey
    )

    small_twin = remote("seq", small_part, small_pair, small_sem.at[0], small_sem.at[1], twin)
    small_twin.start()
    order = [(z + d) % 8 for d in far_first + (0,)]

    def twin_part(h):
        return remote("seq", grads.at[1 - k, h], pair.at[h], pair_send.at[h], pair_recv.at[h], twin)

    for h in order:
        q_rows = qs[pl.ds(pl.multiple_of(h * TOK, TOK), TOK)]
        grads[0, h] = mm_left_exact(q_rows, dquery[h], 0, 0)
        grads[1, h] = mm(comb[h], dstate[h], 1, 1) + mm_left_exact(k_ref[...], dkey[h], 0, 0)
        twin_part(h).start()
    small_twin.wait_recv()
    small_sum[...] = small_part[...] + small_pair[...]
    here = y * 8 + z

    def piece_to(h, a):
        return remote(
            "seq", part.at[h, a], box.at[here], part_send.at[h, a], part_recv.at[here], at(a, h, k)
        )

    for h in order:
        twin_part(h).wait_recv()
        tile = h % 3
        for a in range(2):
            part[h, a, :HALF] = grads[k, h, a * HALF : (a + 1) * HALF] + pair[h, a * HALF : (a + 1) * HALF]
            part[h, a, HALF:] = small_sum[pl.ds(pl.multiple_of(tile * 8, 8), 8)]
            act((h != z) | (a != y), piece_to(h, a))
    box[here] = part[z, y]
    for h in order:
        for a in range(2):
            source = a * 8 + h

            @pl.when((h != z) | (a != y))
            def _(source=source, h=h, a=a):
                remote(
                    "seq", part.at[h, a], box.at[source], part_send.at[h, a], part_recv.at[source], at(a, h, k)
                ).wait_recv()

    whole = box[0]
    for i in range(1, 16):
        whole = whole + box[i]
    done[k, z, y] = whole

    def sum_to(h, a):
        ref = done.at[k, z, y]
        return remote("seq", ref, ref, done_send.at[0, h, a], done_recv.at[0, z, y], at(a, h, k))

    def sum_from(h, a):
        ref = done.at[k, h, a]
        return remote("seq", ref, ref, done_send.at[0, h, a], done_recv.at[0, h, a], at(a, h, k))

    def sum_twin(core, h, a):
        ref = done.at[core, h, a]
        return remote("seq", ref, ref, done_send.at[1, h, a], done_recv.at[1, h, a], twin)

    for h in order:
        for a in range(2):
            act((h != z) | (a != y), sum_to(h, a))
    sum_twin(k, z, y).start()
    for h in [(z + d) % 8 for d in (0, 1, 7, 2, 6, 3, 5, 4)]:
        for a in range(2):

            @pl.when((h != z) | (a != y))
            def _(h=h, a=a):
                sum_from(h, a).wait_recv()
                sum_twin(k, h, a).start()

    for h in range(8):
        for a in range(2):
            sum_twin(1 - k, h, a).wait_recv()

    for phase in range(2):
        own_moves(phase, True)

        for d in far_first:
            act(second & (k == 1), relayed(phase, d), True)
        act(second, to_twin(phase, at(0, z, k)), True)

        def sent(i, carry, phase=phase):
            zs = chip_of(i)
            act(row_first, to_across(phase, zs), True)
            act(zs < z, to_twin(phase, at(y, zs, k)), True)
            act(second, to_twin(phase, at(0, zs, k)), True)
            return carry

        lax.fori_loop(1, 8, sent, 0)
    for copy in outgoing + [small_twin]:
        copy.wait_send()
    for h in order:
        twin_part(h).wait_send()
        for a in range(2):
            act((h != z) | (a != y), piece_to(h, a), True)
            act((h != z) | (a != y), sum_to(h, a), True)
            sum_twin(k, h, a).wait_send()


def written_kernel(done, grad_query, grad_key, levels, gains):
    for which, ref in enumerate((grad_query, grad_key)):
        for a in range(2):
            ref[:, a * HALF : (a + 1) * HALF] = done[which, :, a, :HALF]
    tile = jnp.concatenate(
        [done[0, t, 0, HALF:] for t in range(2)] + [jnp.zeros((TOK - 16, TOK), F32)], axis=0
    ).T
    levels[...] = tile[:HEADS, :LEVELS]
    gains[...] = done[0, 2, 0, HALF:]


VM = pl.BlockSpec(memory_space=pltpu.VMEM)
SM = pl.BlockSpec(memory_space=pltpu.SMEM)
ANY = pl.BlockSpec(memory_space=pl.ANY)
DMA = pltpu.SemaphoreType.DMA


def shaped(shape, dtype=F32):
    return jax.ShapeDtypeStruct(shape, dtype)


def on_device(queries, key_vectors, value_vectors, log_gate, query_map, key_map, lw, norm_gain):
    matrix = pltpu.VMEM((HEADS, TOK, HD), F32)
    small = pltpu.VMEM((SMALL, TOK), F32)
    done = pl.pallas_call(
        whole_kernel,
        out_shape=shaped((2, HEADS, 2, PIECE, HD)),
        in_specs=[ANY, VM, VM, VM, ANY, ANY, SM, VM],
        out_specs=VM,
        scratch_shapes=[
            pltpu.VMEM((HEADS * TOK, HD), BF),
            matrix,
            matrix,
            pltpu.VMEM((SPANS, KEY_ROWS, HD), BF),
            pltpu.VMEM((SPANS, TOK, HD), BF),
            pltpu.VMEM((SPANS // 2, HEADS * TOK, 2 * TOK), F32),
            pltpu.VMEM((HEADS * TOK, TOK), F32),
            pltpu.VMEM((HEADS * TOK, TOK), F32),
            matrix,
            pltpu.VMEM((SPANS * GATE_ROWS, TOK), F32),
            pltpu.VMEM((SPANS, HEADS, TOK), F32),
            pltpu.VMEM((CROSS, HEADS, HD, HD), F32),
            *[matrix] * 12,
            pltpu.VMEM((2, HEADS, HD, HD), F32),
            matrix,
            pltpu.VMEM((HEADS, 2, PIECE, HD), F32),
            pltpu.VMEM((16, PIECE, HD), F32),
            pltpu.VMEM((HEADS, 8, TOK), F32),
            small,
            small,
            small,
            DMA((10,)),
            DMA((2, 8)),
            DMA((2, 8)),
            DMA((2, 8)),
            DMA((2, SPANS)),
            DMA((2, SPANS)),
            DMA((7,)),
            DMA((HEADS,)),
            DMA((8,)),
            DMA((8,)),
            DMA((8, 2)),
            DMA((16,)),
            DMA((2, 8, 2)),
            DMA((2, 8, 2)),
            DMA((2,)),
        ],
        compiler_params=pltpu.CompilerParams(
            collective_id=0, has_side_effects=True, vmem_limit_bytes=LIMIT
        ),
        name="distill",
    )(
        queries, key_vectors, value_vectors, log_gate, query_map, key_map, lw,
        norm_gain.reshape(HEADS, HD),
    )
    grad_query, grad_key, levels, gains = pl.pallas_call(
        written_kernel,
        out_shape=(
            shaped((HEADS, HD, HD)),
            shaped((HEADS, HD, HD)),
            shaped((HEADS, LEVELS)),
            shaped((HEADS, HD)),
        ),
        in_specs=[VM],
        out_specs=(VM,) * 4,
        name="written",
    )(done)
    return grad_query, grad_key, levels, gains.reshape(-1)


def solution(mesh):
    return jax.shard_map(
        on_device,
        mesh=mesh,
        in_specs=(
            P("seq", "head"),
            P("seq", "head"),
            P("seq", "head"),
            P("head", "seq"),
            P("head", None, None),
            P("head", None, None),
            P("head", None),
            P("head"),
        ),
        out_specs=(P("head", None, None), P("head", None, None), P("head", None), P("head")),
        check_vma=False,
    )
```

```python
import jax
import jax.numpy as jnp
from jax import lax
from jax.experimental import pallas as pl
from jax.experimental.pallas import tpu as pltpu
from jax.sharding import PartitionSpec as P

F32 = jnp.float32
BF = jnp.bfloat16
HIGHEST = lax.Precision.HIGHEST
MESH = pl.DeviceIdType.MESH
NEGATIVE = -1e30
EPSILON = 1e-05
HD = 128
TOK = 128
HEADS = 8
SPANS = 32
LEVELS = 13
LOW = 7
CROSS = 5
TOKENS = TOK * SPANS
WIDTH = 64 * HD
SMALL = 24
GATE_ROWS = 32
KEY_ROWS = 128 + GATE_ROWS
PIECE = 128 + 8
LOG2E = 1.4426950408889634
SCALE = HD**-0.5 * LOG2E
LIMIT = 58 << 20


def pieces(a):
    high = a.astype(BF)
    return high, (a - high.astype(F32)).astype(BF)


def dg(a, b, ca, cb, precision=None):
    return lax.dot_general(
        a, b, (((ca,), (cb,)), ((), ())), preferred_element_type=F32, precision=precision
    )


def halves(o):
    n = o.shape[1] // 2
    return o[:, :n] + o[:, n:]


def mm(a, b, ca, cb):
    bh, bl = pieces(b)
    left = jnp.concatenate(pieces(a), axis=ca)
    right = jnp.concatenate(
        [jnp.concatenate([bh, bh], axis=cb), jnp.concatenate([bl, bl], axis=cb)], axis=1 - cb
    )
    return halves(dg(left, right, ca, cb))


def mm_left_exact(a, b, ca, cb):
    return halves(dg(a, jnp.concatenate(pieces(b), axis=1 - cb), ca, cb))


def mm_right_exact(a, b, ca, cb):
    return dg(jnp.concatenate(pieces(a), axis=ca), jnp.concatenate([b, b], axis=cb), ca, cb)


def iota(shape, dim):
    return lax.broadcasted_iota(jnp.int32, shape, dim)


def local_levels():
    x = jnp.bitwise_xor(iota((TOK, TOK), 0), iota((TOK, TOK), 1))
    level = jnp.zeros_like(x)
    for bit in range(LOW):
        level = level + (x >= 1 << bit).astype(jnp.int32)
    return level


def rows(h):
    return slice(h * TOK, (h + 1) * TOK)


def column_cumulative(gates):
    lower = (iota((TOK, TOK), 1) <= iota((TOK, TOK), 0)).astype(F32)
    return dg(lower, gates, 1, 1, HIGHEST)


def pair_of(ref, p):
    return jnp.concatenate([ref[2 * p, :TOK], ref[2 * p + 1, :TOK]], axis=0)


def scored(c, p, masked, qs, keys_all, peak, score):
    keys = pair_of(keys_all, p)
    for h in range(HEADS):
        s = dg(qs[rows(h)], keys, 1, 1)
        if masked:
            place_of = 2 * TOK * p + iota((TOK, 2 * TOK), 1)
            s = jnp.where(place_of <= c * TOK + iota((TOK, 2 * TOK), 0), s, NEGATIVE)
        score[p, rows(h)] = s
        top = jnp.maximum(s[:, :TOK], s[:, TOK:])
        peak[rows(h)] = top if masked else jnp.maximum(peak[rows(h)], top)


def weighed(p, h, values, score, peak, total, tgt):
    s = score[p, rows(h)]
    top = peak[rows(h)]
    w0 = jnp.exp2((s[:, :TOK] - top) * SCALE)
    w1 = jnp.exp2((s[:, TOK:] - top) * SCALE)
    total[rows(h)] += w0 + w1
    tgt[h] += dg(jnp.concatenate([w0.astype(BF), w1.astype(BF)], axis=1), values, 1, 0)


def level_weights(c, keys_all, lc, weights):
    upper = (iota((TOK, TOK), 0) <= iota((TOK, TOK), 1)).astype(BF)
    lc[...] = dg(keys_all[:, TOK:].reshape(SPANS * GATE_ROWS, TOK), upper, 1, 0)

    def step(i, since):
        x = c - 1 - i
        three = lc[pl.ds(pl.multiple_of(x * GATE_ROWS, GATE_ROWS), 3 * HEADS)]
        own = three[:HEADS] + three[HEADS : 2 * HEADS] + three[2 * HEADS :]
        since = since + own[:, TOK - 1 :]
        weights[x] = jnp.exp(since - own)
        return since

    lax.fori_loop(0, c, step, jnp.zeros((HEADS, 1), F32))


def gate_pieces(gate):
    high = gate.astype(BF).astype(F32)
    middle = (gate - high).astype(BF).astype(F32)
    low = gate - high - middle
    return jnp.concatenate([high, middle, low, jnp.zeros_like(gate)], axis=0).astype(BF)


def student_inside(qs, key, gate, wq, wk, lw, qp, kp, mix, sd):
    upper = (iota((TOK, TOK), 0) <= iota((TOK, TOK), 1)).astype(F32)
    row_cum = dg(gate, upper, 1, 0, HIGHEST)
    col_cum = column_cumulative(gate)
    causal = iota((TOK, TOK), 1) <= iota((TOK, TOK), 0)
    level = local_levels()
    for h in range(HEADS):
        qp[h] = mm_left_exact(qs[rows(h)], wq[h], 1, 0)
        kp[h] = mm_left_exact(key, wk[h], 1, 0)
    for h in range(HEADS):
        decay = jnp.exp(
            jnp.where(causal, col_cum[:, h : h + 1] - row_cum[h : h + 1], NEGATIVE)
        )
        mask = jnp.full((TOK, TOK), lw[h, 0], F32)
        for j in range(1, LOW + 1):
            mask = jnp.where(level == j, lw[h, j], mask)
        sd[h] = mm(qp[h], kp[h], 1, 1) * decay
        mix[h] = decay * mask


def student_whole(entry, wk, lw, gain, ls, tgt, qp, ks, comb, raw, local):
    for h in range(HEADS):
        combined = lw[h, LOW + 1] * ls[0, h]
        for j in range(1, CROSS):
            combined = combined + lw[h, LOW + 1 + j] * ls[j, h]
        comb[h] = combined
        ks[h] = mm(wk[h], combined, 0, 0)
    square = jnp.zeros((TOK, HD), F32)
    scaled = jnp.zeros((TOK, HD), F32)
    against = jnp.zeros((TOK, HD), F32)
    for h in range(HEADS):
        r = local[h] + entry[:, h : h + 1] * mm(qp[h], ks[h], 1, 0)
        raw[h] = r
        rg = r * gain[h : h + 1]
        square = square + r * r
        scaled = scaled + rg * rg
        against = against + tgt[h] * rg
    one = jnp.ones((8, HD), F32)
    tile = [dg(one, x, 1, 1, HIGHEST) for x in (square, scaled, against)]
    return jnp.concatenate([t[:1] for t in tile] + [tile[0][:5]], axis=0)


def backward_inside(
    all_sums, entry, value, wk, gain, ls, tgt, qp, kp, ks, mix, sd, raw, res, dstate, dquery, dkey
):
    eye = (iota((TOK, TOK), 0) == iota((TOK, TOK), 1)).astype(F32)
    level = local_levels()
    column = dg(eye, all_sums, 1, 1, HIGHEST)
    inverse = lax.rsqrt(column[:, 0:1] / WIDTH + EPSILON)
    inner = (inverse * column[:, 1:2] - column[:, 2:3]) / TOKENS
    back = inverse * inverse * inverse * inner / WIDTH
    gain_rows = []
    for h in range(HEADS):
        g = gain[h : h + 1]
        normed = raw[h] * inverse
        mismatch = (normed * g - tgt[h]) * (1.0 / TOKENS)
        gain_rows.append(jnp.sum(mismatch * normed, axis=0, keepdims=True))
        res[h] = inverse * (mismatch * g) - raw[h] * back
    lane = iota((16, TOK), 1)
    level_tile = jnp.zeros((16, TOK), F32)
    for h in range(HEADS):
        e = entry[:, h : h + 1]
        d_mix = mm_right_exact(res[h], value, 1, 1)
        d_scores = d_mix * mix[h]
        through = d_mix * sd[h]
        dstate[h] = mm(e * qp[h], res[h], 0, 0)
        d_comb = mm(wk[h], dstate[h], 1, 0)
        dquery[h] = mm(d_scores, kp[h], 1, 0) + e * mm(res[h], ks[h], 1, 1)
        dkey[h] = mm(d_scores, qp[h], 0, 0)
        lines = [
            jnp.sum(jnp.where(level == j, through, 0.0), axis=0, keepdims=True)
            for j in range(LOW + 1)
        ]
        lines += [jnp.sum(ls[j, h] * d_comb, axis=0, keepdims=True) for j in range(CROSS)]
        lines.append(jnp.zeros((16 - LEVELS, TOK), F32))
        summed = jnp.sum(jnp.concatenate(lines, axis=0), axis=1, keepdims=True)
        level_tile = jnp.where(lane == h, summed, level_tile)
    return jnp.concatenate([level_tile] + gain_rows, axis=0)


def at(y, z, k):
    return y * 16 + z * 2 + k


def remote(axis, src, dst, send, recv, target):
    return pltpu.make_async_remote_copy(
        src_ref=src, dst_ref=dst, send_sem=send, recv_sem=recv,
        device_id={axis: target}, device_id_type=MESH,
    )


def whole_kernel(
    q_hbm, k_ref, v_ref, g_ref, wq_hbm, wk_hbm, lw, gain,
    done,
    qs, wq, wk, keys_all, vals, score, peak, total, tgt, lc, weights, ls, qp, kp, ks, comb, mix, sd, raw, res, local,
    dstate, dquery, dkey, grads, pair, part, box, mine, far, sums_box, small_part, small_pair, small_sum,
    load, own_send, across_send, relay_send, twin_send, recv, sums_send, sums_recv, pair_send, pair_recv,
    part_send, part_recv, done_send, done_recv, small_sem, swap_sem,
):
    c = lax.axis_index("seq")
    y, z, k = c // 16, c // 2 % 8, c % 2
    own_pair = c // 2
    second = y == 1
    twin, across = at(y, z, 1 - k), at(1 - y, z, k)
    row_order = (1, 2, 3, 4, 5, 6, 7)
    me = lax.axis_index("head")
    head_peers = [(me + d) % HEADS for d in range(1, HEADS)]

    barrier = pltpu.get_barrier_semaphore()
    for target in [twin, across] + [at(y, (z + d) % 8, k) for d in range(1, 8)]:
        pl.semaphore_signal(barrier, inc=1, device_id={"seq": target}, device_id_type=MESH)
    for peer in head_peers:
        pl.semaphore_signal(barrier, inc=1, device_id={"head": peer}, device_id_type=MESH)

    loads = [
        pltpu.make_async_copy(q_hbm.at[:, rows(h)], qs.at[rows(h)], load.at[h])
        for h in range(HEADS)
    ]
    loads.append(pltpu.make_async_copy(wq_hbm, wq, load.at[8]))
    loads.append(pltpu.make_async_copy(wk_hbm, wk, load.at[9]))
    for copy in loads:
        copy.start()
    keys_all[c, :TOK] = k_ref[...]
    keys_all[c, TOK:] = gate_pieces(g_ref[...])
    vals[c] = v_ref[...]

    @pl.when(k == 0)
    def _():
        keys_all[c + 1] = jnp.zeros((KEY_ROWS, HD), BF)
        vals[c + 1] = jnp.zeros((TOK, HD), BF)

    for copy in loads:
        copy.wait()
    student_inside(qs, k_ref[...], g_ref[...], wq, wk, lw, qp, kp, mix, sd)
    pl.semaphore_wait(barrier, 16)

    def block(phase, slot):
        return keys_all.at[slot] if phase == 0 else vals.at[slot]

    def copy_of(phase, slot, sem, target):
        ref = block(phase, slot)
        return remote("seq", ref, ref, sem, recv.at[phase, slot], target)

    def to_twin(phase, slot):
        return copy_of(phase, slot, twin_send.at[phase, slot], twin)

    def to_across(phase, zs):
        return copy_of(phase, at(0, zs, k), across_send.at[phase, zs], across)

    def to_row(phase, d):
        return copy_of(phase, c, own_send.at[phase, d], at(y, (z + d) % 8, k))

    def relayed(phase, d):
        return copy_of(phase, at(0, z, k), relay_send.at[phase, d], at(y, (z + d) % 8, k))

    def act(when, copy, wait=False):
        @pl.when(when)
        def _():
            if wait:
                copy.wait_send()
            else:
                copy.start()

    row_first = (y == 0) & (k == 0)

    def own_moves(phase, wait=False):
        act(y == 0, to_across(phase, z), wait)
        act(k == 0, to_twin(phase, c), wait)
        for d in row_order:
            act((z + d < 8) | row_first, to_row(phase, d), wait)

    def arrived(phase, slot):
        to_twin(phase, slot).wait_recv()

    def relay(phase):
        @pl.when(second)
        def _():
            slot = at(0, z, k)
            arrived(phase, slot)
            for d in row_order:
                act(k == 1, relayed(phase, d))
            to_twin(phase, slot).start()

    def chip_of(i):
        d = jnp.where(i % 2 == 1, (i + 1) // 2, 8 - i // 2)
        return (z + 8 - d) % 8

    def forward(phase, i):
        zs = chip_of(i)

        @pl.when((zs < z) | row_first)
        def _():
            slot = at(y, zs, k)
            arrived(phase, slot)
            act(row_first, to_across(phase, zs))
            act(zs < z, to_twin(phase, slot))

        @pl.when(second)
        def _():
            slot = at(0, zs, k)
            arrived(phase, slot)
            to_twin(phase, slot).start()

    def pairs(phase, i, use):
        zs = jnp.where(i == 0, z, chip_of(i))

        def one(other, carry):
            @pl.when((other == 0) & (zs < z) | (other == 1) & second)
            def _():
                ys = y * (1 - other)
                arrived(phase, at(ys, zs, 1 - k))
                use(ys * 8 + zs)

            return carry

        lax.fori_loop(0, 2, one, 0)

    own_moves(0)

    @pl.when(k == 1)
    def _():
        arrived(0, c - 1)

    scored(c, own_pair, True, qs, keys_all, peak, score)
    relay(0)
    own_moves(1)
    relay(1)

    def key_step(i, carry):
        @pl.when(i < 8)
        def _():
            forward(0, i)

        pairs(0, i - 1, lambda p: scored(c, p, False, qs, keys_all, peak, score))
        return carry

    lax.fori_loop(1, 9, key_step, 0)
    for h in range(HEADS):
        peak[rows(h)] = jnp.broadcast_to(
            jnp.max(peak[rows(h)], axis=1, keepdims=True), (TOK, TOK)
        )
    total[...] = jnp.zeros_like(total)
    tgt[...] = jnp.zeros_like(tgt)
    ls[...] = jnp.zeros_like(ls)
    level_weights(c, keys_all, lc, weights)

    @pl.when(k == 1)
    def _():
        arrived(1, c - 1)
        keys = keys_all[c - 1, :TOK].astype(F32).T
        for h in range(HEADS):
            ls[0, h] = mm_right_exact(keys * weights[c - 1, h : h + 1], vals[c - 1], 1, 0)

    level = local_levels()
    for h in range(HEADS):
        weighed(own_pair, h, pair_of(vals, own_pair), score, peak, total, tgt)
        mask = jnp.full((TOK, TOK), lw[h, 0], F32)
        for j in range(1, LOW + 1):
            mask = jnp.where(level == j, lw[h, j], mask)
        local[h] = mm_right_exact(sd[h] * mask, v_ref[...], 1, 0)

    def use_values(p):
        values = pair_of(vals, p)
        keys = pair_of(keys_all, p).astype(F32).T
        weight = jnp.concatenate([weights[2 * p], weights[2 * p + 1]], axis=1)
        j = jnp.int32(0)
        for b in range(4):
            j = j + (own_pair // (1 << b) != p // (1 << b)).astype(jnp.int32)
        for h in range(HEADS):
            weighed(p, h, values, score, peak, total, tgt)
            ls[j, h] += mm_right_exact(keys * weight[h : h + 1], values, 1, 0)

    def value_step(i, carry):
        @pl.when(i < 8)
        def _():
            forward(1, i)

        pairs(1, i - 1, use_values)
        return carry

    lax.fori_loop(1, 9, value_step, 0)
    for h in range(HEADS):
        tgt[h] = tgt[h] / jnp.sum(total[rows(h)], axis=1, keepdims=True)
    entry = jnp.exp(column_cumulative(g_ref[...]))
    sums_box[me] = student_whole(entry, wk, lw, gain, ls, tgt, qp, ks, comb, raw, local)

    outgoing = [
        remote("head", sums_box.at[me], sums_box.at[me], sums_send.at[d], sums_recv.at[me], peer)
        for d, peer in enumerate(head_peers)
    ]
    for copy in outgoing:
        copy.start()
    for phase in range(2):
        own_moves(phase, True)

        for d in row_order:
            act(second & (k == 1), relayed(phase, d), True)
        act(second, to_twin(phase, at(0, z, k)), True)

        def sent(i, carry, phase=phase):
            zs = chip_of(i)
            act(row_first, to_across(phase, zs), True)
            act(zs < z, to_twin(phase, at(y, zs, k)), True)
            act(second, to_twin(phase, at(0, zs, k)), True)
            return carry

        lax.fori_loop(1, 8, sent, 0)
    for d, peer in enumerate(head_peers):
        remote(
            "head", sums_box.at[peer], sums_box.at[peer], sums_send.at[d], sums_recv.at[peer], peer
        ).wait_recv()
    all_sums = sums_box[0]
    for i in range(1, HEADS):
        all_sums = all_sums + sums_box[i]
    small_part[...] = backward_inside(
        all_sums, entry, v_ref[...], wk, gain, ls, tgt, qp, kp, ks, mix, sd, raw, res, dstate, dquery, dkey
    )

    small_twin = remote("seq", small_part, small_pair, small_sem.at[0], small_sem.at[1], twin)
    small_twin.start()
    order = [(z + d) % 8 for d in range(1, 9)]

    def twin_part(h):
        return remote("seq", grads.at[1 - k, h], pair.at[h], pair_send.at[h], pair_recv.at[h], twin)

    for h in order:
        q_rows = qs[pl.ds(pl.multiple_of(h * TOK, TOK), TOK)]
        grads[0, h] = mm_left_exact(q_rows, dquery[h], 0, 0)
        grads[1, h] = mm(comb[h], dstate[h], 1, 1) + mm_left_exact(k_ref[...], dkey[h], 0, 0)
        twin_part(h).start()
    small_twin.wait_recv()
    small_sum[...] = small_part[...] + small_pair[...]

    def piece_to(d, h):
        return remote("seq", part.at[h], box.at[z], part_send.at[d], part_recv.at[z], at(y, h, k))

    def piece_from(d, h):
        return remote("seq", part.at[h], box.at[h], part_send.at[d], part_recv.at[h], at(y, h, k))

    def own_piece(h):
        tile = pl.multiple_of(h % 3 * 8, 8)
        return jnp.concatenate([grads[k, h] + pair[h], small_sum[pl.ds(tile, 8)]], axis=0)

    for d, h in enumerate(order):
        twin_part(h).wait_recv()
        if d < 7:
            part[h] = own_piece(h)
            piece_to(d, h).start()
        else:
            box[h] = own_piece(h)
    for h in order:
        twin_part(h).wait_send()
    for d, h in enumerate(order[:7]):
        piece_from(d, h).wait_recv()
    whole = box[0]
    for i in range(1, 8):
        whole = whole + box[i]
    mine[...] = whole
    swap = remote("seq", mine, far, swap_sem.at[0], swap_sem.at[1], across)
    swap.start()
    for d, h in enumerate(order[:7]):
        piece_to(d, h).wait_send()
    swap.wait_recv()
    done[k, z] = mine[...] + far[...]

    def sum_to(d):
        ref = done.at[k, z]
        return remote("seq", ref, ref, done_send.at[0, d], done_recv.at[0, z], at(y, (z + d + 1) % 8, k))

    def sum_from(d, h):
        ref = done.at[k, h]
        return remote("seq", ref, ref, done_send.at[0, d], done_recv.at[0, h], at(y, h, k))

    def sum_twin(core, h):
        ref = done.at[core, h]
        return remote("seq", ref, ref, done_send.at[1, h], done_recv.at[1, h], twin)

    for d in range(7):
        sum_to(d).start()
    sum_twin(k, z).start()
    for d in (0, 6, 1, 5, 2, 4, 3):
        sum_from(d, order[d]).wait_recv()
        sum_twin(k, order[d]).start()
    for h in range(8):
        sum_twin(1 - k, h).wait_recv()
    for copy in outgoing + [small_twin, swap, sum_twin(k, z)]:
        copy.wait_send()
    for d, h in enumerate(order[:7]):
        sum_to(d).wait_send()
        sum_twin(k, h).wait_send()


def written_kernel(done, grad_query, grad_key, levels, gains):
    grad_query[...] = done[0, :, :HD]
    grad_key[...] = done[1, :, :HD]
    tile = jnp.concatenate(
        [done[0, t, HD:] for t in range(2)] + [jnp.zeros((TOK - 16, TOK), F32)], axis=0
    ).T
    levels[...] = tile[:HEADS, :LEVELS]
    gains[...] = done[0, 2, HD:]


VM = pl.BlockSpec(memory_space=pltpu.VMEM)
SM = pl.BlockSpec(memory_space=pltpu.SMEM)
ANY = pl.BlockSpec(memory_space=pl.ANY)
DMA = pltpu.SemaphoreType.DMA


def shaped(shape, dtype=F32):
    return jax.ShapeDtypeStruct(shape, dtype)


def on_device(queries, key_vectors, value_vectors, log_gate, query_map, key_map, lw, norm_gain):
    matrix = pltpu.VMEM((HEADS, TOK, HD), F32)
    small = pltpu.VMEM((SMALL, TOK), F32)
    done = pl.pallas_call(
        whole_kernel,
        out_shape=shaped((2, HEADS, PIECE, HD)),
        in_specs=[ANY, VM, VM, VM, ANY, ANY, SM, VM],
        out_specs=VM,
        scratch_shapes=[
            pltpu.VMEM((HEADS * TOK, HD), BF),
            matrix,
            matrix,
            pltpu.VMEM((SPANS, KEY_ROWS, HD), BF),
            pltpu.VMEM((SPANS, TOK, HD), BF),
            pltpu.VMEM((SPANS // 2, HEADS * TOK, 2 * TOK), F32),
            pltpu.VMEM((HEADS * TOK, TOK), F32),
            pltpu.VMEM((HEADS * TOK, TOK), F32),
            matrix,
            pltpu.VMEM((SPANS * GATE_ROWS, TOK), F32),
            pltpu.VMEM((SPANS, HEADS, TOK), F32),
            pltpu.VMEM((CROSS, HEADS, HD, HD), F32),
            *[matrix] * 12,
            pltpu.VMEM((2, HEADS, HD, HD), F32),
            matrix,
            pltpu.VMEM((HEADS, PIECE, HD), F32),
            pltpu.VMEM((8, PIECE, HD), F32),
            pltpu.VMEM((PIECE, HD), F32),
            pltpu.VMEM((PIECE, HD), F32),
            pltpu.VMEM((HEADS, 8, TOK), F32),
            small,
            small,
            small,
            DMA((10,)),
            DMA((2, 8)),
            DMA((2, 8)),
            DMA((2, 8)),
            DMA((2, SPANS)),
            DMA((2, SPANS)),
            DMA((7,)),
            DMA((HEADS,)),
            DMA((8,)),
            DMA((8,)),
            DMA((7,)),
            DMA((8,)),
            DMA((2, 8)),
            DMA((2, 8)),
            DMA((2,)),
            DMA((2,)),
        ],
        compiler_params=pltpu.CompilerParams(
            collective_id=0, has_side_effects=True, vmem_limit_bytes=LIMIT
        ),
        name="distill",
    )(
        queries, key_vectors, value_vectors, log_gate, query_map, key_map, lw,
        norm_gain.reshape(HEADS, HD),
    )
    grad_query, grad_key, levels, gains = pl.pallas_call(
        written_kernel,
        out_shape=(
            shaped((HEADS, HD, HD)),
            shaped((HEADS, HD, HD)),
            shaped((HEADS, LEVELS)),
            shaped((HEADS, HD)),
        ),
        in_specs=[VM],
        out_specs=(VM,) * 4,
        name="written",
    )(done)
    return grad_query, grad_key, levels, gains.reshape(-1)


def solution(mesh):
    return jax.shard_map(
        on_device,
        mesh=mesh,
        in_specs=(
            P("seq", "head"),
            P("seq", "head"),
            P("seq", "head"),
            P("head", "seq"),
            P("head", None, None),
            P("head", None, None),
            P("head", None),
            P("head"),
        ),
        out_specs=(P("head", None, None), P("head", None, None), P("head", None), P("head")),
        check_vma=False,
    )
```

```python
import jax
import jax.numpy as jnp
from jax import lax
from jax.experimental import pallas as pl
from jax.experimental.pallas import tpu as pltpu
from jax.sharding import PartitionSpec as P

F32 = jnp.float32
BF = jnp.bfloat16
HIGHEST = lax.Precision.HIGHEST
MESH = pl.DeviceIdType.MESH
NEGATIVE = -1e30
EPSILON = 1e-05
HD = 128
TOK = 128
HEADS = 8
SPANS = 32
LEVELS = 13
LOW = 7
CROSS = 5
TOKENS = TOK * SPANS
WIDTH = 64 * HD
SMALL = 24
GATE_ROWS = 32
KEY_ROWS = 128 + GATE_ROWS
PIECE = 128 + 8
LOG2E = 1.4426950408889634
SCALE = HD**-0.5 * LOG2E
LIMIT = 58 << 20


def pieces(a):
    high = a.astype(BF)
    return high, (a - high.astype(F32)).astype(BF)


def dg(a, b, ca, cb, precision=None):
    return lax.dot_general(
        a, b, (((ca,), (cb,)), ((), ())), preferred_element_type=F32, precision=precision
    )


def halves(o):
    n = o.shape[1] // 2
    return o[:, :n] + o[:, n:]


def mm(a, b, ca, cb):
    bh, bl = pieces(b)
    left = jnp.concatenate(pieces(a), axis=ca)
    right = jnp.concatenate(
        [jnp.concatenate([bh, bh], axis=cb), jnp.concatenate([bl, bl], axis=cb)], axis=1 - cb
    )
    return halves(dg(left, right, ca, cb))


def mm_left_exact(a, b, ca, cb):
    return halves(dg(a, jnp.concatenate(pieces(b), axis=1 - cb), ca, cb))


def mm_right_exact(a, b, ca, cb):
    return dg(jnp.concatenate(pieces(a), axis=ca), jnp.concatenate([b, b], axis=cb), ca, cb)


def iota(shape, dim):
    return lax.broadcasted_iota(jnp.int32, shape, dim)


def local_levels():
    x = jnp.bitwise_xor(iota((TOK, TOK), 0), iota((TOK, TOK), 1))
    level = jnp.zeros_like(x)
    for bit in range(LOW):
        level = level + (x >= 1 << bit).astype(jnp.int32)
    return level


def rows(h):
    return slice(h * TOK, (h + 1) * TOK)


def column_cumulative(gates):
    lower = (iota((TOK, TOK), 1) <= iota((TOK, TOK), 0)).astype(F32)
    return dg(lower, gates, 1, 1, HIGHEST)


def pair_of(ref, p):
    return jnp.concatenate([ref[2 * p, :TOK], ref[2 * p + 1, :TOK]], axis=0)


def scored(c, p, masked, qs, keys_all, peak, score):
    keys = pair_of(keys_all, p)
    for h in range(HEADS):
        s = dg(qs[rows(h)], keys, 1, 1)
        if masked:
            place_of = 2 * TOK * p + iota((TOK, 2 * TOK), 1)
            s = jnp.where(place_of <= c * TOK + iota((TOK, 2 * TOK), 0), s, NEGATIVE)
        score[p, rows(h)] = s
        top = jnp.maximum(s[:, :TOK], s[:, TOK:])
        peak[rows(h)] = top if masked else jnp.maximum(peak[rows(h)], top)


def weighed(p, h, values, score, peak, total, tgt):
    s = score[p, rows(h)]
    top = peak[rows(h)]
    w0 = jnp.exp2((s[:, :TOK] - top) * SCALE)
    w1 = jnp.exp2((s[:, TOK:] - top) * SCALE)
    total[rows(h)] += w0 + w1
    tgt[h] += dg(jnp.concatenate([w0.astype(BF), w1.astype(BF)], axis=1), values, 1, 0)


def level_weights(c, keys_all, lc, weights):
    upper = (iota((TOK, TOK), 0) <= iota((TOK, TOK), 1)).astype(BF)
    lc[...] = dg(keys_all[:, TOK:].reshape(SPANS * GATE_ROWS, TOK), upper, 1, 0)

    def step(i, since):
        x = c - 1 - i
        three = lc[pl.ds(pl.multiple_of(x * GATE_ROWS, GATE_ROWS), 3 * HEADS)]
        own = three[:HEADS] + three[HEADS : 2 * HEADS] + three[2 * HEADS :]
        since = since + own[:, TOK - 1 :]
        weights[x] = jnp.exp(since - own)
        return since

    lax.fori_loop(0, c, step, jnp.zeros((HEADS, 1), F32))


def gate_pieces(gate):
    high = gate.astype(BF).astype(F32)
    middle = (gate - high).astype(BF).astype(F32)
    low = gate - high - middle
    return jnp.concatenate([high, middle, low, jnp.zeros_like(gate)], axis=0).astype(BF)


def student_inside(qs, key, gate, wq, wk, lw, qp, kp, mix, sd):
    upper = (iota((TOK, TOK), 0) <= iota((TOK, TOK), 1)).astype(F32)
    row_cum = dg(gate, upper, 1, 0, HIGHEST)
    col_cum = column_cumulative(gate)
    causal = iota((TOK, TOK), 1) <= iota((TOK, TOK), 0)
    level = local_levels()
    for h in range(HEADS):
        qp[h] = mm_left_exact(qs[rows(h)], wq[h], 1, 0)
        kp[h] = mm_left_exact(key, wk[h], 1, 0)
    for h in range(HEADS):
        decay = jnp.exp(
            jnp.where(causal, col_cum[:, h : h + 1] - row_cum[h : h + 1], NEGATIVE)
        )
        mask = jnp.full((TOK, TOK), lw[h, 0], F32)
        for j in range(1, LOW + 1):
            mask = jnp.where(level == j, lw[h, j], mask)
        sd[h] = mm(qp[h], kp[h], 1, 1) * decay
        mix[h] = decay * mask


def student_whole(entry, wk, lw, gain, ls, tgt, qp, ks, comb, raw, local):
    for h in range(HEADS):
        combined = lw[h, LOW + 1] * ls[0, h]
        for j in range(1, CROSS):
            combined = combined + lw[h, LOW + 1 + j] * ls[j, h]
        comb[h] = combined
        ks[h] = mm(wk[h], combined, 0, 0)
    square = jnp.zeros((TOK, HD), F32)
    scaled = jnp.zeros((TOK, HD), F32)
    against = jnp.zeros((TOK, HD), F32)
    for h in range(HEADS):
        r = local[h] + entry[:, h : h + 1] * mm(qp[h], ks[h], 1, 0)
        raw[h] = r
        rg = r * gain[h : h + 1]
        square = square + r * r
        scaled = scaled + rg * rg
        against = against + tgt[h] * rg
    one = jnp.ones((8, HD), F32)
    tile = [dg(one, x, 1, 1, HIGHEST) for x in (square, scaled, against)]
    return jnp.concatenate([t[:1] for t in tile] + [tile[0][:5]], axis=0)


def backward_inside(
    all_sums, entry, value, wk, gain, ls, tgt, qp, kp, ks, mix, sd, raw, res, dstate, dquery, dkey
):
    eye = (iota((TOK, TOK), 0) == iota((TOK, TOK), 1)).astype(F32)
    level = local_levels()
    column = dg(eye, all_sums, 1, 1, HIGHEST)
    inverse = lax.rsqrt(column[:, 0:1] / WIDTH + EPSILON)
    inner = (inverse * column[:, 1:2] - column[:, 2:3]) / TOKENS
    back = inverse * inverse * inverse * inner / WIDTH
    gain_rows = []
    for h in range(HEADS):
        g = gain[h : h + 1]
        normed = raw[h] * inverse
        mismatch = (normed * g - tgt[h]) * (1.0 / TOKENS)
        gain_rows.append(jnp.sum(mismatch * normed, axis=0, keepdims=True))
        res[h] = inverse * (mismatch * g) - raw[h] * back
    lane = iota((16, TOK), 1)
    level_tile = jnp.zeros((16, TOK), F32)
    for h in range(HEADS):
        e = entry[:, h : h + 1]
        d_mix = mm_right_exact(res[h], value, 1, 1)
        d_scores = d_mix * mix[h]
        through = d_mix * sd[h]
        dstate[h] = mm(e * qp[h], res[h], 0, 0)
        d_comb = mm(wk[h], dstate[h], 1, 0)
        dquery[h] = mm(d_scores, kp[h], 1, 0) + e * mm(res[h], ks[h], 1, 1)
        dkey[h] = mm(d_scores, qp[h], 0, 0)
        lines = [
            jnp.sum(jnp.where(level == j, through, 0.0), axis=0, keepdims=True)
            for j in range(LOW + 1)
        ]
        lines += [jnp.sum(ls[j, h] * d_comb, axis=0, keepdims=True) for j in range(CROSS)]
        lines.append(jnp.zeros((16 - LEVELS, TOK), F32))
        summed = jnp.sum(jnp.concatenate(lines, axis=0), axis=1, keepdims=True)
        level_tile = jnp.where(lane == h, summed, level_tile)
    return jnp.concatenate([level_tile] + gain_rows, axis=0)


def at(y, z, k):
    return y * 16 + z * 2 + k


def remote(axis, src, dst, send, recv, target):
    return pltpu.make_async_remote_copy(
        src_ref=src, dst_ref=dst, send_sem=send, recv_sem=recv,
        device_id={axis: target}, device_id_type=MESH,
    )


def whole_kernel(
    q_hbm, k_ref, v_ref, g_ref, wq_hbm, wk_hbm, lw, gain,
    done,
    qs, wq, wk, keys_all, vals, score, peak, total, tgt, lc, weights, ls, qp, kp, ks, comb, mix, sd, raw, res, local,
    dstate, dquery, dkey, grads, pair, part, box, mine, far, sums_box, small_part, small_pair, small_sum,
    load, own_send, across_send, relay_send, twin_send, recv, sums_send, sums_recv, pair_send, pair_recv,
    part_send, part_recv, done_send, done_recv, both_send, both_recv, small_sem, swap_send, swap_recv,
):
    c = lax.axis_index("seq")
    y, z, k = c // 16, c // 2 % 8, c % 2
    own_pair = c // 2
    second = y == 1
    twin, across = at(y, z, 1 - k), at(1 - y, z, k)
    row_order = (1, 2, 3, 4, 5, 6, 7)
    me = lax.axis_index("head")
    head_peers = [(me + d) % HEADS for d in range(1, HEADS)]

    barrier = pltpu.get_barrier_semaphore()
    for target in [twin, across] + [at(y, (z + d) % 8, k) for d in range(1, 8)]:
        pl.semaphore_signal(barrier, inc=1, device_id={"seq": target}, device_id_type=MESH)
    for peer in head_peers:
        pl.semaphore_signal(barrier, inc=1, device_id={"head": peer}, device_id_type=MESH)

    loads = [
        pltpu.make_async_copy(q_hbm.at[:, rows(h)], qs.at[rows(h)], load.at[h])
        for h in range(HEADS)
    ]
    loads.append(pltpu.make_async_copy(wq_hbm, wq, load.at[8]))
    loads.append(pltpu.make_async_copy(wk_hbm, wk, load.at[9]))
    for copy in loads:
        copy.start()
    keys_all[c, :TOK] = k_ref[...]
    keys_all[c, TOK:] = gate_pieces(g_ref[...])
    vals[c] = v_ref[...]

    @pl.when(k == 0)
    def _():
        keys_all[c + 1] = jnp.zeros((KEY_ROWS, HD), BF)
        vals[c + 1] = jnp.zeros((TOK, HD), BF)

    for copy in loads:
        copy.wait()
    student_inside(qs, k_ref[...], g_ref[...], wq, wk, lw, qp, kp, mix, sd)
    pl.semaphore_wait(barrier, 16)

    def block(phase, slot):
        return keys_all.at[slot] if phase == 0 else vals.at[slot]

    def copy_of(phase, slot, sem, target):
        ref = block(phase, slot)
        return remote("seq", ref, ref, sem, recv.at[phase, slot], target)

    def to_twin(phase, slot):
        return copy_of(phase, slot, twin_send.at[phase, slot], twin)

    def to_across(phase, zs):
        return copy_of(phase, at(0, zs, k), across_send.at[phase, zs], across)

    def to_row(phase, d):
        return copy_of(phase, c, own_send.at[phase, d], at(y, (z + d) % 8, k))

    def relayed(phase, d):
        return copy_of(phase, at(0, z, k), relay_send.at[phase, d], at(y, (z + d) % 8, k))

    def act(when, copy, wait=False):
        @pl.when(when)
        def _():
            if wait:
                copy.wait_send()
            else:
                copy.start()

    row_first = (y == 0) & (k == 0)

    def own_moves(phase, wait=False):
        act(y == 0, to_across(phase, z), wait)
        act(k == 0, to_twin(phase, c), wait)
        for d in row_order:
            act((z + d < 8) | row_first, to_row(phase, d), wait)

    def arrived(phase, slot):
        to_twin(phase, slot).wait_recv()

    def relay(phase):
        @pl.when(second)
        def _():
            slot = at(0, z, k)
            arrived(phase, slot)
            for d in row_order:
                act(k == 1, relayed(phase, d))
            to_twin(phase, slot).start()

    def chip_of(i):
        d = jnp.where(i % 2 == 1, (i + 1) // 2, 8 - i // 2)
        return (z + 8 - d) % 8

    def forward(phase, i):
        zs = chip_of(i)

        @pl.when((zs < z) | row_first)
        def _():
            slot = at(y, zs, k)
            arrived(phase, slot)
            act(row_first, to_across(phase, zs))
            act(zs < z, to_twin(phase, slot))

        @pl.when(second)
        def _():
            slot = at(0, zs, k)
            arrived(phase, slot)
            to_twin(phase, slot).start()

    def pairs(phase, i, use):
        zs = jnp.where(i == 0, z, chip_of(i))

        def one(other, carry):
            @pl.when((other == 0) & (zs < z) | (other == 1) & second)
            def _():
                ys = y * (1 - other)
                arrived(phase, at(ys, zs, 1 - k))
                use(ys * 8 + zs)

            return carry

        lax.fori_loop(0, 2, one, 0)

    own_moves(0)

    @pl.when(k == 1)
    def _():
        arrived(0, c - 1)

    scored(c, own_pair, True, qs, keys_all, peak, score)
    relay(0)
    own_moves(1)
    relay(1)

    def key_step(i, carry):
        @pl.when(i < 8)
        def _():
            forward(0, i)

        pairs(0, i - 1, lambda p: scored(c, p, False, qs, keys_all, peak, score))
        return carry

    lax.fori_loop(1, 9, key_step, 0)
    for h in range(HEADS):
        peak[rows(h)] = jnp.broadcast_to(
            jnp.max(peak[rows(h)], axis=1, keepdims=True), (TOK, TOK)
        )
    total[...] = jnp.zeros_like(total)
    tgt[...] = jnp.zeros_like(tgt)
    ls[...] = jnp.zeros_like(ls)
    level_weights(c, keys_all, lc, weights)

    @pl.when(k == 1)
    def _():
        arrived(1, c - 1)
        keys = keys_all[c - 1, :TOK].astype(F32).T
        for h in range(HEADS):
            ls[0, h] = mm_right_exact(keys * weights[c - 1, h : h + 1], vals[c - 1], 1, 0)

    level = local_levels()
    for h in range(HEADS):
        weighed(own_pair, h, pair_of(vals, own_pair), score, peak, total, tgt)
        mask = jnp.full((TOK, TOK), lw[h, 0], F32)
        for j in range(1, LOW + 1):
            mask = jnp.where(level == j, lw[h, j], mask)
        local[h] = mm_right_exact(sd[h] * mask, v_ref[...], 1, 0)

    def use_values(p):
        values = pair_of(vals, p)
        keys = pair_of(keys_all, p).astype(F32).T
        weight = jnp.concatenate([weights[2 * p], weights[2 * p + 1]], axis=1)
        j = jnp.int32(0)
        for b in range(4):
            j = j + (own_pair // (1 << b) != p // (1 << b)).astype(jnp.int32)
        for h in range(HEADS):
            weighed(p, h, values, score, peak, total, tgt)
            ls[j, h] += mm_right_exact(keys * weight[h : h + 1], values, 1, 0)

    def value_step(i, carry):
        @pl.when(i < 8)
        def _():
            forward(1, i)

        pairs(1, i - 1, use_values)
        return carry

    lax.fori_loop(1, 9, value_step, 0)
    for h in range(HEADS):
        tgt[h] = tgt[h] / jnp.sum(total[rows(h)], axis=1, keepdims=True)
    entry = jnp.exp(column_cumulative(g_ref[...]))
    sums_box[me] = student_whole(entry, wk, lw, gain, ls, tgt, qp, ks, comb, raw, local)

    outgoing = [
        remote("head", sums_box.at[me], sums_box.at[me], sums_send.at[d], sums_recv.at[me], peer)
        for d, peer in enumerate(head_peers)
    ]
    for copy in outgoing:
        copy.start()
    for phase in range(2):
        own_moves(phase, True)

        for d in row_order:
            act(second & (k == 1), relayed(phase, d), True)
        act(second, to_twin(phase, at(0, z, k)), True)

        def sent(i, carry, phase=phase):
            zs = chip_of(i)
            act(row_first, to_across(phase, zs), True)
            act(zs < z, to_twin(phase, at(y, zs, k)), True)
            act(second, to_twin(phase, at(0, zs, k)), True)
            return carry

        lax.fori_loop(1, 8, sent, 0)
    for d, peer in enumerate(head_peers):
        remote(
            "head", sums_box.at[peer], sums_box.at[peer], sums_send.at[d], sums_recv.at[peer], peer
        ).wait_recv()
    all_sums = sums_box[0]
    for i in range(1, HEADS):
        all_sums = all_sums + sums_box[i]
    small_part[...] = backward_inside(
        all_sums, entry, v_ref[...], wk, gain, ls, tgt, qp, kp, ks, mix, sd, raw, res, dstate, dquery, dkey
    )

    small_twin = remote("seq", small_part, small_pair, small_sem.at[0], small_sem.at[1], twin)
    small_twin.start()
    order = [(z + d) % 8 for d in (4, 3, 5, 1, 7, 2, 6, 0)]

    def twin_part(h):
        return remote("seq", grads.at[1 - k, h], pair.at[h], pair_send.at[h], pair_recv.at[h], twin)

    for h in order:
        q_rows = qs[pl.ds(pl.multiple_of(h * TOK, TOK), TOK)]
        grads[0, h] = mm_left_exact(q_rows, dquery[h], 0, 0)
        grads[1, h] = mm(comb[h], dstate[h], 1, 1) + mm_left_exact(k_ref[...], dkey[h], 0, 0)
        twin_part(h).start()
    small_twin.wait_recv()
    small_sum[...] = small_part[...] + small_pair[...]

    def lines(a):
        return pl.ds(0, 64) if a == 0 else pl.ds(64, PIECE - 64)

    def chip(d):
        return (z + 8 + d) % 8

    def piece(n, a):
        lean = 1 - 2 * a
        chunk, target = ((-4, -2), (-3, -1), (3, 1), (-1, -1), (1, 1), (-2, -2), (2, 2))[n]
        return remote(
            "seq", part.at[chip(lean * chunk), lines(a)], box.at[n, lines(a)], part_send.at[a, n],
            part_recv.at[a, n], at(y, chip(lean * target), k),
        )

    def ready(h):
        twin_part(h).wait_recv()
        tile = pl.multiple_of(h % 3 * 8, 8)
        part[h, :HD] = grads[k, h] + pair[h]
        part[h, HD:] = small_sum[pl.ds(tile, 8)]

    ready(order[0])
    for a in range(2):
        piece(0, a).start()
    ready(order[1])
    ready(order[2])
    for a in range(2):
        piece(1, a).start()
        piece(2, a).start()
    ready(order[3])
    ready(order[4])
    for a in range(2):
        piece(3, a).start()
        piece(4, a).start()
    for h in order[5:]:
        ready(h)
    for h in order:
        twin_part(h).wait_send()
    for a in range(2):
        lean = 1 - 2 * a
        piece(0, a).wait_recv()
        piece(1, a).wait_recv()
        part[chip(-2 * lean), lines(a)] += box[0, lines(a)] + box[1, lines(a)]
        piece(5, a).start()
        piece(2, a).wait_recv()
        part[chip(2 * lean), lines(a)] += box[2, lines(a)]
        piece(6, a).start()

    def swap(a):
        return remote(
            "seq", mine.at[lines(a)], far.at[lines(a)], swap_send.at[a], swap_recv.at[a], across
        )

    for a in range(2):
        whole = part[z, lines(a)]
        for n in range(3, 7):
            piece(n, a).wait_recv()
            whole = whole + box[n, lines(a)]
        mine[lines(a)] = whole
        swap(a).start()
    for a in range(2):
        for n in range(7):
            piece(n, a).wait_send()

    def spread(n, a):
        lean = 1 - 2 * a
        source, target = ((0, 2), (0, -2), (0, 1), (0, -1), (-2, 1), (-2, 2), (2, -1))[n]
        h = chip(lean * source)
        ref = done.at[k, h, lines(a)]
        return remote(
            "seq", ref, ref, done_send.at[a, n], done_recv.at[h, a], at(y, chip(lean * target), k)
        )

    def came(d, a):
        h = chip(d)
        ref = done.at[k, h, lines(a)]
        return remote("seq", ref, ref, done_send.at[a, 0], done_recv.at[h, a], twin)

    def sum_twin(core, h):
        ref = done.at[core, h]
        return remote("seq", ref, ref, both_send.at[h], both_recv.at[h], twin)

    for a in range(2):
        swap(a).wait_recv()
        done[k, z, lines(a)] = mine[lines(a)] + far[lines(a)]
        for n in range(4):
            spread(n, a).start()
    sum_twin(k, z).start()
    for a in range(2):
        lean = 1 - 2 * a
        came(-2 * lean, a).wait_recv()
        spread(4, a).start()
        spread(5, a).start()
        came(2 * lean, a).wait_recv()
        spread(6, a).start()
    for d in (2, -2):
        sum_twin(k, chip(d)).start()
    for d in (1, -1, 3, -3, 4):
        for a in range(2):
            came(d, a).wait_recv()
        sum_twin(k, chip(d)).start()
    for copy in outgoing + [small_twin]:
        copy.wait_send()
    for a in range(2):
        swap(a).wait_send()
        for n in range(7):
            spread(n, a).wait_send()
    for h in range(8):
        sum_twin(1 - k, h).wait_recv()
    for h in order:
        sum_twin(k, h).wait_send()


def written_kernel(done, grad_query, grad_key, levels, gains):
    grad_query[...] = done[0, :, :HD]
    grad_key[...] = done[1, :, :HD]
    tile = jnp.concatenate(
        [done[0, t, HD:] for t in range(2)] + [jnp.zeros((TOK - 16, TOK), F32)], axis=0
    ).T
    levels[...] = tile[:HEADS, :LEVELS]
    gains[...] = done[0, 2, HD:]


VM = pl.BlockSpec(memory_space=pltpu.VMEM)
SM = pl.BlockSpec(memory_space=pltpu.SMEM)
ANY = pl.BlockSpec(memory_space=pl.ANY)
DMA = pltpu.SemaphoreType.DMA


def shaped(shape, dtype=F32):
    return jax.ShapeDtypeStruct(shape, dtype)


def on_device(queries, key_vectors, value_vectors, log_gate, query_map, key_map, lw, norm_gain):
    matrix = pltpu.VMEM((HEADS, TOK, HD), F32)
    small = pltpu.VMEM((SMALL, TOK), F32)
    done = pl.pallas_call(
        whole_kernel,
        out_shape=shaped((2, HEADS, PIECE, HD)),
        in_specs=[ANY, VM, VM, VM, ANY, ANY, SM, VM],
        out_specs=VM,
        scratch_shapes=[
            pltpu.VMEM((HEADS * TOK, HD), BF),
            matrix,
            matrix,
            pltpu.VMEM((SPANS, KEY_ROWS, HD), BF),
            pltpu.VMEM((SPANS, TOK, HD), BF),
            pltpu.VMEM((SPANS // 2, HEADS * TOK, 2 * TOK), F32),
            pltpu.VMEM((HEADS * TOK, TOK), F32),
            pltpu.VMEM((HEADS * TOK, TOK), F32),
            matrix,
            pltpu.VMEM((SPANS * GATE_ROWS, TOK), F32),
            pltpu.VMEM((SPANS, HEADS, TOK), F32),
            pltpu.VMEM((CROSS, HEADS, HD, HD), F32),
            *[matrix] * 12,
            pltpu.VMEM((2, HEADS, HD, HD), F32),
            matrix,
            pltpu.VMEM((HEADS, PIECE, HD), F32),
            pltpu.VMEM((7, PIECE, HD), F32),
            pltpu.VMEM((PIECE, HD), F32),
            pltpu.VMEM((PIECE, HD), F32),
            pltpu.VMEM((HEADS, 8, TOK), F32),
            small,
            small,
            small,
            DMA((10,)),
            DMA((2, 8)),
            DMA((2, 8)),
            DMA((2, 8)),
            DMA((2, SPANS)),
            DMA((2, SPANS)),
            DMA((7,)),
            DMA((HEADS,)),
            DMA((8,)),
            DMA((8,)),
            DMA((2, 7)),
            DMA((2, 7)),
            DMA((2, 7)),
            DMA((8, 2)),
            DMA((8,)),
            DMA((8,)),
            DMA((2,)),
            DMA((2,)),
            DMA((2,)),
        ],
        compiler_params=pltpu.CompilerParams(
            collective_id=0, has_side_effects=True, vmem_limit_bytes=LIMIT
        ),
        name="distill",
    )(
        queries, key_vectors, value_vectors, log_gate, query_map, key_map, lw,
        norm_gain.reshape(HEADS, HD),
    )
    grad_query, grad_key, levels, gains = pl.pallas_call(
        written_kernel,
        out_shape=(
            shaped((HEADS, HD, HD)),
            shaped((HEADS, HD, HD)),
            shaped((HEADS, LEVELS)),
            shaped((HEADS, HD)),
        ),
        in_specs=[VM],
        out_specs=(VM,) * 4,
        name="written",
    )(done)
    return grad_query, grad_key, levels, gains.reshape(-1)


def solution(mesh):
    return jax.shard_map(
        on_device,
        mesh=mesh,
        in_specs=(
            P("seq", "head"),
            P("seq", "head"),
            P("seq", "head"),
            P("head", "seq"),
            P("head", None, None),
            P("head", None, None),
            P("head", None),
            P("head"),
        ),
        out_specs=(P("head", None, None), P("head", None, None), P("head", None), P("head")),
        check_vma=False,
    )
```

```python
import jax
import jax.numpy as jnp
from jax import lax
from jax.experimental import pallas as pl
from jax.experimental.pallas import tpu as pltpu
from jax.sharding import PartitionSpec as P

F32 = jnp.float32
BF = jnp.bfloat16
HIGHEST = lax.Precision.HIGHEST
MESH = pl.DeviceIdType.MESH
NEGATIVE = -1e30
EPSILON = 1e-05
HD = 128
TOK = 128
HEADS = 8
SPANS = 32
LEVELS = 13
LOW = 7
CROSS = 5
TOKENS = TOK * SPANS
WIDTH = 64 * HD
SMALL = 24
GATE_ROWS = 32
KEY_ROWS = 128 + GATE_ROWS
PIECE = 128 + 8
LOG2E = 1.4426950408889634
SCALE = HD**-0.5 * LOG2E
LIMIT = 58 << 20


def pieces(a):
    high = a.astype(BF)
    return high, (a - high.astype(F32)).astype(BF)


def dg(a, b, ca, cb, precision=None):
    return lax.dot_general(
        a, b, (((ca,), (cb,)), ((), ())), preferred_element_type=F32, precision=precision
    )


def halves(o):
    n = o.shape[1] // 2
    return o[:, :n] + o[:, n:]


def mm(a, b, ca, cb):
    bh, bl = pieces(b)
    left = jnp.concatenate(pieces(a), axis=ca)
    right = jnp.concatenate(
        [jnp.concatenate([bh, bh], axis=cb), jnp.concatenate([bl, bl], axis=cb)], axis=1 - cb
    )
    return halves(dg(left, right, ca, cb))


def mm_left_exact(a, b, ca, cb):
    return halves(dg(a, jnp.concatenate(pieces(b), axis=1 - cb), ca, cb))


def mm_right_exact(a, b, ca, cb):
    return dg(jnp.concatenate(pieces(a), axis=ca), jnp.concatenate([b, b], axis=cb), ca, cb)


def iota(shape, dim):
    return lax.broadcasted_iota(jnp.int32, shape, dim)


def local_levels():
    x = jnp.bitwise_xor(iota((TOK, TOK), 0), iota((TOK, TOK), 1))
    level = jnp.zeros_like(x)
    for bit in range(LOW):
        level = level + (x >= 1 << bit).astype(jnp.int32)
    return level


def rows(h):
    return slice(h * TOK, (h + 1) * TOK)


def column_cumulative(gates):
    lower = (iota((TOK, TOK), 1) <= iota((TOK, TOK), 0)).astype(F32)
    return dg(lower, gates, 1, 1, HIGHEST)


def pair_of(ref, p):
    return jnp.concatenate([ref[2 * p, :TOK], ref[2 * p + 1, :TOK]], axis=0)


def scored(c, p, masked, qs, keys_all, peak, score):
    keys = pair_of(keys_all, p)
    for h in range(HEADS):
        s = dg(qs[rows(h)], keys, 1, 1)
        if masked:
            place_of = 2 * TOK * p + iota((TOK, 2 * TOK), 1)
            s = jnp.where(place_of <= c * TOK + iota((TOK, 2 * TOK), 0), s, NEGATIVE)
        score[p, rows(h)] = s
        top = jnp.maximum(s[:, :TOK], s[:, TOK:])
        peak[rows(h)] = top if masked else jnp.maximum(peak[rows(h)], top)


def weighed(p, h, values, score, peak, total, tgt):
    s = score[p, rows(h)]
    top = peak[rows(h)]
    w0 = jnp.exp2((s[:, :TOK] - top) * SCALE)
    w1 = jnp.exp2((s[:, TOK:] - top) * SCALE)
    total[rows(h)] += w0 + w1
    tgt[h] += dg(jnp.concatenate([w0.astype(BF), w1.astype(BF)], axis=1), values, 1, 0)


def level_weights(c, keys_all, lc, weights):
    upper = (iota((TOK, TOK), 0) <= iota((TOK, TOK), 1)).astype(BF)
    lc[...] = dg(keys_all[:, TOK:].reshape(SPANS * GATE_ROWS, TOK), upper, 1, 0)

    def step(i, since):
        x = c - 1 - i
        three = lc[pl.ds(pl.multiple_of(x * GATE_ROWS, GATE_ROWS), 3 * HEADS)]
        own = three[:HEADS] + three[HEADS : 2 * HEADS] + three[2 * HEADS :]
        since = since + own[:, TOK - 1 :]
        weights[x] = jnp.exp(since - own)
        return since

    lax.fori_loop(0, c, step, jnp.zeros((HEADS, 1), F32))


def gate_pieces(gate):
    high = gate.astype(BF).astype(F32)
    middle = (gate - high).astype(BF).astype(F32)
    low = gate - high - middle
    return jnp.concatenate([high, middle, low, jnp.zeros_like(gate)], axis=0).astype(BF)


def student_inside(qs, key, gate, wq, wk, lw, qp, kp, mix, sd):
    upper = (iota((TOK, TOK), 0) <= iota((TOK, TOK), 1)).astype(F32)
    row_cum = dg(gate, upper, 1, 0, HIGHEST)
    col_cum = column_cumulative(gate)
    causal = iota((TOK, TOK), 1) <= iota((TOK, TOK), 0)
    level = local_levels()
    for h in range(HEADS):
        qp[h] = mm_left_exact(qs[rows(h)], wq[h], 1, 0)
        kp[h] = mm_left_exact(key, wk[h], 1, 0)
    for h in range(HEADS):
        decay = jnp.exp(
            jnp.where(causal, col_cum[:, h : h + 1] - row_cum[h : h + 1], NEGATIVE)
        )
        mask = jnp.full((TOK, TOK), lw[h, 0], F32)
        for j in range(1, LOW + 1):
            mask = jnp.where(level == j, lw[h, j], mask)
        sd[h] = mm(qp[h], kp[h], 1, 1) * decay
        mix[h] = decay * mask


def student_whole(entry, wk, lw, gain, ls, tgt, qp, ks, comb, raw, local):
    for h in range(HEADS):
        combined = lw[h, LOW + 1] * ls[0, h]
        for j in range(1, CROSS):
            combined = combined + lw[h, LOW + 1 + j] * ls[j, h]
        comb[h] = combined
        ks[h] = mm(wk[h], combined, 0, 0)
    square = jnp.zeros((TOK, HD), F32)
    scaled = jnp.zeros((TOK, HD), F32)
    against = jnp.zeros((TOK, HD), F32)
    for h in range(HEADS):
        r = local[h] + entry[:, h : h + 1] * mm(qp[h], ks[h], 1, 0)
        raw[h] = r
        rg = r * gain[h : h + 1]
        square = square + r * r
        scaled = scaled + rg * rg
        against = against + tgt[h] * rg
    one = jnp.ones((8, HD), F32)
    tile = [dg(one, x, 1, 1, HIGHEST) for x in (square, scaled, against)]
    return jnp.concatenate([t[:1] for t in tile] + [tile[0][:5]], axis=0)


def backward_inside(
    all_sums, entry, value, wk, gain, ls, tgt, qp, kp, ks, mix, sd, raw, res, dstate, dquery, dkey
):
    eye = (iota((TOK, TOK), 0) == iota((TOK, TOK), 1)).astype(F32)
    level = local_levels()
    column = dg(eye, all_sums, 1, 1, HIGHEST)
    inverse = lax.rsqrt(column[:, 0:1] / WIDTH + EPSILON)
    inner = (inverse * column[:, 1:2] - column[:, 2:3]) / TOKENS
    back = inverse * inverse * inverse * inner / WIDTH
    gain_rows = []
    for h in range(HEADS):
        g = gain[h : h + 1]
        normed = raw[h] * inverse
        mismatch = (normed * g - tgt[h]) * (1.0 / TOKENS)
        gain_rows.append(jnp.sum(mismatch * normed, axis=0, keepdims=True))
        res[h] = inverse * (mismatch * g) - raw[h] * back
    lane = iota((16, TOK), 1)
    level_tile = jnp.zeros((16, TOK), F32)
    for h in range(HEADS):
        e = entry[:, h : h + 1]
        d_mix = mm_right_exact(res[h], value, 1, 1)
        d_scores = d_mix * mix[h]
        through = d_mix * sd[h]
        dstate[h] = mm(e * qp[h], res[h], 0, 0)
        d_comb = mm(wk[h], dstate[h], 1, 0)
        dquery[h] = mm(d_scores, kp[h], 1, 0) + e * mm(res[h], ks[h], 1, 1)
        dkey[h] = mm(d_scores, qp[h], 0, 0)
        lines = [
            jnp.sum(jnp.where(level == j, through, 0.0), axis=0, keepdims=True)
            for j in range(LOW + 1)
        ]
        lines += [jnp.sum(ls[j, h] * d_comb, axis=0, keepdims=True) for j in range(CROSS)]
        lines.append(jnp.zeros((16 - LEVELS, TOK), F32))
        summed = jnp.sum(jnp.concatenate(lines, axis=0), axis=1, keepdims=True)
        level_tile = jnp.where(lane == h, summed, level_tile)
    return jnp.concatenate([level_tile] + gain_rows, axis=0)


def at(y, z, k):
    return y * 16 + z * 2 + k


def remote(axis, src, dst, send, recv, target):
    return pltpu.make_async_remote_copy(
        src_ref=src, dst_ref=dst, send_sem=send, recv_sem=recv,
        device_id={axis: target}, device_id_type=MESH,
    )


def whole_kernel(
    q_hbm, k_ref, v_ref, g_ref, wq_hbm, wk_hbm, lw, gain,
    done,
    qs, wq, wk, keys_all, vals, scores, peak, total, tgt, lc, weights, ls, qp, kp, ks, comb, mix, sd, raw, res, local,
    dstate, dquery, dkey, grads, pair, part, box, mine, far, sums_box, small_part, small_pair, small_sum,
    load, own_send, across_send, relay_send, onward_send, twin_send, recv, sums_send, sums_recv, pair_send, pair_recv,
    part_send, part_recv, done_send, done_recv, both_send, both_recv, small_sem, swap_send, swap_recv,
):
    c = lax.axis_index("seq")
    y, z, k = c // 16, c // 2 % 8, c % 2
    own_pair = c // 2
    second = y == 1
    twin, across = at(y, z, 1 - k), at(1 - y, z, k)
    me = lax.axis_index("head")
    head_peers = [(me + d) % HEADS for d in range(1, HEADS)]

    barrier = pltpu.get_barrier_semaphore()
    for target in [twin, across] + [at(y, (z + d) % 8, k) for d in (1, 2, 6, 7)]:
        pl.semaphore_signal(barrier, inc=1, device_id={"seq": target}, device_id_type=MESH)
    for peer in head_peers:
        pl.semaphore_signal(barrier, inc=1, device_id={"head": peer}, device_id_type=MESH)

    loads = [
        pltpu.make_async_copy(q_hbm.at[:, rows(h)], qs.at[rows(h)], load.at[h])
        for h in range(HEADS)
    ]
    loads.append(pltpu.make_async_copy(wq_hbm, wq, load.at[8]))
    loads.append(pltpu.make_async_copy(wk_hbm, wk, load.at[9]))
    for copy in loads:
        copy.start()
    keys_all[c, :TOK] = k_ref[...]
    keys_all[c, TOK:] = gate_pieces(g_ref[...])
    vals[c] = v_ref[...]

    @pl.when(k == 0)
    def _():
        keys_all[c + 1] = jnp.zeros((KEY_ROWS, HD), BF)
        vals[c + 1] = jnp.zeros((TOK, HD), BF)

    for copy in loads:
        copy.wait()
    student_inside(qs, k_ref[...], g_ref[...], wq, wk, lw, qp, kp, mix, sd)
    pl.semaphore_wait(barrier, 13)

    def block(phase, slot):
        return keys_all.at[slot] if phase == 0 else vals.at[slot]

    def copy_of(phase, slot, sem, target):
        ref = block(phase, slot)
        return remote("seq", ref, ref, sem, recv.at[phase, slot], target)

    def to_twin(phase, slot):
        return copy_of(phase, slot, twin_send.at[phase, slot], twin)

    def to_across(phase, zs):
        return copy_of(phase, at(0, zs, k), across_send.at[phase, zs], across)

    lean_core = 1 - 2 * k
    direct = (2, -2, 1, -1)

    def chip_at(o):
        return (z + 8 + lean_core * o) % 8

    def source_at(o):
        return (z + 8 - lean_core * o) % 8

    def need(zs, o):
        return (zs + 8 + lean_core * o) % 8 > zs

    def wanted(zs, o):
        if o == 2:
            return need(zs, 2) | need(zs, 3) | need(zs, 4)
        return need(zs, -2) | need(zs, -3) if o == -2 else need(zs, o)

    def to_row(phase, slot, sem, o):
        return copy_of(phase, slot, sem, at(y, chip_at(o), k))

    def act(when, copy, wait=False):
        @pl.when(when)
        def _():
            if wait:
                copy.wait_send()
            else:
                copy.start()

    row_first = (y == 0) & (k == 0)

    def own_moves(phase, wait=False):
        act(y == 0, to_across(phase, z), wait)
        act(k == 0, to_twin(phase, c), wait)
        for n, o in enumerate(direct):
            act(row_first | wanted(z, o), to_row(phase, c, own_send.at[phase, n], o), wait)

    def arrived(phase, slot):
        to_twin(phase, slot).wait_recv()

    def relay(phase, wait=False):
        @pl.when(second)
        def _():
            slot = at(0, z, k)
            if not wait:
                arrived(phase, slot)
            for n, o in enumerate(direct):
                act(k == 1, to_row(phase, slot, relay_send.at[phase, n], o), wait)
            act(second, to_twin(phase, slot), wait)

    def chip_of(i):
        far = jnp.where(i == 5, 3, jnp.where(i == 6, -3, 4))
        near = jnp.where(i == 1, 2, jnp.where(i == 2, -2, jnp.where(i == 3, 1, -1)))
        return source_at(jnp.where(i < 5, near, far))

    def onward(o):
        return ((0, 1), (1, 2)) if o == 2 else ((2, -1),) if o == -2 else ()

    def forward_own(phase, zs, o=0, wait=False):
        @pl.when(row_first | (wanted(zs, o) if o else zs < z))
        def _():
            slot = at(y, zs, k)
            if not wait:
                arrived(phase, slot)
            for n, step in onward(o):
                act(
                    row_first | need(zs, o + step),
                    to_row(phase, slot, onward_send.at[phase, 0, n], step),
                    wait,
                )
            act(row_first, to_across(phase, zs), wait)
            act(zs < z, to_twin(phase, slot), wait)

    def forward_other(phase, zs, o=0, wait=False):
        @pl.when(second)
        def _():
            slot = at(0, zs, k)
            if not wait:
                arrived(phase, slot)
            for n, step in onward(o):
                act(k == 1, to_row(phase, slot, onward_send.at[phase, 1, n], step), wait)
            act(second, to_twin(phase, slot), wait)

    def pairs(phase, i, use):
        zs = jnp.where(i == 0, z, chip_of(i))

        def one(other, carry):
            @pl.when((other == 0) & (zs < z) | (other == 1) & second)
            def _():
                ys = y * (1 - other)
                arrived(phase, at(ys, zs, 1 - k))
                use(ys * 8 + zs)

            return carry

        lax.fori_loop(0, 2, one, 0)

    own_moves(0)

    @pl.when(k == 1)
    def _():
        arrived(0, c - 1)

    scored(c, own_pair, True, qs, keys_all, peak, scores)
    relay(0)
    own_moves(1)
    relay(1)

    def score(p):
        scored(c, p, False, qs, keys_all, peak, scores)

    for o in (2, -2):
        forward_own(0, source_at(o), o)
    pairs(0, 0, score)
    for o in (2, -2):
        forward_other(0, source_at(o), o)

    def key_step(i, carry):
        @pl.when(i < 8)
        def _():
            forward_own(0, chip_of(i))
            forward_other(0, chip_of(i))

        pairs(0, i - 2, score)

        @pl.when(i == 5)
        def _():
            for o in (2, -2):
                forward_own(1, source_at(o), o)

        @pl.when(i == 7)
        def _():
            for o in (2, -2):
                forward_other(1, source_at(o), o)

        return carry

    lax.fori_loop(3, 10, key_step, 0)
    for h in range(HEADS):
        peak[rows(h)] = jnp.broadcast_to(
            jnp.max(peak[rows(h)], axis=1, keepdims=True), (TOK, TOK)
        )
    total[...] = jnp.zeros_like(total)
    tgt[...] = jnp.zeros_like(tgt)
    ls[...] = jnp.zeros_like(ls)
    level_weights(c, keys_all, lc, weights)

    @pl.when(k == 1)
    def _():
        arrived(1, c - 1)
        keys = keys_all[c - 1, :TOK].astype(F32).T
        for h in range(HEADS):
            ls[0, h] = mm_right_exact(keys * weights[c - 1, h : h + 1], vals[c - 1], 1, 0)

    level = local_levels()
    for h in range(HEADS):
        weighed(own_pair, h, pair_of(vals, own_pair), scores, peak, total, tgt)
        mask = jnp.full((TOK, TOK), lw[h, 0], F32)
        for j in range(1, LOW + 1):
            mask = jnp.where(level == j, lw[h, j], mask)
        local[h] = mm_right_exact(sd[h] * mask, v_ref[...], 1, 0)

    def use_values(p):
        values = pair_of(vals, p)
        keys = pair_of(keys_all, p).astype(F32).T
        weight = jnp.concatenate([weights[2 * p], weights[2 * p + 1]], axis=1)
        j = jnp.int32(0)
        for b in range(4):
            j = j + (own_pair // (1 << b) != p // (1 << b)).astype(jnp.int32)
        for h in range(HEADS):
            weighed(p, h, values, scores, peak, total, tgt)
            ls[j, h] += mm_right_exact(keys * weight[h : h + 1], values, 1, 0)

    pairs(1, 0, use_values)

    def value_step(i, carry):
        @pl.when(i < 8)
        def _():
            forward_own(1, chip_of(i))
            forward_other(1, chip_of(i))

        pairs(1, i - 2, use_values)
        return carry

    lax.fori_loop(3, 10, value_step, 0)
    for h in range(HEADS):
        tgt[h] = tgt[h] / jnp.sum(total[rows(h)], axis=1, keepdims=True)
    entry = jnp.exp(column_cumulative(g_ref[...]))
    sums_box[me] = student_whole(entry, wk, lw, gain, ls, tgt, qp, ks, comb, raw, local)

    outgoing = [
        remote("head", sums_box.at[me], sums_box.at[me], sums_send.at[d], sums_recv.at[me], peer)
        for d, peer in enumerate(head_peers)
    ]
    for copy in outgoing:
        copy.start()
    for phase in range(2):
        own_moves(phase, True)

        relay(phase, True)
        for o in direct[:2]:
            forward_own(phase, source_at(o), o, True)
            forward_other(phase, source_at(o), o, True)

        def sent(i, carry, phase=phase):
            forward_own(phase, chip_of(i), 0, True)
            forward_other(phase, chip_of(i), 0, True)
            return carry

        lax.fori_loop(3, 8, sent, 0)
    for d, peer in enumerate(head_peers):
        remote(
            "head", sums_box.at[peer], sums_box.at[peer], sums_send.at[d], sums_recv.at[peer], peer
        ).wait_recv()
    all_sums = sums_box[0]
    for i in range(1, HEADS):
        all_sums = all_sums + sums_box[i]
    small_part[...] = backward_inside(
        all_sums, entry, v_ref[...], wk, gain, ls, tgt, qp, kp, ks, mix, sd, raw, res, dstate, dquery, dkey
    )

    small_twin = remote("seq", small_part, small_pair, small_sem.at[0], small_sem.at[1], twin)
    small_twin.start()
    order = [(z + d) % 8 for d in (4, 3, 5, 1, 7, 2, 6, 0)]

    def twin_part(h):
        return remote("seq", grads.at[1 - k, h], pair.at[h], pair_send.at[h], pair_recv.at[h], twin)

    for h in order:
        q_rows = qs[pl.ds(pl.multiple_of(h * TOK, TOK), TOK)]
        grads[0, h] = mm_left_exact(q_rows, dquery[h], 0, 0)
        grads[1, h] = mm(comb[h], dstate[h], 1, 1) + mm_left_exact(k_ref[...], dkey[h], 0, 0)
        twin_part(h).start()
    small_twin.wait_recv()
    small_sum[...] = small_part[...] + small_pair[...]

    def lines(a):
        return pl.ds(0, 64) if a == 0 else pl.ds(64, PIECE - 64)

    def chip(d):
        return (z + 8 + d) % 8

    def piece(n, a):
        lean = 1 - 2 * a
        chunk, target = ((-4, -2), (-3, -1), (3, 1), (-1, -1), (1, 1), (-2, -2), (2, 2))[n]
        return remote(
            "seq", part.at[chip(lean * chunk), lines(a)], box.at[n, lines(a)], part_send.at[a, n],
            part_recv.at[a, n], at(y, chip(lean * target), k),
        )

    def ready(h):
        twin_part(h).wait_recv()
        tile = pl.multiple_of(h % 3 * 8, 8)
        part[h, :HD] = grads[k, h] + pair[h]
        part[h, HD:] = small_sum[pl.ds(tile, 8)]

    ready(order[0])
    for a in range(2):
        piece(0, a).start()
    ready(order[1])
    ready(order[2])
    for a in range(2):
        piece(1, a).start()
        piece(2, a).start()
    ready(order[3])
    ready(order[4])
    for a in range(2):
        piece(3, a).start()
        piece(4, a).start()
    for h in order[5:]:
        ready(h)
    for h in order:
        twin_part(h).wait_send()
    for a in range(2):
        lean = 1 - 2 * a
        piece(0, a).wait_recv()
        piece(1, a).wait_recv()
        part[chip(-2 * lean), lines(a)] += box[0, lines(a)] + box[1, lines(a)]
        piece(5, a).start()
        piece(2, a).wait_recv()
        part[chip(2 * lean), lines(a)] += box[2, lines(a)]
        piece(6, a).start()

    def swap(a):
        return remote(
            "seq", mine.at[lines(a)], far.at[lines(a)], swap_send.at[a], swap_recv.at[a], across
        )

    for a in range(2):
        whole = part[z, lines(a)]
        for n in range(3, 7):
            piece(n, a).wait_recv()
            whole = whole + box[n, lines(a)]
        mine[lines(a)] = whole
        swap(a).start()
    for a in range(2):
        for n in range(7):
            piece(n, a).wait_send()

    def spread(n, a):
        lean = 1 - 2 * a
        source, target = ((0, 2), (0, -2), (0, 1), (0, -1), (-2, 1), (-2, 2), (2, -1))[n]
        h = chip(lean * source)
        ref = done.at[k, h, lines(a)]
        return remote(
            "seq", ref, ref, done_send.at[a, n], done_recv.at[h, a], at(y, chip(lean * target), k)
        )

    def came(d, a):
        h = chip(d)
        ref = done.at[k, h, lines(a)]
        return remote("seq", ref, ref, done_send.at[a, 0], done_recv.at[h, a], twin)

    def sum_twin(core, h):
        ref = done.at[core, h]
        return remote("seq", ref, ref, both_send.at[h], both_recv.at[h], twin)

    for a in range(2):
        swap(a).wait_recv()
        done[k, z, lines(a)] = mine[lines(a)] + far[lines(a)]
        for n in range(4):
            spread(n, a).start()
    sum_twin(k, z).start()
    for a in range(2):
        lean = 1 - 2 * a
        came(-2 * lean, a).wait_recv()
        spread(4, a).start()
        spread(5, a).start()
        came(2 * lean, a).wait_recv()
        spread(6, a).start()
    for d in (2, -2):
        sum_twin(k, chip(d)).start()
    for d in (1, -1, 3, -3, 4):
        for a in range(2):
            came(d, a).wait_recv()
        sum_twin(k, chip(d)).start()
    for copy in outgoing + [small_twin]:
        copy.wait_send()
    for a in range(2):
        swap(a).wait_send()
        for n in range(7):
            spread(n, a).wait_send()
    for h in range(8):
        sum_twin(1 - k, h).wait_recv()
    for h in order:
        sum_twin(k, h).wait_send()


def written_kernel(done, grad_query, grad_key, levels, gains):
    grad_query[...] = done[0, :, :HD]
    grad_key[...] = done[1, :, :HD]
    tile = jnp.concatenate(
        [done[0, t, HD:] for t in range(2)] + [jnp.zeros((TOK - 16, TOK), F32)], axis=0
    ).T
    levels[...] = tile[:HEADS, :LEVELS]
    gains[...] = done[0, 2, HD:]


VM = pl.BlockSpec(memory_space=pltpu.VMEM)
SM = pl.BlockSpec(memory_space=pltpu.SMEM)
ANY = pl.BlockSpec(memory_space=pl.ANY)
DMA = pltpu.SemaphoreType.DMA


def shaped(shape, dtype=F32):
    return jax.ShapeDtypeStruct(shape, dtype)


def on_device(queries, key_vectors, value_vectors, log_gate, query_map, key_map, lw, norm_gain):
    matrix = pltpu.VMEM((HEADS, TOK, HD), F32)
    small = pltpu.VMEM((SMALL, TOK), F32)
    done = pl.pallas_call(
        whole_kernel,
        out_shape=shaped((2, HEADS, PIECE, HD)),
        in_specs=[ANY, VM, VM, VM, ANY, ANY, SM, VM],
        out_specs=VM,
        scratch_shapes=[
            pltpu.VMEM((HEADS * TOK, HD), BF),
            matrix,
            matrix,
            pltpu.VMEM((SPANS, KEY_ROWS, HD), BF),
            pltpu.VMEM((SPANS, TOK, HD), BF),
            pltpu.VMEM((SPANS // 2, HEADS * TOK, 2 * TOK), F32),
            pltpu.VMEM((HEADS * TOK, TOK), F32),
            pltpu.VMEM((HEADS * TOK, TOK), F32),
            matrix,
            pltpu.VMEM((SPANS * GATE_ROWS, TOK), F32),
            pltpu.VMEM((SPANS, HEADS, TOK), F32),
            pltpu.VMEM((CROSS, HEADS, HD, HD), F32),
            *[matrix] * 12,
            pltpu.VMEM((2, HEADS, HD, HD), F32),
            matrix,
            pltpu.VMEM((HEADS, PIECE, HD), F32),
            pltpu.VMEM((7, PIECE, HD), F32),
            pltpu.VMEM((PIECE, HD), F32),
            pltpu.VMEM((PIECE, HD), F32),
            pltpu.VMEM((HEADS, 8, TOK), F32),
            small,
            small,
            small,
            DMA((10,)),
            DMA((2, 4)),
            DMA((2, 8)),
            DMA((2, 4)),
            DMA((2, 2, 3)),
            DMA((2, SPANS)),
            DMA((2, SPANS)),
            DMA((7,)),
            DMA((HEADS,)),
            DMA((8,)),
            DMA((8,)),
            DMA((2, 7)),
            DMA((2, 7)),
            DMA((2, 7)),
            DMA((8, 2)),
            DMA((8,)),
            DMA((8,)),
            DMA((2,)),
            DMA((2,)),
            DMA((2,)),
        ],
        compiler_params=pltpu.CompilerParams(
            collective_id=0, has_side_effects=True, vmem_limit_bytes=LIMIT
        ),
        name="distill",
    )(
        queries, key_vectors, value_vectors, log_gate, query_map, key_map, lw,
        norm_gain.reshape(HEADS, HD),
    )
    grad_query, grad_key, levels, gains = pl.pallas_call(
        written_kernel,
        out_shape=(
            shaped((HEADS, HD, HD)),
            shaped((HEADS, HD, HD)),
            shaped((HEADS, LEVELS)),
            shaped((HEADS, HD)),
        ),
        in_specs=[VM],
        out_specs=(VM,) * 4,
        name="written",
    )(done)
    return grad_query, grad_key, levels, gains.reshape(-1)


def solution(mesh):
    return jax.shard_map(
        on_device,
        mesh=mesh,
        in_specs=(
            P("seq", "head"),
            P("seq", "head"),
            P("seq", "head"),
            P("head", "seq"),
            P("head", None, None),
            P("head", None, None),
            P("head", None),
            P("head"),
        ),
        out_specs=(P("head", None, None), P("head", None, None), P("head", None), P("head")),
        check_vma=False,
    )
```

```python
import jax
import jax.numpy as jnp
from jax import lax
from jax.experimental import pallas as pl
from jax.experimental.pallas import tpu as pltpu
from jax.sharding import PartitionSpec as P

F32 = jnp.float32
BF = jnp.bfloat16
HIGHEST = lax.Precision.HIGHEST
MESH = pl.DeviceIdType.MESH
NEGATIVE = -1e30
EPSILON = 1e-05
HD = 128
TOK = 128
HEADS = 8
SPANS = 32
LEVELS = 13
LOW = 7
CROSS = 5
TOKENS = TOK * SPANS
WIDTH = 64 * HD
SMALL = 24
GATE_ROWS = 32
KEY_ROWS = 128 + GATE_ROWS
PIECE = 128 + 8
LOG2E = 1.4426950408889634
SCALE = HD**-0.5 * LOG2E
LIMIT = 58 << 20


def pieces(a):
    high = a.astype(BF)
    return high, (a - high.astype(F32)).astype(BF)


def dg(a, b, ca, cb, precision=None):
    return lax.dot_general(
        a, b, (((ca,), (cb,)), ((), ())), preferred_element_type=F32, precision=precision
    )


def halves(o):
    n = o.shape[1] // 2
    return o[:, :n] + o[:, n:]


def mm(a, b, ca, cb):
    bh, bl = pieces(b)
    left = jnp.concatenate(pieces(a), axis=ca)
    right = jnp.concatenate(
        [jnp.concatenate([bh, bh], axis=cb), jnp.concatenate([bl, bl], axis=cb)], axis=1 - cb
    )
    return halves(dg(left, right, ca, cb))


def mm_left_exact(a, b, ca, cb):
    return halves(dg(a, jnp.concatenate(pieces(b), axis=1 - cb), ca, cb))


def mm_right_exact(a, b, ca, cb):
    return dg(jnp.concatenate(pieces(a), axis=ca), jnp.concatenate([b, b], axis=cb), ca, cb)


def iota(shape, dim):
    return lax.broadcasted_iota(jnp.int32, shape, dim)


def local_levels():
    x = jnp.bitwise_xor(iota((TOK, TOK), 0), iota((TOK, TOK), 1))
    level = jnp.zeros_like(x)
    for bit in range(LOW):
        level = level + (x >= 1 << bit).astype(jnp.int32)
    return level


def rows(h):
    return slice(h * TOK, (h + 1) * TOK)


def column_cumulative(gates):
    lower = (iota((TOK, TOK), 1) <= iota((TOK, TOK), 0)).astype(F32)
    return dg(lower, gates, 1, 1, HIGHEST)


def pair_of(ref, p):
    return jnp.concatenate([ref[2 * p, :TOK], ref[2 * p + 1, :TOK]], axis=0)


def scored(c, p, masked, qs, keys_all, peak, score):
    keys = pair_of(keys_all, p)
    for h in range(HEADS):
        s = dg(qs[rows(h)], keys, 1, 1)
        if masked:
            place_of = 2 * TOK * p + iota((TOK, 2 * TOK), 1)
            s = jnp.where(place_of <= c * TOK + iota((TOK, 2 * TOK), 0), s, NEGATIVE)
        score[p, rows(h)] = s
        top = jnp.maximum(s[:, :TOK], s[:, TOK:])
        peak[rows(h)] = top if masked else jnp.maximum(peak[rows(h)], top)


def weighed(p, h, values, score, peak, total, tgt):
    s = score[p, rows(h)]
    top = peak[rows(h)]
    w0 = jnp.exp2((s[:, :TOK] - top) * SCALE)
    w1 = jnp.exp2((s[:, TOK:] - top) * SCALE)
    total[rows(h)] += w0 + w1
    tgt[h] += dg(jnp.concatenate([w0.astype(BF), w1.astype(BF)], axis=1), values, 1, 0)


def level_weights(c, keys_all, lc, weights):
    later = (iota((TOK, TOK), 0) > iota((TOK, TOK), 1)).astype(BF)
    both = jnp.concatenate([later, jnp.ones((TOK, TOK), BF)], axis=1)
    lc[...] = dg(keys_all[:, TOK:].reshape(SPANS * GATE_ROWS, TOK), both, 1, 0)

    def step(i, since):
        x = c - 1 - i
        three = lc[pl.ds(pl.multiple_of(x * GATE_ROWS, GATE_ROWS), 3 * HEADS)]
        own = three[:HEADS] + three[HEADS : 2 * HEADS] + three[2 * HEADS :]
        weights[x] = jnp.exp(since + own[:, :TOK])
        return since + own[:, TOK:]

    lax.fori_loop(0, c, step, jnp.zeros((HEADS, TOK), F32))


def gate_pieces(gate):
    high = gate.astype(BF).astype(F32)
    middle = (gate - high).astype(BF).astype(F32)
    low = gate - high - middle
    return jnp.concatenate([high, middle, low, jnp.zeros_like(gate)], axis=0).astype(BF)


def student_inside(qs, key, value, gate, wq, wk, lw, qp, kp, mix, sd, local):
    upper = (iota((TOK, TOK), 0) <= iota((TOK, TOK), 1)).astype(F32)
    row_cum = dg(gate, upper, 1, 0, HIGHEST)
    col_cum = column_cumulative(gate)
    causal = iota((TOK, TOK), 1) <= iota((TOK, TOK), 0)
    level = local_levels()
    for h in range(HEADS):
        qp[h] = mm_left_exact(qs[rows(h)], wq[h], 1, 0)
        kp[h] = mm_left_exact(key, wk[h], 1, 0)
    for h in range(HEADS):
        decay = jnp.exp(
            jnp.where(causal, col_cum[:, h : h + 1] - row_cum[h : h + 1], NEGATIVE)
        )
        mask = jnp.full((TOK, TOK), lw[h, 0], F32)
        for j in range(1, LOW + 1):
            mask = jnp.where(level == j, lw[h, j], mask)
        sd[h] = mm(qp[h], kp[h], 1, 1) * decay
        mix[h] = decay * mask
        local[h] = mm_right_exact(sd[h] * mask, value, 1, 0)


def student_whole(entry, wk, lw, gain, ls, tgt, qp, ks, comb, raw, local):
    for h in range(HEADS):
        combined = lw[h, LOW + 1] * ls[0, h]
        for j in range(1, CROSS):
            combined = combined + lw[h, LOW + 1 + j] * ls[j, h]
        comb[h] = combined
        ks[h] = mm(wk[h], combined, 0, 0)
    square = jnp.zeros((TOK, HD), F32)
    scaled = jnp.zeros((TOK, HD), F32)
    against = jnp.zeros((TOK, HD), F32)
    for h in range(HEADS):
        r = local[h] + entry[:, h : h + 1] * mm(qp[h], ks[h], 1, 0)
        raw[h] = r
        rg = r * gain[h : h + 1]
        square = square + r * r
        scaled = scaled + rg * rg
        against = against + tgt[h] * rg
    one = jnp.ones((8, HD), F32)
    tile = [dg(one, x, 1, 1, HIGHEST) for x in (square, scaled, against)]
    return jnp.concatenate([t[:1] for t in tile] + [tile[0][:5]], axis=0)


def backward_inside(
    all_sums, entry, value, wk, gain, ls, tgt, qp, kp, ks, mix, sd, raw, res, dstate, dquery, dkey
):
    eye = (iota((TOK, TOK), 0) == iota((TOK, TOK), 1)).astype(F32)
    level = local_levels()
    column = dg(eye, all_sums, 1, 1, HIGHEST)
    inverse = lax.rsqrt(column[:, 0:1] / WIDTH + EPSILON)
    inner = (inverse * column[:, 1:2] - column[:, 2:3]) / TOKENS
    back = inverse * inverse * inverse * inner / WIDTH
    gain_rows = []
    for h in range(HEADS):
        g = gain[h : h + 1]
        normed = raw[h] * inverse
        mismatch = (normed * g - tgt[h]) * (1.0 / TOKENS)
        gain_rows.append(jnp.sum(mismatch * normed, axis=0, keepdims=True))
        res[h] = inverse * (mismatch * g) - raw[h] * back
    lane = iota((16, TOK), 1)
    level_tile = jnp.zeros((16, TOK), F32)
    for h in range(HEADS):
        e = entry[:, h : h + 1]
        d_mix = mm_right_exact(res[h], value, 1, 1)
        d_scores = d_mix * mix[h]
        through = d_mix * sd[h]
        dstate[h] = mm(e * qp[h], res[h], 0, 0)
        d_comb = mm(wk[h], dstate[h], 1, 0)
        dquery[h] = mm(d_scores, kp[h], 1, 0) + e * mm(res[h], ks[h], 1, 1)
        dkey[h] = mm(d_scores, qp[h], 0, 0)
        lines = [
            jnp.sum(jnp.where(level == j, through, 0.0), axis=0, keepdims=True)
            for j in range(LOW + 1)
        ]
        lines += [jnp.sum(ls[j, h] * d_comb, axis=0, keepdims=True) for j in range(CROSS)]
        lines.append(jnp.zeros((16 - LEVELS, TOK), F32))
        summed = jnp.sum(jnp.concatenate(lines, axis=0), axis=1, keepdims=True)
        level_tile = jnp.where(lane == h, summed, level_tile)
    return jnp.concatenate([level_tile] + gain_rows, axis=0)


def at(y, z, k):
    return y * 16 + z * 2 + k


def remote(axis, src, dst, send, recv, target):
    return pltpu.make_async_remote_copy(
        src_ref=src, dst_ref=dst, send_sem=send, recv_sem=recv,
        device_id={axis: target}, device_id_type=MESH,
    )


def whole_kernel(
    q_hbm, k_ref, v_ref, g_ref, wq_hbm, wk_hbm, lw, gain,
    done,
    qs, wq, wk, keys_all, vals, scores, peak, total, tgt, lc, weights, ls, qp, kp, ks, comb, mix, sd, raw, res, local,
    dstate, dquery, dkey, grads, pair, part, box, mine, far, sums_box, small_part, small_pair, small_sum,
    load, own_send, across_send, relay_send, onward_send, twin_send, recv, sums_send, sums_recv, pair_send, pair_recv,
    part_send, part_recv, done_send, done_recv, both_send, both_recv, small_sem, swap_send, swap_recv,
):
    c = lax.axis_index("seq")
    y, z, k = c // 16, c // 2 % 8, c % 2
    own_pair = c // 2
    second = y == 1
    twin, across = at(y, z, 1 - k), at(1 - y, z, k)
    me = lax.axis_index("head")
    head_peers = [(me + d) % HEADS for d in range(1, HEADS)]

    barrier = pltpu.get_barrier_semaphore()
    for target in [twin, across] + [at(y, (z + d) % 8, k) for d in (1, 2, 6, 7)]:
        pl.semaphore_signal(barrier, inc=1, device_id={"seq": target}, device_id_type=MESH)
    for peer in head_peers:
        pl.semaphore_signal(barrier, inc=1, device_id={"head": peer}, device_id_type=MESH)

    loads = [
        pltpu.make_async_copy(q_hbm.at[:, rows(h)], qs.at[rows(h)], load.at[h])
        for h in range(HEADS)
    ]
    loads.append(pltpu.make_async_copy(wq_hbm, wq, load.at[8]))
    loads.append(pltpu.make_async_copy(wk_hbm, wk, load.at[9]))
    for copy in loads:
        copy.start()
    keys_all[c, :TOK] = k_ref[...]
    keys_all[c, TOK:] = gate_pieces(g_ref[...])
    vals[c] = v_ref[...]

    @pl.when(k == 0)
    def _():
        keys_all[c + 1] = jnp.zeros((KEY_ROWS, HD), BF)
        vals[c + 1] = jnp.zeros((TOK, HD), BF)

    for copy in loads:
        copy.wait()
    student_inside(
        qs, k_ref[...], v_ref[...], g_ref[...], wq, wk, lw, qp, kp, mix, sd, local
    )
    pl.semaphore_wait(barrier, 13)

    def block(phase, slot):
        return keys_all.at[slot] if phase == 0 else vals.at[slot]

    def copy_of(phase, slot, sem, target):
        ref = block(phase, slot)
        return remote("seq", ref, ref, sem, recv.at[phase, slot], target)

    def to_twin(phase, slot):
        return copy_of(phase, slot, twin_send.at[phase, slot], twin)

    def to_across(phase, zs):
        return copy_of(phase, at(0, zs, k), across_send.at[phase, zs], across)

    lean_core = 1 - 2 * k
    direct = (2, -2, 1, -1)

    def chip_at(o):
        return (z + 8 + lean_core * o) % 8

    def source_at(o):
        return (z + 8 - lean_core * o) % 8

    def need(zs, o):
        return (zs + 8 + lean_core * o) % 8 > zs

    def wanted(zs, o):
        if o == 2:
            return need(zs, 2) | need(zs, 3) | need(zs, 4)
        return need(zs, -2) | need(zs, -3) if o == -2 else need(zs, o)

    def to_row(phase, slot, sem, o):
        return copy_of(phase, slot, sem, at(y, chip_at(o), k))

    def act(when, copy, wait=False):
        @pl.when(when)
        def _():
            if wait:
                copy.wait_send()
            else:
                copy.start()

    row_first = (y == 0) & (k == 0)

    def own_moves(phase, wait=False):
        act(y == 0, to_across(phase, z), wait)
        act(k == 0, to_twin(phase, c), wait)
        for n, o in enumerate(direct):
            act(row_first | wanted(z, o), to_row(phase, c, own_send.at[phase, n], o), wait)

    def arrived(phase, slot):
        to_twin(phase, slot).wait_recv()

    def relay(phase, wait=False):
        @pl.when(second)
        def _():
            slot = at(0, z, k)
            if not wait:
                arrived(phase, slot)
            for n, o in enumerate(direct):
                act(k == 1, to_row(phase, slot, relay_send.at[phase, n], o), wait)
            act(second, to_twin(phase, slot), wait)

    def chip_of(i):
        far = jnp.where(i == 5, 3, jnp.where(i == 6, -3, 4))
        near = jnp.where(i == 1, 2, jnp.where(i == 2, -2, jnp.where(i == 3, 1, -1)))
        return source_at(jnp.where(i < 5, near, far))

    def onward(o):
        return ((0, 1), (1, 2)) if o == 2 else ((2, -1),) if o == -2 else ()

    def forward_own(phase, zs, o=0, wait=False):
        @pl.when(row_first | (wanted(zs, o) if o else zs < z))
        def _():
            slot = at(y, zs, k)
            if not wait:
                arrived(phase, slot)
            for n, step in onward(o):
                act(
                    row_first | need(zs, o + step),
                    to_row(phase, slot, onward_send.at[phase, 0, n], step),
                    wait,
                )
            act(row_first, to_across(phase, zs), wait)
            act(zs < z, to_twin(phase, slot), wait)

    def forward_other(phase, zs, o=0, wait=False):
        @pl.when(second)
        def _():
            slot = at(0, zs, k)
            if not wait:
                arrived(phase, slot)
            for n, step in onward(o):
                act(k == 1, to_row(phase, slot, onward_send.at[phase, 1, n], step), wait)
            act(second, to_twin(phase, slot), wait)

    def pairs(phase, i, use):
        zs = jnp.where(i == 0, z, chip_of(i))

        def one(other, carry):
            @pl.when((other == 0) & (zs < z) | (other == 1) & second)
            def _():
                ys = y * (1 - other)
                arrived(phase, at(ys, zs, 1 - k))
                use(ys * 8 + zs)

            return carry

        lax.fori_loop(0, 2, one, 0)

    own_moves(0)

    @pl.when(k == 1)
    def _():
        arrived(0, c - 1)

    scored(c, own_pair, True, qs, keys_all, peak, scores)
    relay(0)
    own_moves(1)
    relay(1)

    def score(p):
        scored(c, p, False, qs, keys_all, peak, scores)

    for o in (2, -2):
        forward_own(0, source_at(o), o)
    pairs(0, 0, score)
    for o in (2, -2):
        forward_other(0, source_at(o), o)

    def key_step(i, carry):
        @pl.when(i < 8)
        def _():
            forward_own(0, chip_of(i))
            forward_other(0, chip_of(i))

        pairs(0, i - 2, score)

        @pl.when(i == 5)
        def _():
            for o in (2, -2):
                forward_own(1, source_at(o), o)

        @pl.when(i == 7)
        def _():
            for o in (2, -2):
                forward_other(1, source_at(o), o)

        return carry

    lax.fori_loop(3, 10, key_step, 0)
    for h in range(HEADS):
        peak[rows(h)] = jnp.broadcast_to(
            jnp.max(peak[rows(h)], axis=1, keepdims=True), (TOK, TOK)
        )
    total[...] = jnp.zeros_like(total)
    tgt[...] = jnp.zeros_like(tgt)
    ls[...] = jnp.zeros_like(ls)
    level_weights(c, keys_all, lc, weights)

    @pl.when(k == 1)
    def _():
        arrived(1, c - 1)
        keys = keys_all[c - 1, :TOK].astype(F32).T
        for h in range(HEADS):
            ls[0, h] = mm_right_exact(keys * weights[c - 1, h : h + 1], vals[c - 1], 1, 0)

    for h in range(HEADS):
        weighed(own_pair, h, pair_of(vals, own_pair), scores, peak, total, tgt)

    def use_values(p):
        values = pair_of(vals, p)
        keys = pair_of(keys_all, p).astype(F32).T
        weight = jnp.concatenate([weights[2 * p], weights[2 * p + 1]], axis=1)
        j = jnp.int32(0)
        for b in range(4):
            j = j + (own_pair // (1 << b) != p // (1 << b)).astype(jnp.int32)
        for h in range(HEADS):
            weighed(p, h, values, scores, peak, total, tgt)
            ls[j, h] += mm_right_exact(keys * weight[h : h + 1], values, 1, 0)

    pairs(1, 0, use_values)

    def value_step(i, carry):
        @pl.when(i < 8)
        def _():
            forward_own(1, chip_of(i))
            forward_other(1, chip_of(i))

        pairs(1, i - 2, use_values)
        return carry

    lax.fori_loop(3, 10, value_step, 0)
    for h in range(HEADS):
        tgt[h] = tgt[h] / jnp.sum(total[rows(h)], axis=1, keepdims=True)
    entry = jnp.exp(column_cumulative(g_ref[...]))
    sums_box[me] = student_whole(entry, wk, lw, gain, ls, tgt, qp, ks, comb, raw, local)

    outgoing = [
        remote("head", sums_box.at[me], sums_box.at[me], sums_send.at[d], sums_recv.at[me], peer)
        for d, peer in enumerate(head_peers)
    ]
    for copy in outgoing:
        copy.start()
    for phase in range(2):
        own_moves(phase, True)

        relay(phase, True)
        for o in direct[:2]:
            forward_own(phase, source_at(o), o, True)
            forward_other(phase, source_at(o), o, True)

        def sent(i, carry, phase=phase):
            forward_own(phase, chip_of(i), 0, True)
            forward_other(phase, chip_of(i), 0, True)
            return carry

        lax.fori_loop(3, 8, sent, 0)
    for d, peer in enumerate(head_peers):
        remote(
            "head", sums_box.at[peer], sums_box.at[peer], sums_send.at[d], sums_recv.at[peer], peer
        ).wait_recv()
    all_sums = sums_box[0]
    for i in range(1, HEADS):
        all_sums = all_sums + sums_box[i]
    small_part[...] = backward_inside(
        all_sums, entry, v_ref[...], wk, gain, ls, tgt, qp, kp, ks, mix, sd, raw, res, dstate, dquery, dkey
    )

    small_twin = remote("seq", small_part, small_pair, small_sem.at[0], small_sem.at[1], twin)
    small_twin.start()
    order = [(z + d) % 8 for d in (4, 3, 5, 1, 7, 2, 6, 0)]

    def twin_part(h):
        return remote("seq", grads.at[1 - k, h], pair.at[h], pair_send.at[h], pair_recv.at[h], twin)

    def product(h):
        q_rows = qs[pl.ds(pl.multiple_of(h * TOK, TOK), TOK)]
        grads[0, h] = mm_left_exact(q_rows, dquery[h], 0, 0)
        grads[1, h] = mm(comb[h], dstate[h], 1, 1) + mm_left_exact(k_ref[...], dkey[h], 0, 0)

    def products(heads):
        for h in heads:
            product(h)
        for h in heads:
            twin_part(h).start()

    products(order[:3])
    products(order[3:6])
    small_twin.wait_recv()
    small_sum[...] = small_part[...] + small_pair[...]

    def lines(a):
        return pl.ds(0, 64) if a == 0 else pl.ds(64, PIECE - 64)

    def chip(d):
        return (z + 8 + d) % 8

    def piece(n, a):
        lean = 1 - 2 * a
        chunk, target = ((-4, -2), (-3, -1), (3, 1), (-1, -1), (1, 1), (-2, -2), (2, 2))[n]
        return remote(
            "seq", part.at[chip(lean * chunk), lines(a)], box.at[n, lines(a)], part_send.at[a, n],
            part_recv.at[a, n], at(y, chip(lean * target), k),
        )

    def ready(h):
        twin_part(h).wait_recv()
        tile = pl.multiple_of(h % 3 * 8, 8)
        part[h, :HD] = grads[k, h] + pair[h]
        part[h, HD:] = small_sum[pl.ds(tile, 8)]

    ready(order[0])
    for a in range(2):
        piece(0, a).start()
    ready(order[1])
    ready(order[2])
    for a in range(2):
        piece(1, a).start()
        piece(2, a).start()
    products(order[6:])
    ready(order[3])
    ready(order[4])
    for a in range(2):
        piece(3, a).start()
        piece(4, a).start()
    for h in order[5:]:
        ready(h)
    for h in order:
        twin_part(h).wait_send()
    for a in range(2):
        lean = 1 - 2 * a
        piece(0, a).wait_recv()
        piece(1, a).wait_recv()
        part[chip(-2 * lean), lines(a)] += box[0, lines(a)] + box[1, lines(a)]
        piece(5, a).start()
        piece(2, a).wait_recv()
        part[chip(2 * lean), lines(a)] += box[2, lines(a)]
        piece(6, a).start()

    def swap(a):
        return remote(
            "seq", mine.at[lines(a)], far.at[lines(a)], swap_send.at[a], swap_recv.at[a], across
        )

    for a in range(2):
        whole = part[z, lines(a)]
        for n in range(3, 7):
            piece(n, a).wait_recv()
            whole = whole + box[n, lines(a)]
        mine[lines(a)] = whole
        swap(a).start()
    for a in range(2):
        for n in range(7):
            piece(n, a).wait_send()

    def spread(n, a):
        lean = 1 - 2 * a
        source, target = ((0, 2), (0, -2), (0, 1), (0, -1), (-2, 1), (-2, 2), (2, -1))[n]
        h = chip(lean * source)
        ref = done.at[k, h, lines(a)]
        return remote(
            "seq", ref, ref, done_send.at[a, n], done_recv.at[h, a], at(y, chip(lean * target), k)
        )

    def came(d, a):
        h = chip(d)
        ref = done.at[k, h, lines(a)]
        return remote("seq", ref, ref, done_send.at[a, 0], done_recv.at[h, a], twin)

    def sum_twin(core, h):
        ref = done.at[core, h]
        return remote("seq", ref, ref, both_send.at[h], both_recv.at[h], twin)

    for a in range(2):
        swap(a).wait_recv()
        done[k, z, lines(a)] = mine[lines(a)] + far[lines(a)]
        for n in range(4):
            spread(n, a).start()
    sum_twin(k, z).start()
    for a in range(2):
        lean = 1 - 2 * a
        came(-2 * lean, a).wait_recv()
        spread(4, a).start()
        spread(5, a).start()
        came(2 * lean, a).wait_recv()
        spread(6, a).start()
    for d in (2, -2):
        sum_twin(k, chip(d)).start()
    for d in (1, -1, 3, -3, 4):
        for a in range(2):
            came(d, a).wait_recv()
        sum_twin(k, chip(d)).start()
    for copy in outgoing + [small_twin]:
        copy.wait_send()
    for a in range(2):
        swap(a).wait_send()
        for n in range(7):
            spread(n, a).wait_send()
    for h in range(8):
        sum_twin(1 - k, h).wait_recv()
    for h in order:
        sum_twin(k, h).wait_send()


def written_kernel(done, grad_query, grad_key, levels, gains, small, sems):
    copies = [
        pltpu.make_async_copy(done.at[0, :3, HD:], small, sems.at[0]),
        pltpu.make_async_copy(done.at[0, :, :HD], grad_query, sems.at[1]),
        pltpu.make_async_copy(done.at[1, :, :HD], grad_key, sems.at[2]),
    ]
    for copy in copies:
        copy.start()
    copies[0].wait()
    tile = jnp.concatenate([small[0], small[1], jnp.zeros((TOK - 16, TOK), F32)], axis=0).T
    levels[...] = tile[:HEADS, :LEVELS]
    gains[...] = small[2]
    for copy in copies[1:]:
        copy.wait()


VM = pl.BlockSpec(memory_space=pltpu.VMEM)
SM = pl.BlockSpec(memory_space=pltpu.SMEM)
ANY = pl.BlockSpec(memory_space=pl.ANY)
DMA = pltpu.SemaphoreType.DMA


def shaped(shape, dtype=F32):
    return jax.ShapeDtypeStruct(shape, dtype)


def on_device(queries, key_vectors, value_vectors, log_gate, query_map, key_map, lw, norm_gain):
    matrix = pltpu.VMEM((HEADS, TOK, HD), F32)
    small = pltpu.VMEM((SMALL, TOK), F32)
    done = pl.pallas_call(
        whole_kernel,
        out_shape=shaped((2, HEADS, PIECE, HD)),
        in_specs=[ANY, VM, VM, VM, ANY, ANY, SM, VM],
        out_specs=VM,
        scratch_shapes=[
            pltpu.VMEM((HEADS * TOK, HD), BF),
            matrix,
            matrix,
            pltpu.VMEM((SPANS, KEY_ROWS, HD), BF),
            pltpu.VMEM((SPANS, TOK, HD), BF),
            pltpu.VMEM((SPANS // 2, HEADS * TOK, 2 * TOK), F32),
            pltpu.VMEM((HEADS * TOK, TOK), F32),
            pltpu.VMEM((HEADS * TOK, TOK), F32),
            matrix,
            pltpu.VMEM((SPANS * GATE_ROWS, 2 * TOK), F32),
            pltpu.VMEM((SPANS, HEADS, TOK), F32),
            pltpu.VMEM((CROSS, HEADS, HD, HD), F32),
            *[matrix] * 12,
            pltpu.VMEM((2, HEADS, HD, HD), F32),
            matrix,
            pltpu.VMEM((HEADS, PIECE, HD), F32),
            pltpu.VMEM((7, PIECE, HD), F32),
            pltpu.VMEM((PIECE, HD), F32),
            pltpu.VMEM((PIECE, HD), F32),
            pltpu.VMEM((HEADS, 8, TOK), F32),
            small,
            small,
            small,
            DMA((10,)),
            DMA((2, 4)),
            DMA((2, 8)),
            DMA((2, 4)),
            DMA((2, 2, 3)),
            DMA((2, SPANS)),
            DMA((2, SPANS)),
            DMA((7,)),
            DMA((HEADS,)),
            DMA((8,)),
            DMA((8,)),
            DMA((2, 7)),
            DMA((2, 7)),
            DMA((2, 7)),
            DMA((8, 2)),
            DMA((8,)),
            DMA((8,)),
            DMA((2,)),
            DMA((2,)),
            DMA((2,)),
        ],
        compiler_params=pltpu.CompilerParams(
            collective_id=0, has_side_effects=True, vmem_limit_bytes=LIMIT
        ),
        name="distill",
    )(
        queries, key_vectors, value_vectors, log_gate, query_map, key_map, lw,
        norm_gain.reshape(HEADS, HD),
    )
    grad_query, grad_key, levels, gains = pl.pallas_call(
        written_kernel,
        out_shape=(
            shaped((HEADS, HD, HD)),
            shaped((HEADS, HD, HD)),
            shaped((HEADS, LEVELS)),
            shaped((HEADS, HD)),
        ),
        in_specs=[ANY],
        out_specs=(ANY, ANY, VM, VM),
        scratch_shapes=[pltpu.VMEM((3, 8, TOK), F32), DMA((3,))],
        name="written",
    )(done)
    return grad_query, grad_key, levels, gains.reshape(-1)


def solution(mesh):
    return jax.shard_map(
        on_device,
        mesh=mesh,
        in_specs=(
            P("seq", "head"),
            P("seq", "head"),
            P("seq", "head"),
            P("head", "seq"),
            P("head", None, None),
            P("head", None, None),
            P("head", None),
            P("head"),
        ),
        out_specs=(P("head", None, None), P("head", None, None), P("head", None), P("head")),
        check_vma=False,
    )
```

```python
import jax
import jax.numpy as jnp
from jax import lax
from jax.experimental import pallas as pl
from jax.experimental.pallas import tpu as pltpu
from jax.sharding import PartitionSpec as P

F32 = jnp.float32
BF = jnp.bfloat16
HIGHEST = lax.Precision.HIGHEST
MESH = pl.DeviceIdType.MESH
NEGATIVE = -1e30
EPSILON = 1e-05
HD = 128
TOK = 128
HEADS = 8
SPANS = 32
LEVELS = 13
LOW = 7
CROSS = 5
TOKENS = TOK * SPANS
WIDTH = 64 * HD
SMALL = 24
GATE_ROWS = 32
KEY_ROWS = 128 + GATE_ROWS
PIECE = 128 + 8
LOG2E = 1.4426950408889634
SCALE = HD**-0.5 * LOG2E
LIMIT = 58 << 20


def pieces(a):
    high = a.astype(BF)
    return high, (a - high.astype(F32)).astype(BF)


def dg(a, b, ca, cb, precision=None):
    return lax.dot_general(
        a, b, (((ca,), (cb,)), ((), ())), preferred_element_type=F32, precision=precision
    )


def halves(o):
    n = o.shape[1] // 2
    return o[:, :n] + o[:, n:]


def mm(a, b, ca, cb):
    bh, bl = pieces(b)
    left = jnp.concatenate(pieces(a), axis=ca)
    right = jnp.concatenate(
        [jnp.concatenate([bh, bh], axis=cb), jnp.concatenate([bl, bl], axis=cb)], axis=1 - cb
    )
    return halves(dg(left, right, ca, cb))


def mm_left_exact(a, b, ca, cb):
    return halves(dg(a, jnp.concatenate(pieces(b), axis=1 - cb), ca, cb))


def mm_right_exact(a, b, ca, cb):
    return dg(jnp.concatenate(pieces(a), axis=ca), jnp.concatenate([b, b], axis=cb), ca, cb)


def iota(shape, dim):
    return lax.broadcasted_iota(jnp.int32, shape, dim)


def local_levels():
    x = jnp.bitwise_xor(iota((TOK, TOK), 0), iota((TOK, TOK), 1))
    level = jnp.zeros_like(x)
    for bit in range(LOW):
        level = level + (x >= 1 << bit).astype(jnp.int32)
    return level


def rows(h):
    return slice(h * TOK, (h + 1) * TOK)


def column_cumulative(gates):
    lower = (iota((TOK, TOK), 1) <= iota((TOK, TOK), 0)).astype(F32)
    return dg(lower, gates, 1, 1, HIGHEST)


def pair_of(ref, p):
    return jnp.concatenate([ref[2 * p, :TOK], ref[2 * p + 1, :TOK]], axis=0)


def scored(c, p, masked, qs, keys_all, peak, score):
    keys = pair_of(keys_all, p)
    for h in range(HEADS):
        s = dg(qs[rows(h)], keys, 1, 1)
        if masked:
            place_of = 2 * TOK * p + iota((TOK, 2 * TOK), 1)
            s = jnp.where(place_of <= c * TOK + iota((TOK, 2 * TOK), 0), s, NEGATIVE)
        score[p, rows(h)] = s
        top = jnp.maximum(s[:, :TOK], s[:, TOK:])
        peak[rows(h)] = top if masked else jnp.maximum(peak[rows(h)], top)


def weighed(p, h, values, score, peak, total, tgt):
    s = score[p, rows(h)]
    top = peak[rows(h)]
    w0 = jnp.exp2((s[:, :TOK] - top) * SCALE)
    w1 = jnp.exp2((s[:, TOK:] - top) * SCALE)
    total[rows(h)] += w0 + w1
    tgt[h] += dg(jnp.concatenate([w0.astype(BF), w1.astype(BF)], axis=1), values, 1, 0)


def level_weights(c, keys_all, lc, weights):
    later = (iota((TOK, TOK), 0) > iota((TOK, TOK), 1)).astype(BF)
    both = jnp.concatenate([later, jnp.ones((TOK, TOK), BF)], axis=1)
    lc[...] = dg(keys_all[:, TOK:].reshape(SPANS * GATE_ROWS, TOK), both, 1, 0)

    def step(i, since):
        x = c - 1 - i
        three = lc[pl.ds(pl.multiple_of(x * GATE_ROWS, GATE_ROWS), 3 * HEADS)]
        own = three[:HEADS] + three[HEADS : 2 * HEADS] + three[2 * HEADS :]
        weights[x] = jnp.exp(since + own[:, :TOK])
        return since + own[:, TOK:]

    lax.fori_loop(0, c, step, jnp.zeros((HEADS, TOK), F32))


def gate_pieces(gate):
    high = gate.astype(BF).astype(F32)
    middle = (gate - high).astype(BF).astype(F32)
    low = gate - high - middle
    return jnp.concatenate([high, middle, low, jnp.zeros_like(gate)], axis=0).astype(BF)


def student_inside(qs, key, value, gate, wq, wk, lw, qp, kp, mix, sd, local):
    upper = (iota((TOK, TOK), 0) <= iota((TOK, TOK), 1)).astype(F32)
    row_cum = dg(gate, upper, 1, 0, HIGHEST)
    col_cum = column_cumulative(gate)
    causal = iota((TOK, TOK), 1) <= iota((TOK, TOK), 0)
    level = local_levels()
    for h in range(HEADS):
        qp[h] = mm_left_exact(qs[rows(h)], wq[h], 1, 0)
        kp[h] = mm_left_exact(key, wk[h], 1, 0)
    for h in range(HEADS):
        decay = jnp.exp(
            jnp.where(causal, col_cum[:, h : h + 1] - row_cum[h : h + 1], NEGATIVE)
        )
        mask = jnp.full((TOK, TOK), lw[h, 0], F32)
        for j in range(1, LOW + 1):
            mask = jnp.where(level == j, lw[h, j], mask)
        sd[h] = mm(qp[h], kp[h], 1, 1) * decay
        mix[h] = decay * mask
        local[h] = mm_right_exact(sd[h] * mask, value, 1, 0)


def student_whole(entry, wk, lw, gain, ls, tgt, qp, ks, comb, raw, local):
    for h in range(HEADS):
        combined = lw[h, LOW + 1] * ls[0, h]
        for j in range(1, CROSS):
            combined = combined + lw[h, LOW + 1 + j] * ls[j, h]
        comb[h] = combined
        ks[h] = mm(wk[h], combined, 0, 0)
    square = jnp.zeros((TOK, HD), F32)
    scaled = jnp.zeros((TOK, HD), F32)
    against = jnp.zeros((TOK, HD), F32)
    for h in range(HEADS):
        r = local[h] + entry[:, h : h + 1] * mm(qp[h], ks[h], 1, 0)
        raw[h] = r
        rg = r * gain[h : h + 1]
        square = square + r * r
        scaled = scaled + rg * rg
        against = against + tgt[h] * rg
    one = jnp.ones((8, HD), F32)
    tile = [dg(one, x, 1, 1, HIGHEST) for x in (square, scaled, against)]
    return jnp.concatenate([t[:1] for t in tile] + [tile[0][:5]], axis=0)


def backward_inside(
    all_sums, entry, value, wk, gain, ls, tgt, qp, kp, ks, mix, sd, raw, res, dstate, dquery, dkey
):
    eye = (iota((TOK, TOK), 0) == iota((TOK, TOK), 1)).astype(F32)
    level = local_levels()
    column = dg(eye, all_sums, 1, 1, HIGHEST)
    inverse = lax.rsqrt(column[:, 0:1] / WIDTH + EPSILON)
    inner = (inverse * column[:, 1:2] - column[:, 2:3]) / TOKENS
    back = inverse * inverse * inverse * inner / WIDTH
    gain_rows = []
    for h in range(HEADS):
        g = gain[h : h + 1]
        normed = raw[h] * inverse
        mismatch = (normed * g - tgt[h]) * (1.0 / TOKENS)
        gain_rows.append(jnp.sum(mismatch * normed, axis=0, keepdims=True))
        res[h] = inverse * (mismatch * g) - raw[h] * back
    lane = iota((16, TOK), 1)
    level_tile = jnp.zeros((16, TOK), F32)
    for h in range(HEADS):
        e = entry[:, h : h + 1]
        d_mix = mm_right_exact(res[h], value, 1, 1)
        d_scores = d_mix * mix[h]
        through = d_mix * sd[h]
        dstate[h] = mm(e * qp[h], res[h], 0, 0)
        d_comb = mm(wk[h], dstate[h], 1, 0)
        dquery[h] = mm(d_scores, kp[h], 1, 0) + e * mm(res[h], ks[h], 1, 1)
        dkey[h] = mm(d_scores, qp[h], 0, 0)
        lines = [
            jnp.sum(jnp.where(level == j, through, 0.0), axis=0, keepdims=True)
            for j in range(LOW + 1)
        ]
        lines += [jnp.sum(ls[j, h] * d_comb, axis=0, keepdims=True) for j in range(CROSS)]
        lines.append(jnp.zeros((16 - LEVELS, TOK), F32))
        summed = jnp.sum(jnp.concatenate(lines, axis=0), axis=1, keepdims=True)
        level_tile = jnp.where(lane == h, summed, level_tile)
    return jnp.concatenate([level_tile] + gain_rows, axis=0)


def at(y, z, k):
    return y * 16 + z * 2 + k


def remote(axis, src, dst, send, recv, target):
    return pltpu.make_async_remote_copy(
        src_ref=src, dst_ref=dst, send_sem=send, recv_sem=recv,
        device_id={axis: target}, device_id_type=MESH,
    )


def whole_kernel(
    q_hbm, k_hbm, v_hbm, g_hbm, wq_hbm, wk_hbm, lw, gain_hbm,
    done,
    k_ref, v_ref, g_ref, gain, qs, wq, wk, keys_all, vals, scores, peak, total, tgt, lc, weights, ls, qp, kp, ks, comb, mix, sd, raw, res, local,
    dstate, dquery, dkey, grads, pair, part, box, mine, far, sums_box, small_part, small_pair, small_sum,
    load, own_send, across_send, relay_send, onward_send, twin_send, recv, sums_send, sums_recv, pair_send, pair_recv,
    part_send, part_recv, done_send, done_recv, both_send, both_recv, small_sem, swap_send, swap_recv,
):
    c = lax.axis_index("seq")
    y, z, k = c // 16, c // 2 % 8, c % 2
    own_pair = c // 2
    second = y == 1
    twin, across = at(y, z, 1 - k), at(1 - y, z, k)
    me = lax.axis_index("head")
    head_peers = [(me + d) % HEADS for d in range(1, HEADS)]

    barrier = pltpu.get_barrier_semaphore()
    for target in [twin, across] + [at(y, (z + d) % 8, k) for d in (1, 2, 6, 7)]:
        pl.semaphore_signal(barrier, inc=1, device_id={"seq": target}, device_id_type=MESH)
    for peer in head_peers:
        pl.semaphore_signal(barrier, inc=1, device_id={"head": peer}, device_id_type=MESH)

    loads = [
        pltpu.make_async_copy(q_hbm.at[:, rows(h)], qs.at[rows(h)], load.at[h])
        for h in range(HEADS)
    ]
    loads.append(pltpu.make_async_copy(wq_hbm, wq, load.at[8]))
    loads.append(pltpu.make_async_copy(wk_hbm, wk, load.at[9]))
    own = ((k_hbm, k_ref), (v_hbm, v_ref), (g_hbm, g_ref), (gain_hbm, gain))
    first_loads = [pltpu.make_async_copy(a, b, load.at[10 + n]) for n, (a, b) in enumerate(own)]
    for copy in first_loads + loads:
        copy.start()
    for copy in first_loads:
        copy.wait()
    keys_all[c, :TOK] = k_ref[...]
    keys_all[c, TOK:] = gate_pieces(g_ref[...])
    vals[c] = v_ref[...]

    @pl.when(k == 0)
    def _():
        keys_all[c + 1] = jnp.zeros((KEY_ROWS, HD), BF)
        vals[c + 1] = jnp.zeros((TOK, HD), BF)

    for copy in loads:
        copy.wait()
    student_inside(
        qs, k_ref[...], v_ref[...], g_ref[...], wq, wk, lw, qp, kp, mix, sd, local
    )
    pl.semaphore_wait(barrier, 13)

    def block(phase, slot):
        return keys_all.at[slot] if phase == 0 else vals.at[slot]

    def copy_of(phase, slot, sem, target):
        ref = block(phase, slot)
        return remote("seq", ref, ref, sem, recv.at[phase, slot], target)

    def to_twin(phase, slot):
        return copy_of(phase, slot, twin_send.at[phase, slot], twin)

    def to_across(phase, zs):
        return copy_of(phase, at(0, zs, k), across_send.at[phase, zs], across)

    lean_core = 1 - 2 * k
    direct = (2, -2, 1, -1)

    def chip_at(o):
        return (z + 8 + lean_core * o) % 8

    def source_at(o):
        return (z + 8 - lean_core * o) % 8

    def need(zs, o):
        return (zs + 8 + lean_core * o) % 8 > zs

    def wanted(zs, o):
        if o == 2:
            return need(zs, 2) | need(zs, 3) | need(zs, 4)
        return need(zs, -2) | need(zs, -3) if o == -2 else need(zs, o)

    def to_row(phase, slot, sem, o):
        return copy_of(phase, slot, sem, at(y, chip_at(o), k))

    def act(when, copy, wait=False):
        @pl.when(when)
        def _():
            if wait:
                copy.wait_send()
            else:
                copy.start()

    row_first = (y == 0) & (k == 0)

    def own_moves(phase, wait=False):
        act(y == 0, to_across(phase, z), wait)
        act(k == 0, to_twin(phase, c), wait)
        for n, o in enumerate(direct):
            act(row_first | wanted(z, o), to_row(phase, c, own_send.at[phase, n], o), wait)

    def arrived(phase, slot):
        to_twin(phase, slot).wait_recv()

    def relay(phase, wait=False):
        @pl.when(second)
        def _():
            slot = at(0, z, k)
            if not wait:
                arrived(phase, slot)
            for n, o in enumerate(direct):
                act(k == 1, to_row(phase, slot, relay_send.at[phase, n], o), wait)
            act(second, to_twin(phase, slot), wait)

    def chip_of(i):
        far = jnp.where(i == 5, 3, jnp.where(i == 6, -3, 4))
        near = jnp.where(i == 1, 2, jnp.where(i == 2, -2, jnp.where(i == 3, 1, -1)))
        return source_at(jnp.where(i < 5, near, far))

    def onward(o):
        return ((0, 1), (1, 2)) if o == 2 else ((2, -1),) if o == -2 else ()

    def forward_own(phase, zs, o=0, wait=False):
        @pl.when(row_first | (wanted(zs, o) if o else zs < z))
        def _():
            slot = at(y, zs, k)
            if not wait:
                arrived(phase, slot)
            for n, step in onward(o):
                act(
                    row_first | need(zs, o + step),
                    to_row(phase, slot, onward_send.at[phase, 0, n], step),
                    wait,
                )
            act(row_first, to_across(phase, zs), wait)
            act(zs < z, to_twin(phase, slot), wait)

    def forward_other(phase, zs, o=0, wait=False):
        @pl.when(second)
        def _():
            slot = at(0, zs, k)
            if not wait:
                arrived(phase, slot)
            for n, step in onward(o):
                act(k == 1, to_row(phase, slot, onward_send.at[phase, 1, n], step), wait)
            act(second, to_twin(phase, slot), wait)

    def pairs(phase, i, use):
        zs = jnp.where(i == 0, z, chip_of(i))

        def one(other, carry):
            @pl.when((other == 0) & (zs < z) | (other == 1) & second)
            def _():
                ys = y * (1 - other)
                arrived(phase, at(ys, zs, 1 - k))
                use(ys * 8 + zs)

            return carry

        lax.fori_loop(0, 2, one, 0)

    own_moves(0)

    @pl.when(k == 1)
    def _():
        arrived(0, c - 1)

    scored(c, own_pair, True, qs, keys_all, peak, scores)
    relay(0)
    own_moves(1)
    relay(1)

    def score(p):
        scored(c, p, False, qs, keys_all, peak, scores)

    for o in (2, -2):
        forward_own(0, source_at(o), o)
    pairs(0, 0, score)
    for o in (2, -2):
        forward_other(0, source_at(o), o)

    def key_step(i, carry):
        @pl.when(i < 8)
        def _():
            forward_own(0, chip_of(i))
            forward_other(0, chip_of(i))

        pairs(0, i - 2, score)

        @pl.when(i == 5)
        def _():
            for o in (2, -2):
                forward_own(1, source_at(o), o)

        @pl.when(i == 7)
        def _():
            for o in (2, -2):
                forward_other(1, source_at(o), o)

        return carry

    lax.fori_loop(3, 10, key_step, 0)
    for h in range(HEADS):
        peak[rows(h)] = jnp.broadcast_to(
            jnp.max(peak[rows(h)], axis=1, keepdims=True), (TOK, TOK)
        )
    total[...] = jnp.zeros_like(total)
    tgt[...] = jnp.zeros_like(tgt)
    ls[...] = jnp.zeros_like(ls)
    level_weights(c, keys_all, lc, weights)

    @pl.when(k == 1)
    def _():
        arrived(1, c - 1)
        keys = keys_all[c - 1, :TOK].astype(F32).T
        for h in range(HEADS):
            ls[0, h] = mm_right_exact(keys * weights[c - 1, h : h + 1], vals[c - 1], 1, 0)

    for h in range(HEADS):
        weighed(own_pair, h, pair_of(vals, own_pair), scores, peak, total, tgt)

    def use_values(p):
        values = pair_of(vals, p)
        keys = pair_of(keys_all, p).astype(F32).T
        weight = jnp.concatenate([weights[2 * p], weights[2 * p + 1]], axis=1)
        j = jnp.int32(0)
        for b in range(4):
            j = j + (own_pair // (1 << b) != p // (1 << b)).astype(jnp.int32)
        for h in range(HEADS):
            weighed(p, h, values, scores, peak, total, tgt)
            ls[j, h] += mm_right_exact(keys * weight[h : h + 1], values, 1, 0)

    pairs(1, 0, use_values)

    def value_step(i, carry):
        @pl.when(i < 8)
        def _():
            forward_own(1, chip_of(i))
            forward_other(1, chip_of(i))

        pairs(1, i - 2, use_values)
        return carry

    lax.fori_loop(3, 10, value_step, 0)
    for h in range(HEADS):
        tgt[h] = tgt[h] / jnp.sum(total[rows(h)], axis=1, keepdims=True)
    entry = jnp.exp(column_cumulative(g_ref[...]))
    sums_box[me] = student_whole(entry, wk, lw, gain, ls, tgt, qp, ks, comb, raw, local)

    outgoing = [
        remote("head", sums_box.at[me], sums_box.at[me], sums_send.at[d], sums_recv.at[me], peer)
        for d, peer in enumerate(head_peers)
    ]
    for copy in outgoing:
        copy.start()
    for phase in range(2):
        own_moves(phase, True)

        relay(phase, True)
        for o in direct[:2]:
            forward_own(phase, source_at(o), o, True)
            forward_other(phase, source_at(o), o, True)

        def sent(i, carry, phase=phase):
            forward_own(phase, chip_of(i), 0, True)
            forward_other(phase, chip_of(i), 0, True)
            return carry

        lax.fori_loop(3, 8, sent, 0)
    for d, peer in enumerate(head_peers):
        remote(
            "head", sums_box.at[peer], sums_box.at[peer], sums_send.at[d], sums_recv.at[peer], peer
        ).wait_recv()
    all_sums = sums_box[0]
    for i in range(1, HEADS):
        all_sums = all_sums + sums_box[i]
    small_part[...] = backward_inside(
        all_sums, entry, v_ref[...], wk, gain, ls, tgt, qp, kp, ks, mix, sd, raw, res, dstate, dquery, dkey
    )

    small_twin = remote("seq", small_part, small_pair, small_sem.at[0], small_sem.at[1], twin)
    small_twin.start()
    order = [(z + d) % 8 for d in (4, 3, 5, 1, 7, 2, 6, 0)]

    def twin_part(h):
        return remote("seq", grads.at[1 - k, h], pair.at[h], pair_send.at[h], pair_recv.at[h], twin)

    def product(h):
        q_rows = qs[pl.ds(pl.multiple_of(h * TOK, TOK), TOK)]
        grads[0, h] = mm_left_exact(q_rows, dquery[h], 0, 0)
        grads[1, h] = mm(comb[h], dstate[h], 1, 1) + mm_left_exact(k_ref[...], dkey[h], 0, 0)

    def products(heads):
        for h in heads:
            product(h)
        for h in heads:
            twin_part(h).start()

    products(order[:3])
    products(order[3:6])
    small_twin.wait_recv()
    small_sum[...] = small_part[...] + small_pair[...]

    def lines(a):
        return pl.ds(0, 64) if a == 0 else pl.ds(64, PIECE - 64)

    def chip(d):
        return (z + 8 + d) % 8

    def piece(n, a):
        lean = 1 - 2 * a
        chunk, target = ((-4, -2), (-3, -1), (3, 1), (-1, -1), (1, 1), (-2, -2), (2, 2))[n]
        return remote(
            "seq", part.at[chip(lean * chunk), lines(a)], box.at[n, lines(a)], part_send.at[a, n],
            part_recv.at[a, n], at(y, chip(lean * target), k),
        )

    def ready(h):
        twin_part(h).wait_recv()
        tile = pl.multiple_of(h % 3 * 8, 8)
        part[h, :HD] = grads[k, h] + pair[h]
        part[h, HD:] = small_sum[pl.ds(tile, 8)]

    ready(order[0])
    for a in range(2):
        piece(0, a).start()
    ready(order[1])
    ready(order[2])
    for a in range(2):
        piece(1, a).start()
        piece(2, a).start()
    products(order[6:])
    ready(order[3])
    ready(order[4])
    for a in range(2):
        piece(3, a).start()
        piece(4, a).start()
    for h in order[5:]:
        ready(h)
    for h in order:
        twin_part(h).wait_send()
    for a in range(2):
        lean = 1 - 2 * a
        piece(0, a).wait_recv()
        piece(1, a).wait_recv()
        part[chip(-2 * lean), lines(a)] += box[0, lines(a)] + box[1, lines(a)]
        piece(5, a).start()
        piece(2, a).wait_recv()
        part[chip(2 * lean), lines(a)] += box[2, lines(a)]
        piece(6, a).start()

    def swap(a):
        return remote(
            "seq", mine.at[lines(a)], far.at[lines(a)], swap_send.at[a], swap_recv.at[a], across
        )

    for a in range(2):
        whole = part[z, lines(a)]
        for n in range(3, 7):
            piece(n, a).wait_recv()
            whole = whole + box[n, lines(a)]
        mine[lines(a)] = whole
        swap(a).start()
    for a in range(2):
        for n in range(7):
            piece(n, a).wait_send()

    def spread(n, a):
        lean = 1 - 2 * a
        source, target = ((0, 2), (0, -2), (0, 1), (0, -1), (-2, 1), (-2, 2), (2, -1))[n]
        h = chip(lean * source)
        ref = done.at[k, h, lines(a)]
        return remote(
            "seq", ref, ref, done_send.at[a, n], done_recv.at[h, a], at(y, chip(lean * target), k)
        )

    def came(d, a):
        h = chip(d)
        ref = done.at[k, h, lines(a)]
        return remote("seq", ref, ref, done_send.at[a, 0], done_recv.at[h, a], twin)

    def sum_twin(core, h):
        ref = done.at[core, h]
        return remote("seq", ref, ref, both_send.at[h], both_recv.at[h], twin)

    for a in range(2):
        swap(a).wait_recv()
        done[k, z, lines(a)] = mine[lines(a)] + far[lines(a)]
        for n in range(4):
            spread(n, a).start()
    sum_twin(k, z).start()
    for a in range(2):
        lean = 1 - 2 * a
        came(-2 * lean, a).wait_recv()
        spread(4, a).start()
        spread(5, a).start()
        came(2 * lean, a).wait_recv()
        spread(6, a).start()
    for d in (2, -2):
        sum_twin(k, chip(d)).start()
    for d in (1, -1, 3, -3, 4):
        for a in range(2):
            came(d, a).wait_recv()
        sum_twin(k, chip(d)).start()
    for copy in outgoing + [small_twin]:
        copy.wait_send()
    for a in range(2):
        swap(a).wait_send()
        for n in range(7):
            spread(n, a).wait_send()
    for h in range(8):
        sum_twin(1 - k, h).wait_recv()
    for h in order:
        sum_twin(k, h).wait_send()


def written_kernel(done, grad_query, grad_key, levels, gains):
    grad_query[...] = done[0, :, :HD]
    grad_key[...] = done[1, :, :HD]
    tile = jnp.concatenate(
        [done[0, t, HD:] for t in range(2)] + [jnp.zeros((TOK - 16, TOK), F32)], axis=0
    ).T
    levels[...] = tile[:HEADS, :LEVELS]
    gains[...] = done[0, 2, HD:]


VM = pl.BlockSpec(memory_space=pltpu.VMEM)
SM = pl.BlockSpec(memory_space=pltpu.SMEM)
ANY = pl.BlockSpec(memory_space=pl.ANY)
DMA = pltpu.SemaphoreType.DMA


def shaped(shape, dtype=F32):
    return jax.ShapeDtypeStruct(shape, dtype)


def on_device(queries, key_vectors, value_vectors, log_gate, query_map, key_map, lw, norm_gain):
    matrix = pltpu.VMEM((HEADS, TOK, HD), F32)
    small = pltpu.VMEM((SMALL, TOK), F32)
    done = pl.pallas_call(
        whole_kernel,
        out_shape=shaped((2, HEADS, PIECE, HD)),
        in_specs=[ANY] * 6 + [SM, ANY],
        out_specs=VM,
        scratch_shapes=[
            pltpu.VMEM((TOK, HD), BF),
            pltpu.VMEM((TOK, HD), BF),
            pltpu.VMEM((HEADS, TOK), F32),
            pltpu.VMEM((HEADS, HD), F32),
            pltpu.VMEM((HEADS * TOK, HD), BF),
            matrix,
            matrix,
            pltpu.VMEM((SPANS, KEY_ROWS, HD), BF),
            pltpu.VMEM((SPANS, TOK, HD), BF),
            pltpu.VMEM((SPANS // 2, HEADS * TOK, 2 * TOK), F32),
            pltpu.VMEM((HEADS * TOK, TOK), F32),
            pltpu.VMEM((HEADS * TOK, TOK), F32),
            matrix,
            pltpu.VMEM((SPANS * GATE_ROWS, 2 * TOK), F32),
            pltpu.VMEM((SPANS, HEADS, TOK), F32),
            pltpu.VMEM((CROSS, HEADS, HD, HD), F32),
            *[matrix] * 12,
            pltpu.VMEM((2, HEADS, HD, HD), F32),
            matrix,
            pltpu.VMEM((HEADS, PIECE, HD), F32),
            pltpu.VMEM((7, PIECE, HD), F32),
            pltpu.VMEM((PIECE, HD), F32),
            pltpu.VMEM((PIECE, HD), F32),
            pltpu.VMEM((HEADS, 8, TOK), F32),
            small,
            small,
            small,
            DMA((14,)),
            DMA((2, 4)),
            DMA((2, 8)),
            DMA((2, 4)),
            DMA((2, 2, 3)),
            DMA((2, SPANS)),
            DMA((2, SPANS)),
            DMA((7,)),
            DMA((HEADS,)),
            DMA((8,)),
            DMA((8,)),
            DMA((2, 7)),
            DMA((2, 7)),
            DMA((2, 7)),
            DMA((8, 2)),
            DMA((8,)),
            DMA((8,)),
            DMA((2,)),
            DMA((2,)),
            DMA((2,)),
        ],
        compiler_params=pltpu.CompilerParams(
            collective_id=0, has_side_effects=True, vmem_limit_bytes=LIMIT
        ),
        name="distill",
    )(
        queries, key_vectors, value_vectors, log_gate, query_map, key_map, lw,
        norm_gain.reshape(HEADS, HD),
    )
    grad_query, grad_key, levels, gains = pl.pallas_call(
        written_kernel,
        out_shape=(
            shaped((HEADS, HD, HD)),
            shaped((HEADS, HD, HD)),
            shaped((HEADS, LEVELS)),
            shaped((HEADS, HD)),
        ),
        in_specs=[VM],
        out_specs=(VM,) * 4,
        name="written",
    )(done)
    return grad_query, grad_key, levels, gains.reshape(-1)


def solution(mesh):
    return jax.shard_map(
        on_device,
        mesh=mesh,
        in_specs=(
            P("seq", "head"),
            P("seq", "head"),
            P("seq", "head"),
            P("head", "seq"),
            P("head", None, None),
            P("head", None, None),
            P("head", None),
            P("head"),
        ),
        out_specs=(P("head", None, None), P("head", None, None), P("head", None), P("head")),
        check_vma=False,
    )
```

```python
import jax
import jax.numpy as jnp
from jax import lax
from jax.experimental import pallas as pl
from jax.experimental.pallas import tpu as pltpu
from jax.sharding import PartitionSpec as P

F32 = jnp.float32
BF = jnp.bfloat16
HIGHEST = lax.Precision.HIGHEST
MESH = pl.DeviceIdType.MESH
NEGATIVE = -1e30
EPSILON = 1e-05
HD = 128
TOK = 128
HEADS = 8
SPANS = 32
LEVELS = 13
LOW = 7
CROSS = 5
TOKENS = TOK * SPANS
WIDTH = 64 * HD
SMALL = 24
GATE_ROWS = 32
KEY_ROWS = 128 + GATE_ROWS
PIECE = 128 + 8
LOG2E = 1.4426950408889634
SCALE = HD**-0.5 * LOG2E
LIMIT = 50 << 20


def pieces(a):
    high = a.astype(BF)
    return high, (a - high.astype(F32)).astype(BF)


def dg(a, b, ca, cb, precision=None):
    return lax.dot_general(
        a, b, (((ca,), (cb,)), ((), ())), preferred_element_type=F32, precision=precision
    )


def halves(o):
    n = o.shape[1] // 2
    return o[:, :n] + o[:, n:]


def mm(a, b, ca, cb):
    bh, bl = pieces(b)
    left = jnp.concatenate(pieces(a), axis=ca)
    right = jnp.concatenate(
        [jnp.concatenate([bh, bh], axis=cb), jnp.concatenate([bl, bl], axis=cb)], axis=1 - cb
    )
    return halves(dg(left, right, ca, cb))


def mm_left_exact(a, b, ca, cb):
    return halves(dg(a, jnp.concatenate(pieces(b), axis=1 - cb), ca, cb))


def mm_right_exact(a, b, ca, cb):
    return dg(jnp.concatenate(pieces(a), axis=ca), jnp.concatenate([b, b], axis=cb), ca, cb)


def iota(shape, dim):
    return lax.broadcasted_iota(jnp.int32, shape, dim)


def local_levels():
    x = jnp.bitwise_xor(iota((TOK, TOK), 0), iota((TOK, TOK), 1))
    level = jnp.zeros_like(x)
    for bit in range(LOW):
        level = level + (x >= 1 << bit).astype(jnp.int32)
    return level


def rows(h):
    return slice(h * TOK, (h + 1) * TOK)


def column_cumulative(gates):
    lower = (iota((TOK, TOK), 1) <= iota((TOK, TOK), 0)).astype(F32)
    return dg(lower, gates, 1, 1, HIGHEST)


def pair_of(ref, p):
    return jnp.concatenate([ref[2 * p, :TOK], ref[2 * p + 1, :TOK]], axis=0)


def scored(c, p, masked, qs, keys_all, peak, score):
    keys = pair_of(keys_all, p)
    for h in range(HEADS):
        s = dg(qs[rows(h)], keys, 1, 1)
        if masked:
            place_of = 2 * TOK * p + iota((TOK, 2 * TOK), 1)
            s = jnp.where(place_of <= c * TOK + iota((TOK, 2 * TOK), 0), s, NEGATIVE)
        score[p, rows(h)] = s
        top = jnp.maximum(s[:, :TOK], s[:, TOK:])
        peak[rows(h)] = top if masked else jnp.maximum(peak[rows(h)], top)


def weighed(p, h, values, score, peak, total, tgt):
    s = score[p, rows(h)]
    top = peak[rows(h)]
    w0 = jnp.exp2((s[:, :TOK] - top) * SCALE)
    w1 = jnp.exp2((s[:, TOK:] - top) * SCALE)
    total[rows(h)] += w0 + w1
    tgt[h] += dg(jnp.concatenate([w0.astype(BF), w1.astype(BF)], axis=1), values, 1, 0)


def level_weights(c, keys_all, lc, weights):
    later = (iota((TOK, TOK), 0) > iota((TOK, TOK), 1)).astype(BF)
    both = jnp.concatenate([later, jnp.ones((TOK, TOK), BF)], axis=1)
    lc[...] = dg(keys_all[:, TOK:].reshape(SPANS * GATE_ROWS, TOK), both, 1, 0)

    def step(i, since):
        x = c - 1 - i
        three = lc[pl.ds(pl.multiple_of(x * GATE_ROWS, GATE_ROWS), 3 * HEADS)]
        own = three[:HEADS] + three[HEADS : 2 * HEADS] + three[2 * HEADS :]
        weights[x] = jnp.exp(since + own[:, :TOK])
        return since + own[:, TOK:]

    lax.fori_loop(0, c, step, jnp.zeros((HEADS, TOK), F32))


def gate_pieces(gate):
    high = gate.astype(BF).astype(F32)
    middle = (gate - high).astype(BF).astype(F32)
    low = gate - high - middle
    return jnp.concatenate([high, middle, low, jnp.zeros_like(gate)], axis=0).astype(BF)


def student_inside(qs, key, value, gate, wq, wk, lw, qp, kp, mix, sd, local):
    upper = (iota((TOK, TOK), 0) <= iota((TOK, TOK), 1)).astype(F32)
    row_cum = dg(gate, upper, 1, 0, HIGHEST)
    col_cum = column_cumulative(gate)
    causal = iota((TOK, TOK), 1) <= iota((TOK, TOK), 0)
    level = local_levels()
    for h in range(HEADS):
        qp[h] = mm_left_exact(qs[rows(h)], wq[h], 1, 0)
        kp[h] = mm_left_exact(key, wk[h], 1, 0)
    for h in range(HEADS):
        decay = jnp.exp(
            jnp.where(causal, col_cum[:, h : h + 1] - row_cum[h : h + 1], NEGATIVE)
        )
        mask = jnp.full((TOK, TOK), lw[h, 0], F32)
        for j in range(1, LOW + 1):
            mask = jnp.where(level == j, lw[h, j], mask)
        sd[h] = mm(qp[h], kp[h], 1, 1) * decay
        mix[h] = decay * mask
        local[h] = mm_right_exact(sd[h] * mask, value, 1, 0)


def student_whole(entry, wk, lw, gain, ls, tgt, qp, ks, comb, raw, local):
    for h in range(HEADS):
        combined = lw[h, LOW + 1] * ls[0, h]
        for j in range(1, CROSS):
            combined = combined + lw[h, LOW + 1 + j] * ls[j, h]
        comb[h] = combined
        ks[h] = mm(wk[h], combined, 0, 0)
    square = jnp.zeros((TOK, HD), F32)
    scaled = jnp.zeros((TOK, HD), F32)
    against = jnp.zeros((TOK, HD), F32)
    for h in range(HEADS):
        r = local[h] + entry[:, h : h + 1] * mm(qp[h], ks[h], 1, 0)
        raw[h] = r
        rg = r * gain[h : h + 1]
        square = square + r * r
        scaled = scaled + rg * rg
        against = against + tgt[h] * rg
    one = jnp.ones((8, HD), F32)
    tile = [dg(one, x, 1, 1, HIGHEST) for x in (square, scaled, against)]
    return jnp.concatenate([t[:1] for t in tile] + [tile[0][:5]], axis=0)


def backward_inside(
    all_sums, entry, value, wk, gain, ls, tgt, qp, kp, ks, mix, sd, raw, res, dstate, dquery, dkey
):
    eye = (iota((TOK, TOK), 0) == iota((TOK, TOK), 1)).astype(F32)
    level = local_levels()
    column = dg(eye, all_sums, 1, 1, HIGHEST)
    inverse = lax.rsqrt(column[:, 0:1] / WIDTH + EPSILON)
    inner = (inverse * column[:, 1:2] - column[:, 2:3]) / TOKENS
    back = inverse * inverse * inverse * inner / WIDTH
    gain_rows = []
    for h in range(HEADS):
        g = gain[h : h + 1]
        normed = raw[h] * inverse
        mismatch = (normed * g - tgt[h]) * (1.0 / TOKENS)
        gain_rows.append(jnp.sum(mismatch * normed, axis=0, keepdims=True))
        res[h] = inverse * (mismatch * g) - raw[h] * back
    lane = iota((16, TOK), 1)
    level_tile = jnp.zeros((16, TOK), F32)
    for h in range(HEADS):
        e = entry[:, h : h + 1]
        d_mix = mm_right_exact(res[h], value, 1, 1)
        d_scores = d_mix * mix[h]
        through = d_mix * sd[h]
        dstate[h] = mm(e * qp[h], res[h], 0, 0)
        d_comb = mm(wk[h], dstate[h], 1, 0)
        dquery[h] = mm(d_scores, kp[h], 1, 0) + e * mm(res[h], ks[h], 1, 1)
        dkey[h] = mm(d_scores, qp[h], 0, 0)
        lines = [
            jnp.sum(jnp.where(level == j, through, 0.0), axis=0, keepdims=True)
            for j in range(LOW + 1)
        ]
        lines += [jnp.sum(ls[j, h] * d_comb, axis=0, keepdims=True) for j in range(CROSS)]
        lines.append(jnp.zeros((16 - LEVELS, TOK), F32))
        summed = jnp.sum(jnp.concatenate(lines, axis=0), axis=1, keepdims=True)
        level_tile = jnp.where(lane == h, summed, level_tile)
    return jnp.concatenate([level_tile] + gain_rows, axis=0)


def at(y, z, k):
    return y * 16 + z * 2 + k


def remote(axis, src, dst, send, recv, target):
    return pltpu.make_async_remote_copy(
        src_ref=src, dst_ref=dst, send_sem=send, recv_sem=recv,
        device_id={axis: target}, device_id_type=MESH,
    )


def whole_kernel(
    q_hbm, k_hbm, v_hbm, g_hbm, wq_hbm, wk_hbm, lw, gain_hbm,
    done,
    k_ref, v_ref, g_ref, gain, qs, wq, wk, keys_all, vals, scores, peak, total, tgt, lc, weights, ls, qp, kp, ks, comb, mix, sd, raw, res, local,
    dstate, dquery, dkey, grads, pair, part, box, mine, far, sums_box, small_part, small_pair, small_sum,
    load, own_send, across_send, relay_send, onward_send, twin_send, recv, sums_send, sums_recv, pair_send, pair_recv,
    part_send, part_recv, done_send, done_recv, both_send, both_recv, small_sem, swap_send, swap_recv,
):
    c = lax.axis_index("seq")
    y, z, k = c // 16, c // 2 % 8, c % 2
    own_pair = c // 2
    second = y == 1
    twin, across = at(y, z, 1 - k), at(1 - y, z, k)
    me = lax.axis_index("head")
    head_peers = [(me + d) % HEADS for d in range(1, HEADS)]

    barrier = pltpu.get_barrier_semaphore()
    for target in [twin, across] + [at(y, (z + d) % 8, k) for d in (1, 2, 6, 7)]:
        pl.semaphore_signal(barrier, inc=1, device_id={"seq": target}, device_id_type=MESH)
    for peer in head_peers:
        pl.semaphore_signal(barrier, inc=1, device_id={"head": peer}, device_id_type=MESH)

    loads = [
        pltpu.make_async_copy(q_hbm.at[:, rows(h)], qs.at[rows(h)], load.at[h])
        for h in range(HEADS)
    ]
    loads.append(pltpu.make_async_copy(wq_hbm, wq, load.at[8]))
    loads.append(pltpu.make_async_copy(wk_hbm, wk, load.at[9]))
    own = ((k_hbm, k_ref), (v_hbm, v_ref), (g_hbm, g_ref), (gain_hbm, gain))
    first_loads = [pltpu.make_async_copy(a, b, load.at[10 + n]) for n, (a, b) in enumerate(own)]
    for copy in first_loads + loads:
        copy.start()
    for copy in first_loads:
        copy.wait()
    keys_all[c, :TOK] = k_ref[...]
    keys_all[c, TOK:] = gate_pieces(g_ref[...])
    vals[c] = v_ref[...]

    @pl.when(k == 0)
    def _():
        keys_all[c + 1] = jnp.zeros((KEY_ROWS, HD), BF)
        vals[c + 1] = jnp.zeros((TOK, HD), BF)

    for copy in loads:
        copy.wait()
    student_inside(
        qs, k_ref[...], v_ref[...], g_ref[...], wq, wk, lw, qp, kp, mix, sd, local
    )
    pl.semaphore_wait(barrier, 13)

    def block(phase, slot):
        return keys_all.at[slot] if phase == 0 else vals.at[slot]

    def copy_of(phase, slot, sem, target):
        ref = block(phase, slot)
        return remote("seq", ref, ref, sem, recv.at[phase, slot], target)

    def to_twin(phase, slot):
        return copy_of(phase, slot, twin_send.at[phase, slot], twin)

    def to_across(phase, zs):
        return copy_of(phase, at(0, zs, k), across_send.at[phase, zs], across)

    lean_core = 1 - 2 * k
    direct = (2, -2, 1, -1)

    def chip_at(o):
        return (z + 8 + lean_core * o) % 8

    def source_at(o):
        return (z + 8 - lean_core * o) % 8

    def need(zs, o):
        return (zs + 8 + lean_core * o) % 8 > zs

    def wanted(zs, o):
        if o == 2:
            return need(zs, 2) | need(zs, 3) | need(zs, 4)
        return need(zs, -2) | need(zs, -3) if o == -2 else need(zs, o)

    def to_row(phase, slot, sem, o):
        return copy_of(phase, slot, sem, at(y, chip_at(o), k))

    def act(when, copy, wait=False):
        @pl.when(when)
        def _():
            if wait:
                copy.wait_send()
            else:
                copy.start()

    row_first = (y == 0) & (k == 0)

    def own_moves(phase, wait=False):
        act(y == 0, to_across(phase, z), wait)
        act(k == 0, to_twin(phase, c), wait)
        for n, o in enumerate(direct):
            act(row_first | wanted(z, o), to_row(phase, c, own_send.at[phase, n], o), wait)

    def arrived(phase, slot):
        to_twin(phase, slot).wait_recv()

    def relay(phase, wait=False):
        @pl.when(second)
        def _():
            slot = at(0, z, k)
            if not wait:
                arrived(phase, slot)
            for n, o in enumerate(direct):
                act(k == 1, to_row(phase, slot, relay_send.at[phase, n], o), wait)
            act(second, to_twin(phase, slot), wait)

    def chip_of(i):
        far = jnp.where(i == 5, 3, jnp.where(i == 6, -3, 4))
        near = jnp.where(i == 1, 2, jnp.where(i == 2, -2, jnp.where(i == 3, 1, -1)))
        return source_at(jnp.where(i < 5, near, far))

    def onward(o):
        return ((0, 1), (1, 2)) if o == 2 else ((2, -1),) if o == -2 else ()

    def forward_own(phase, zs, o=0, wait=False):
        @pl.when(row_first | (wanted(zs, o) if o else zs < z))
        def _():
            slot = at(y, zs, k)
            if not wait:
                arrived(phase, slot)
            for n, step in onward(o):
                act(
                    row_first | need(zs, o + step),
                    to_row(phase, slot, onward_send.at[phase, 0, n], step),
                    wait,
                )
            act(row_first, to_across(phase, zs), wait)
            act(zs < z, to_twin(phase, slot), wait)

    def forward_other(phase, zs, o=0, wait=False):
        @pl.when(second)
        def _():
            slot = at(0, zs, k)
            if not wait:
                arrived(phase, slot)
            for n, step in onward(o):
                act(k == 1, to_row(phase, slot, onward_send.at[phase, 1, n], step), wait)
            act(second, to_twin(phase, slot), wait)

    def pairs(phase, i, use):
        zs = jnp.where(i == 0, z, chip_of(i))

        def one(other, carry):
            @pl.when((other == 0) & (zs < z) | (other == 1) & second)
            def _():
                ys = y * (1 - other)
                arrived(phase, at(ys, zs, 1 - k))
                use(ys * 8 + zs)

            return carry

        lax.fori_loop(0, 2, one, 0)

    own_moves(0)

    @pl.when(k == 1)
    def _():
        arrived(0, c - 1)

    scored(c, own_pair, True, qs, keys_all, peak, scores)
    relay(0)
    own_moves(1)
    relay(1)

    def score(p):
        scored(c, p, False, qs, keys_all, peak, scores)

    for o in (2, -2):
        forward_own(0, source_at(o), o)
    pairs(0, 0, score)
    for o in (2, -2):
        forward_other(0, source_at(o), o)

    def key_step(i, carry):
        @pl.when(i < 8)
        def _():
            forward_own(0, chip_of(i))
            forward_other(0, chip_of(i))

        pairs(0, i - 2, score)

        @pl.when(i == 5)
        def _():
            for o in (2, -2):
                forward_own(1, source_at(o), o)

        @pl.when(i == 7)
        def _():
            for o in (2, -2):
                forward_other(1, source_at(o), o)

        return carry

    lax.fori_loop(3, 10, key_step, 0)
    for h in range(HEADS):
        peak[rows(h)] = jnp.broadcast_to(
            jnp.max(peak[rows(h)], axis=1, keepdims=True), (TOK, TOK)
        )
    total[...] = jnp.zeros_like(total)
    tgt[...] = jnp.zeros_like(tgt)
    ls[...] = jnp.zeros_like(ls)
    level_weights(c, keys_all, lc, weights)

    @pl.when(k == 1)
    def _():
        arrived(1, c - 1)
        keys = keys_all[c - 1, :TOK].astype(F32).T
        for h in range(HEADS):
            ls[0, h] = mm_right_exact(keys * weights[c - 1, h : h + 1], vals[c - 1], 1, 0)

    for h in range(HEADS):
        weighed(own_pair, h, pair_of(vals, own_pair), scores, peak, total, tgt)

    def use_values(p):
        values = pair_of(vals, p)
        keys = pair_of(keys_all, p).astype(F32).T
        weight = jnp.concatenate([weights[2 * p], weights[2 * p + 1]], axis=1)
        j = jnp.int32(0)
        for b in range(4):
            j = j + (own_pair // (1 << b) != p // (1 << b)).astype(jnp.int32)
        for h in range(HEADS):
            weighed(p, h, values, scores, peak, total, tgt)
            ls[j, h] += mm_right_exact(keys * weight[h : h + 1], values, 1, 0)

    pairs(1, 0, use_values)

    def value_step(i, carry):
        @pl.when(i < 8)
        def _():
            forward_own(1, chip_of(i))
            forward_other(1, chip_of(i))

        pairs(1, i - 2, use_values)
        return carry

    lax.fori_loop(3, 10, value_step, 0)
    for h in range(HEADS):
        tgt[h] = tgt[h] / jnp.sum(total[rows(h)], axis=1, keepdims=True)
    entry = jnp.exp(column_cumulative(g_ref[...]))
    sums_box[me] = student_whole(entry, wk, lw, gain, ls, tgt, qp, ks, comb, raw, local)

    outgoing = [
        remote("head", sums_box.at[me], sums_box.at[me], sums_send.at[d], sums_recv.at[me], peer)
        for d, peer in enumerate(head_peers)
    ]
    for copy in outgoing:
        copy.start()
    for phase in range(2):
        own_moves(phase, True)

        relay(phase, True)
        for o in direct[:2]:
            forward_own(phase, source_at(o), o, True)
            forward_other(phase, source_at(o), o, True)

        def sent(i, carry, phase=phase):
            forward_own(phase, chip_of(i), 0, True)
            forward_other(phase, chip_of(i), 0, True)
            return carry

        lax.fori_loop(3, 8, sent, 0)
    for d, peer in enumerate(head_peers):
        remote(
            "head", sums_box.at[peer], sums_box.at[peer], sums_send.at[d], sums_recv.at[peer], peer
        ).wait_recv()
    all_sums = sums_box[0]
    for i in range(1, HEADS):
        all_sums = all_sums + sums_box[i]
    small_part[...] = backward_inside(
        all_sums, entry, v_ref[...], wk, gain, ls, tgt, qp, kp, ks, mix, sd, raw, res, dstate, dquery, dkey
    )

    small_twin = remote("seq", small_part, small_pair, small_sem.at[0], small_sem.at[1], twin)
    small_twin.start()
    order = [(z + d) % 8 for d in (4, 3, 5, 1, 7, 2, 6, 0)]

    def twin_part(h):
        return remote("seq", grads.at[1 - k, h], pair.at[h], pair_send.at[h], pair_recv.at[h], twin)

    def product(h):
        q_rows = qs[pl.ds(pl.multiple_of(h * TOK, TOK), TOK)]
        grads[0, h] = mm_left_exact(q_rows, dquery[h], 0, 0)
        grads[1, h] = mm(comb[h], dstate[h], 1, 1) + mm_left_exact(k_ref[...], dkey[h], 0, 0)

    def products(heads):
        for h in heads:
            product(h)
        for h in heads:
            twin_part(h).start()

    products(order[:3])
    products(order[3:6])
    small_twin.wait_recv()
    small_sum[...] = small_part[...] + small_pair[...]

    def lines(a):
        return pl.ds(0, 64) if a == 0 else pl.ds(64, PIECE - 64)

    def chip(d):
        return (z + 8 + d) % 8

    def piece(n, a):
        lean = 1 - 2 * a
        chunk, target = ((-4, -2), (-3, -1), (3, 1), (-1, -1), (1, 1), (-2, -2), (2, 2))[n]
        return remote(
            "seq", part.at[chip(lean * chunk), lines(a)], box.at[n, lines(a)], part_send.at[a, n],
            part_recv.at[a, n], at(y, chip(lean * target), k),
        )

    def ready(h):
        twin_part(h).wait_recv()
        tile = pl.multiple_of(h % 3 * 8, 8)
        part[h, :HD] = grads[k, h] + pair[h]
        part[h, HD:] = small_sum[pl.ds(tile, 8)]

    ready(order[0])
    for a in range(2):
        piece(0, a).start()
    ready(order[1])
    ready(order[2])
    for a in range(2):
        piece(1, a).start()
        piece(2, a).start()
    products(order[6:])
    ready(order[3])
    ready(order[4])
    for a in range(2):
        piece(3, a).start()
        piece(4, a).start()
    for h in order[5:]:
        ready(h)
    for h in order:
        twin_part(h).wait_send()
    for a in range(2):
        lean = 1 - 2 * a
        piece(0, a).wait_recv()
        piece(1, a).wait_recv()
        part[chip(-2 * lean), lines(a)] += box[0, lines(a)] + box[1, lines(a)]
        piece(5, a).start()
        piece(2, a).wait_recv()
        part[chip(2 * lean), lines(a)] += box[2, lines(a)]
        piece(6, a).start()

    def swap(a):
        return remote(
            "seq", mine.at[lines(a)], far.at[lines(a)], swap_send.at[a], swap_recv.at[a], across
        )

    for a in range(2):
        whole = part[z, lines(a)]
        for n in range(3, 7):
            piece(n, a).wait_recv()
            whole = whole + box[n, lines(a)]
        mine[lines(a)] = whole
        swap(a).start()
    for a in range(2):
        for n in range(7):
            piece(n, a).wait_send()

    def spread(n, a):
        lean = 1 - 2 * a
        source, target = ((0, 2), (0, -2), (0, 1), (0, -1), (-2, 1), (-2, 2), (2, -1))[n]
        h = chip(lean * source)
        ref = done.at[k, h, lines(a)]
        return remote(
            "seq", ref, ref, done_send.at[a, n], done_recv.at[h, a], at(y, chip(lean * target), k)
        )

    def came(d, a):
        h = chip(d)
        ref = done.at[k, h, lines(a)]
        return remote("seq", ref, ref, done_send.at[a, 0], done_recv.at[h, a], twin)

    def sum_twin(core, h):
        ref = done.at[core, h]
        return remote("seq", ref, ref, both_send.at[h], both_recv.at[h], twin)

    for a in range(2):
        swap(a).wait_recv()
        done[k, z, lines(a)] = mine[lines(a)] + far[lines(a)]
        for n in range(4):
            spread(n, a).start()
    sum_twin(k, z).start()
    for a in range(2):
        lean = 1 - 2 * a
        came(-2 * lean, a).wait_recv()
        spread(4, a).start()
        spread(5, a).start()
        came(2 * lean, a).wait_recv()
        spread(6, a).start()
    for d in (2, -2):
        sum_twin(k, chip(d)).start()
    for d in (1, -1, 3, -3, 4):
        for a in range(2):
            came(d, a).wait_recv()
        sum_twin(k, chip(d)).start()
    for copy in outgoing + [small_twin]:
        copy.wait_send()
    for a in range(2):
        swap(a).wait_send()
        for n in range(7):
            spread(n, a).wait_send()
    for h in range(8):
        sum_twin(1 - k, h).wait_recv()
    for h in order:
        sum_twin(k, h).wait_send()


def written_kernel(done, grad_query, grad_key, levels, gains):
    grad_query[...] = done[0, :, :HD]
    grad_key[...] = done[1, :, :HD]
    tile = jnp.concatenate(
        [done[0, t, HD:] for t in range(2)] + [jnp.zeros((TOK - 16, TOK), F32)], axis=0
    ).T
    levels[...] = tile[:HEADS, :LEVELS]
    gains[...] = done[0, 2, HD:]


VM = pl.BlockSpec(memory_space=pltpu.VMEM)
SM = pl.BlockSpec(memory_space=pltpu.SMEM)
ANY = pl.BlockSpec(memory_space=pl.ANY)
DMA = pltpu.SemaphoreType.DMA


def shaped(shape, dtype=F32):
    return jax.ShapeDtypeStruct(shape, dtype)


def on_device(queries, key_vectors, value_vectors, log_gate, query_map, key_map, lw, norm_gain):
    matrix = pltpu.VMEM((HEADS, TOK, HD), F32)
    small = pltpu.VMEM((SMALL, TOK), F32)
    done = pl.pallas_call(
        whole_kernel,
        out_shape=pltpu.VMEM((2, HEADS, PIECE, HD), F32),
        in_specs=[ANY] * 6 + [SM, ANY],
        out_specs=VM,
        scratch_shapes=[
            pltpu.VMEM((TOK, HD), BF),
            pltpu.VMEM((TOK, HD), BF),
            pltpu.VMEM((HEADS, TOK), F32),
            pltpu.VMEM((HEADS, HD), F32),
            pltpu.VMEM((HEADS * TOK, HD), BF),
            matrix,
            matrix,
            pltpu.VMEM((SPANS, KEY_ROWS, HD), BF),
            pltpu.VMEM((SPANS, TOK, HD), BF),
            pltpu.VMEM((SPANS // 2, HEADS * TOK, 2 * TOK), F32),
            pltpu.VMEM((HEADS * TOK, TOK), F32),
            pltpu.VMEM((HEADS * TOK, TOK), F32),
            matrix,
            pltpu.VMEM((SPANS * GATE_ROWS, 2 * TOK), F32),
            pltpu.VMEM((SPANS, HEADS, TOK), F32),
            pltpu.VMEM((CROSS, HEADS, HD, HD), F32),
            *[matrix] * 12,
            pltpu.VMEM((2, HEADS, HD, HD), F32),
            matrix,
            pltpu.VMEM((HEADS, PIECE, HD), F32),
            pltpu.VMEM((7, PIECE, HD), F32),
            pltpu.VMEM((PIECE, HD), F32),
            pltpu.VMEM((PIECE, HD), F32),
            pltpu.VMEM((HEADS, 8, TOK), F32),
            small,
            small,
            small,
            DMA((14,)),
            DMA((2, 4)),
            DMA((2, 8)),
            DMA((2, 4)),
            DMA((2, 2, 3)),
            DMA((2, SPANS)),
            DMA((2, SPANS)),
            DMA((7,)),
            DMA((HEADS,)),
            DMA((8,)),
            DMA((8,)),
            DMA((2, 7)),
            DMA((2, 7)),
            DMA((2, 7)),
            DMA((8, 2)),
            DMA((8,)),
            DMA((8,)),
            DMA((2,)),
            DMA((2,)),
            DMA((2,)),
        ],
        compiler_params=pltpu.CompilerParams(
            collective_id=0, has_side_effects=True, vmem_limit_bytes=LIMIT
        ),
        name="distill",
    )(
        queries, key_vectors, value_vectors, log_gate, query_map, key_map, lw,
        norm_gain.reshape(HEADS, HD),
    )
    grad_query, grad_key, levels, gains = pl.pallas_call(
        written_kernel,
        out_shape=(
            shaped((HEADS, HD, HD)),
            shaped((HEADS, HD, HD)),
            shaped((HEADS, LEVELS)),
            shaped((HEADS, HD)),
        ),
        in_specs=[VM],
        out_specs=(VM,) * 4,
        name="written",
    )(pltpu.with_memory_space_constraint(done, pltpu.VMEM))
    return grad_query, grad_key, levels, gains.reshape(-1)


def solution(mesh):
    return jax.shard_map(
        on_device,
        mesh=mesh,
        in_specs=(
            P("seq", "head"),
            P("seq", "head"),
            P("seq", "head"),
            P("head", "seq"),
            P("head", None, None),
            P("head", None, None),
            P("head", None),
            P("head"),
        ),
        out_specs=(P("head", None, None), P("head", None, None), P("head", None), P("head")),
        check_vma=False,
    )
```

```python
import jax
import jax.numpy as jnp
from jax import lax
from jax.experimental import pallas as pl
from jax.experimental.pallas import tpu as pltpu
from jax.sharding import PartitionSpec as P

F32 = jnp.float32
BF = jnp.bfloat16
HIGHEST = lax.Precision.HIGHEST
MESH = pl.DeviceIdType.MESH
NEGATIVE = -1e30
EPSILON = 1e-05
HD = 128
TOK = 128
HEADS = 8
SPANS = 32
LEVELS = 13
LOW = 7
CROSS = 5
TOKENS = TOK * SPANS
WIDTH = 64 * HD
SMALL = 24
GATE_ROWS = 32
KEY_ROWS = 128 + GATE_ROWS
PIECE = 128 + 8
LOG2E = 1.4426950408889634
SCALE = HD**-0.5 * LOG2E
LIMIT = 58 << 20


def pieces(a):
    high = a.astype(BF)
    return high, (a - high.astype(F32)).astype(BF)


def dg(a, b, ca, cb, precision=None):
    return lax.dot_general(
        a, b, (((ca,), (cb,)), ((), ())), preferred_element_type=F32, precision=precision
    )


def halves(o):
    n = o.shape[1] // 2
    return o[:, :n] + o[:, n:]


def mm(a, b, ca, cb):
    bh, bl = pieces(b)
    left = jnp.concatenate(pieces(a), axis=ca)
    right = jnp.concatenate(
        [jnp.concatenate([bh, bh], axis=cb), jnp.concatenate([bl, bl], axis=cb)], axis=1 - cb
    )
    return halves(dg(left, right, ca, cb))


def mm_left_exact(a, b, ca, cb):
    return halves(dg(a, jnp.concatenate(pieces(b), axis=1 - cb), ca, cb))


def mm_right_exact(a, b, ca, cb):
    return dg(jnp.concatenate(pieces(a), axis=ca), jnp.concatenate([b, b], axis=cb), ca, cb)


def iota(shape, dim):
    return lax.broadcasted_iota(jnp.int32, shape, dim)


def local_levels():
    x = jnp.bitwise_xor(iota((TOK, TOK), 0), iota((TOK, TOK), 1))
    level = jnp.zeros_like(x)
    for bit in range(LOW):
        level = level + (x >= 1 << bit).astype(jnp.int32)
    return level


def rows(h):
    return slice(h * TOK, (h + 1) * TOK)


def column_cumulative(gates):
    lower = (iota((TOK, TOK), 1) <= iota((TOK, TOK), 0)).astype(F32)
    return dg(lower, gates, 1, 1, HIGHEST)


def pair_of(ref, p):
    return jnp.concatenate([ref[2 * p, :TOK], ref[2 * p + 1, :TOK]], axis=0)


def scored(c, p, masked, qs, keys_all, peak, score):
    keys = pair_of(keys_all, p)
    for h in range(HEADS):
        s = dg(qs[rows(h)], keys, 1, 1)
        if masked:
            place_of = 2 * TOK * p + iota((TOK, 2 * TOK), 1)
            s = jnp.where(place_of <= c * TOK + iota((TOK, 2 * TOK), 0), s, NEGATIVE)
        score[p, rows(h)] = s
        top = jnp.maximum(s[:, :TOK], s[:, TOK:])
        peak[rows(h)] = top if masked else jnp.maximum(peak[rows(h)], top)


def weighed(p, h, values, score, peak, total, tgt):
    s = score[p, rows(h)]
    top = peak[rows(h)]
    w0 = jnp.exp2((s[:, :TOK] - top) * SCALE)
    w1 = jnp.exp2((s[:, TOK:] - top) * SCALE)
    total[rows(h)] += w0 + w1
    tgt[h] += dg(jnp.concatenate([w0.astype(BF), w1.astype(BF)], axis=1), values, 1, 0)


def level_weights(c, keys_all, lc, weights):
    later = (iota((TOK, TOK), 0) > iota((TOK, TOK), 1)).astype(BF)
    both = jnp.concatenate([later, jnp.ones((TOK, TOK), BF)], axis=1)
    lc[...] = dg(keys_all[:, TOK:].reshape(SPANS * GATE_ROWS, TOK), both, 1, 0)

    def step(i, since):
        x = c - 1 - i
        three = lc[pl.ds(pl.multiple_of(x * GATE_ROWS, GATE_ROWS), 3 * HEADS)]
        own = three[:HEADS] + three[HEADS : 2 * HEADS] + three[2 * HEADS :]
        weights[x] = jnp.exp(since + own[:, :TOK])
        return since + own[:, TOK:]

    lax.fori_loop(0, c, step, jnp.zeros((HEADS, TOK), F32))


def gate_pieces(gate):
    high = gate.astype(BF).astype(F32)
    middle = (gate - high).astype(BF).astype(F32)
    low = gate - high - middle
    return jnp.concatenate([high, middle, low, jnp.zeros_like(gate)], axis=0).astype(BF)


def student_inside(qs, key, value, gate, wq, wk, lw, qp, kp, mix, sd, local):
    upper = (iota((TOK, TOK), 0) <= iota((TOK, TOK), 1)).astype(F32)
    row_cum = dg(gate, upper, 1, 0, HIGHEST)
    col_cum = column_cumulative(gate)
    causal = iota((TOK, TOK), 1) <= iota((TOK, TOK), 0)
    level = local_levels()
    for h in range(HEADS):
        qp[h] = mm_left_exact(qs[rows(h)], wq[h], 1, 0)
        kp[h] = mm_left_exact(key, wk[h], 1, 0)
    for h in range(HEADS):
        decay = jnp.exp(
            jnp.where(causal, col_cum[:, h : h + 1] - row_cum[h : h + 1], NEGATIVE)
        )
        mask = jnp.full((TOK, TOK), lw[h, 0], F32)
        for j in range(1, LOW + 1):
            mask = jnp.where(level == j, lw[h, j], mask)
        sd[h] = mm(qp[h], kp[h], 1, 1) * decay
        mix[h] = decay * mask
        local[h] = mm_right_exact(sd[h] * mask, value, 1, 0)


def student_whole(entry, wk, lw, gain, ls, tgt, qp, ks, comb, raw, local):
    for h in range(HEADS):
        combined = lw[h, LOW + 1] * ls[0, h]
        for j in range(1, CROSS):
            combined = combined + lw[h, LOW + 1 + j] * ls[j, h]
        comb[h] = combined
        ks[h] = mm(wk[h], combined, 0, 0)
    square = jnp.zeros((TOK, HD), F32)
    scaled = jnp.zeros((TOK, HD), F32)
    against = jnp.zeros((TOK, HD), F32)
    for h in range(HEADS):
        r = local[h] + entry[:, h : h + 1] * mm(qp[h], ks[h], 1, 0)
        raw[h] = r
        rg = r * gain[h : h + 1]
        square = square + r * r
        scaled = scaled + rg * rg
        against = against + tgt[h] * rg
    one = jnp.ones((8, HD), F32)
    tile = [dg(one, x, 1, 1, HIGHEST) for x in (square, scaled, against)]
    return jnp.concatenate([t[:1] for t in tile] + [tile[0][:5]], axis=0)


def backward_inside(
    all_sums, entry, value, wk, gain, ls, tgt, qp, kp, ks, mix, sd, raw, res, dstate, dquery, dkey
):
    eye = (iota((TOK, TOK), 0) == iota((TOK, TOK), 1)).astype(F32)
    level = local_levels()
    column = dg(eye, all_sums, 1, 1, HIGHEST)
    inverse = lax.rsqrt(column[:, 0:1] / WIDTH + EPSILON)
    inner = (inverse * column[:, 1:2] - column[:, 2:3]) / TOKENS
    back = inverse * inverse * inverse * inner / WIDTH
    gain_rows = []
    for h in range(HEADS):
        g = gain[h : h + 1]
        normed = raw[h] * inverse
        mismatch = (normed * g - tgt[h]) * (1.0 / TOKENS)
        gain_rows.append(jnp.sum(mismatch * normed, axis=0, keepdims=True))
        res[h] = inverse * (mismatch * g) - raw[h] * back
    lane = iota((16, TOK), 1)
    level_tile = jnp.zeros((16, TOK), F32)
    for h in range(HEADS):
        e = entry[:, h : h + 1]
        d_mix = mm_right_exact(res[h], value, 1, 1)
        d_scores = d_mix * mix[h]
        through = d_mix * sd[h]
        dstate[h] = mm(e * qp[h], res[h], 0, 0)
        d_comb = mm(wk[h], dstate[h], 1, 0)
        dquery[h] = mm(d_scores, kp[h], 1, 0) + e * mm(res[h], ks[h], 1, 1)
        dkey[h] = mm(d_scores, qp[h], 0, 0)
        lines = [
            jnp.sum(jnp.where(level == j, through, 0.0), axis=0, keepdims=True)
            for j in range(LOW + 1)
        ]
        lines += [jnp.sum(ls[j, h] * d_comb, axis=0, keepdims=True) for j in range(CROSS)]
        lines.append(jnp.zeros((16 - LEVELS, TOK), F32))
        summed = jnp.sum(jnp.concatenate(lines, axis=0), axis=1, keepdims=True)
        level_tile = jnp.where(lane == h, summed, level_tile)
    return jnp.concatenate([level_tile] + gain_rows, axis=0)


def at(y, z, k):
    return y * 16 + z * 2 + k


def remote(axis, src, dst, send, recv, target):
    return pltpu.make_async_remote_copy(
        src_ref=src, dst_ref=dst, send_sem=send, recv_sem=recv,
        device_id={axis: target}, device_id_type=MESH,
    )


def whole_kernel(
    q_hbm, k_hbm, v_hbm, g_hbm, wq_hbm, wk_hbm, lw, gain_hbm,
    done,
    k_ref, v_ref, g_ref, gain, qs, wq, wk, keys_all, vals, scores, peak, total, tgt, lc, weights, ls, qp, kp, ks, comb, mix, sd, raw, res, local,
    dstate, dquery, dkey, grads, pair, part, box, mine, far, sums_box, small_part, small_pair, small_sum,
    load, own_send, across_send, relay_send, onward_send, twin_send, recv, sums_send, sums_recv, pair_send, pair_recv,
    part_send, part_recv, done_send, done_recv, both_send, both_recv, small_sem, swap_send, swap_recv,
):
    c = lax.axis_index("seq")
    y, z, k = c // 16, c // 2 % 8, c % 2
    own_pair = c // 2
    second = y == 1
    twin, across = at(y, z, 1 - k), at(1 - y, z, k)
    me = lax.axis_index("head")
    head_peers = [(me + d) % HEADS for d in range(1, HEADS)]

    barrier = pltpu.get_barrier_semaphore()
    for target in [twin, across] + [at(y, (z + d) % 8, k) for d in (1, 2, 6, 7)]:
        pl.semaphore_signal(barrier, inc=1, device_id={"seq": target}, device_id_type=MESH)
    for peer in head_peers:
        pl.semaphore_signal(barrier, inc=1, device_id={"head": peer}, device_id_type=MESH)

    loads = [
        pltpu.make_async_copy(q_hbm.at[:, rows(h)], qs.at[rows(h)], load.at[h])
        for h in range(HEADS)
    ]
    loads.append(pltpu.make_async_copy(wq_hbm, wq, load.at[8]))
    loads.append(pltpu.make_async_copy(wk_hbm, wk, load.at[9]))
    own = ((k_hbm, k_ref), (v_hbm, v_ref), (g_hbm, g_ref), (gain_hbm, gain))
    first_loads = [pltpu.make_async_copy(a, b, load.at[10 + n]) for n, (a, b) in enumerate(own)]
    for copy in first_loads + loads:
        copy.start()
    for copy in first_loads:
        copy.wait()
    keys_all[c, :TOK] = k_ref[...]
    keys_all[c, TOK:] = gate_pieces(g_ref[...])
    vals[c] = v_ref[...]

    @pl.when(k == 0)
    def _():
        keys_all[c + 1] = jnp.zeros((KEY_ROWS, HD), BF)
        vals[c + 1] = jnp.zeros((TOK, HD), BF)

    for copy in loads:
        copy.wait()
    student_inside(
        qs, k_ref[...], v_ref[...], g_ref[...], wq, wk, lw, qp, kp, mix, sd, local
    )
    pl.semaphore_wait(barrier, 13)

    def block(phase, slot):
        return keys_all.at[slot] if phase == 0 else vals.at[slot]

    def copy_of(phase, slot, sem, target):
        ref = block(phase, slot)
        return remote("seq", ref, ref, sem, recv.at[phase, slot], target)

    def to_twin(phase, slot):
        return copy_of(phase, slot, twin_send.at[phase, slot], twin)

    def to_across(phase, zs):
        return copy_of(phase, at(0, zs, k), across_send.at[phase, zs], across)

    lean_core = 1 - 2 * k
    direct = (2, -2, 1, -1)

    def chip_at(o):
        return (z + 8 + lean_core * o) % 8

    def source_at(o):
        return (z + 8 - lean_core * o) % 8

    def need(zs, o):
        return (zs + 8 + lean_core * o) % 8 > zs

    def wanted(zs, o):
        if o == 2:
            return need(zs, 2) | need(zs, 3) | need(zs, 4)
        return need(zs, -2) | need(zs, -3) if o == -2 else need(zs, o)

    def to_row(phase, slot, sem, o):
        return copy_of(phase, slot, sem, at(y, chip_at(o), k))

    def act(when, copy, wait=False):
        @pl.when(when)
        def _():
            if wait:
                copy.wait_send()
            else:
                copy.start()

    row_first = (y == 0) & (k == 0)

    def own_moves(phase, wait=False):
        act(y == 0, to_across(phase, z), wait)
        act(k == 0, to_twin(phase, c), wait)
        for n, o in enumerate(direct):
            act(row_first | wanted(z, o), to_row(phase, c, own_send.at[phase, n], o), wait)

    def arrived(phase, slot):
        to_twin(phase, slot).wait_recv()

    def relay(phase, wait=False):
        @pl.when(second)
        def _():
            slot = at(0, z, k)
            if not wait:
                arrived(phase, slot)
            for n, o in enumerate(direct):
                act(k == 1, to_row(phase, slot, relay_send.at[phase, n], o), wait)
            act(second, to_twin(phase, slot), wait)

    def chip_of(i):
        far = jnp.where(i == 5, 3, jnp.where(i == 6, -3, 4))
        near = jnp.where(i == 1, 2, jnp.where(i == 2, -2, jnp.where(i == 3, 1, -1)))
        return source_at(jnp.where(i < 5, near, far))

    def onward(o):
        return ((0, 1), (1, 2)) if o == 2 else ((2, -1),) if o == -2 else ()

    def forward_own(phase, zs, o=0, wait=False):
        @pl.when(row_first | (wanted(zs, o) if o else zs < z))
        def _():
            slot = at(y, zs, k)
            if not wait:
                arrived(phase, slot)
            for n, step in onward(o):
                act(
                    row_first | need(zs, o + step),
                    to_row(phase, slot, onward_send.at[phase, 0, n], step),
                    wait,
                )
            act(row_first, to_across(phase, zs), wait)
            act(zs < z, to_twin(phase, slot), wait)

    def forward_other(phase, zs, o=0, wait=False):
        @pl.when(second)
        def _():
            slot = at(0, zs, k)
            if not wait:
                arrived(phase, slot)
            for n, step in onward(o):
                act(k == 1, to_row(phase, slot, onward_send.at[phase, 1, n], step), wait)
            act(second, to_twin(phase, slot), wait)

    def pairs(phase, i, use):
        zs = jnp.where(i == 0, z, chip_of(i))

        def one(other, carry):
            @pl.when((other == 0) & (zs < z) | (other == 1) & second)
            def _():
                ys = y * (1 - other)
                arrived(phase, at(ys, zs, 1 - k))
                use(ys * 8 + zs)

            return carry

        lax.fori_loop(0, 2, one, 0)

    own_moves(0)

    @pl.when(k == 1)
    def _():
        arrived(0, c - 1)

    scored(c, own_pair, True, qs, keys_all, peak, scores)
    relay(0)
    own_moves(1)
    relay(1)

    def score(p):
        scored(c, p, False, qs, keys_all, peak, scores)

    for o in (2, -2):
        forward_own(0, source_at(o), o)
    pairs(0, 0, score)
    for o in (2, -2):
        forward_other(0, source_at(o), o)

    def key_step(i, carry):
        @pl.when(i < 8)
        def _():
            forward_own(0, chip_of(i))
            forward_other(0, chip_of(i))

        pairs(0, i - 2, score)

        @pl.when(i == 5)
        def _():
            for o in (2, -2):
                forward_own(1, source_at(o), o)

        @pl.when(i == 7)
        def _():
            for o in (2, -2):
                forward_other(1, source_at(o), o)

        return carry

    lax.fori_loop(3, 10, key_step, 0)
    for h in range(HEADS):
        peak[rows(h)] = jnp.broadcast_to(
            jnp.max(peak[rows(h)], axis=1, keepdims=True), (TOK, TOK)
        )
    total[...] = jnp.zeros_like(total)
    tgt[...] = jnp.zeros_like(tgt)
    ls[...] = jnp.zeros_like(ls)
    level_weights(c, keys_all, lc, weights)

    @pl.when(k == 1)
    def _():
        arrived(1, c - 1)
        keys = keys_all[c - 1, :TOK].astype(F32).T
        for h in range(HEADS):
            ls[0, h] = mm_right_exact(keys * weights[c - 1, h : h + 1], vals[c - 1], 1, 0)

    for h in range(HEADS):
        weighed(own_pair, h, pair_of(vals, own_pair), scores, peak, total, tgt)

    def use_values(p):
        values = pair_of(vals, p)
        keys = pair_of(keys_all, p).astype(F32).T
        weight = jnp.concatenate([weights[2 * p], weights[2 * p + 1]], axis=1)
        j = jnp.int32(0)
        for b in range(4):
            j = j + (own_pair // (1 << b) != p // (1 << b)).astype(jnp.int32)
        for h in range(HEADS):
            weighed(p, h, values, scores, peak, total, tgt)
            ls[j, h] += mm_right_exact(keys * weight[h : h + 1], values, 1, 0)

    pairs(1, 0, use_values)

    def value_step(i, carry):
        @pl.when(i < 8)
        def _():
            forward_own(1, chip_of(i))
            forward_other(1, chip_of(i))

        pairs(1, i - 2, use_values)
        return carry

    lax.fori_loop(3, 10, value_step, 0)
    for h in range(HEADS):
        tgt[h] = tgt[h] / jnp.sum(total[rows(h)], axis=1, keepdims=True)
    entry = jnp.exp(column_cumulative(g_ref[...]))
    sums_box[me] = student_whole(entry, wk, lw, gain, ls, tgt, qp, ks, comb, raw, local)

    outgoing = [
        remote("head", sums_box.at[me], sums_box.at[me], sums_send.at[d], sums_recv.at[me], peer)
        for d, peer in enumerate(head_peers)
    ]
    for copy in outgoing:
        copy.start()
    for phase in range(2):
        own_moves(phase, True)

        relay(phase, True)
        for o in direct[:2]:
            forward_own(phase, source_at(o), o, True)
            forward_other(phase, source_at(o), o, True)

        def sent(i, carry, phase=phase):
            forward_own(phase, chip_of(i), 0, True)
            forward_other(phase, chip_of(i), 0, True)
            return carry

        lax.fori_loop(3, 8, sent, 0)
    for d, peer in enumerate(head_peers):
        remote(
            "head", sums_box.at[peer], sums_box.at[peer], sums_send.at[d], sums_recv.at[peer], peer
        ).wait_recv()
    all_sums = sums_box[0]
    for i in range(1, HEADS):
        all_sums = all_sums + sums_box[i]
    small_part[...] = backward_inside(
        all_sums, entry, v_ref[...], wk, gain, ls, tgt, qp, kp, ks, mix, sd, raw, res, dstate, dquery, dkey
    )

    small_twin = remote("seq", small_part, small_pair, small_sem.at[0], small_sem.at[1], twin)
    small_twin.start()
    order = [(z + d) % 8 for d in (4, 3, 5, 1, 7, 2, 6, 0)]

    def twin_part(h):
        return remote("seq", grads.at[1 - k, h], pair.at[h], pair_send.at[h], pair_recv.at[h], twin)

    def product(h):
        q_rows = qs[pl.ds(pl.multiple_of(h * TOK, TOK), TOK)]
        grads[0, h] = mm_left_exact(q_rows, dquery[h], 0, 0)
        grads[1, h] = mm(comb[h], dstate[h], 1, 1) + mm_left_exact(k_ref[...], dkey[h], 0, 0)

    def products(heads):
        for h in heads:
            product(h)
        for h in heads:
            twin_part(h).start()

    products(order[:3])
    products(order[3:6])
    small_twin.wait_recv()
    small_sum[...] = small_part[...] + small_pair[...]

    def lines(a):
        return pl.ds(0, 64) if a == 0 else pl.ds(64, PIECE - 64)

    def chip(d):
        return (z + 8 + d) % 8

    def piece(n, a):
        lean = 1 - 2 * a
        chunk, target = ((-4, -2), (-3, -1), (3, 1), (-1, -1), (1, 1), (-2, -2), (2, 2))[n]
        return remote(
            "seq", part.at[chip(lean * chunk), lines(a)], box.at[n, lines(a)], part_send.at[a, n],
            part_recv.at[a, n], at(y, chip(lean * target), k),
        )

    def ready(h):
        twin_part(h).wait_recv()
        tile = pl.multiple_of(h % 3 * 8, 8)
        part[h, :HD] = grads[k, h] + pair[h]
        part[h, HD:] = small_sum[pl.ds(tile, 8)]

    ready(order[0])
    for a in range(2):
        piece(0, a).start()
    ready(order[1])
    ready(order[2])
    for a in range(2):
        piece(1, a).start()
        piece(2, a).start()
    products(order[6:])
    ready(order[3])
    ready(order[4])
    for a in range(2):
        piece(3, a).start()
        piece(4, a).start()
    for h in order[5:]:
        ready(h)
    for h in order:
        twin_part(h).wait_send()
    for a in range(2):
        lean = 1 - 2 * a
        piece(0, a).wait_recv()
        piece(1, a).wait_recv()
        part[chip(-2 * lean), lines(a)] += box[0, lines(a)] + box[1, lines(a)]
        piece(5, a).start()
        piece(2, a).wait_recv()
        part[chip(2 * lean), lines(a)] += box[2, lines(a)]
        piece(6, a).start()

    def swap(a):
        return remote(
            "seq", mine.at[lines(a)], far.at[lines(a)], swap_send.at[a], swap_recv.at[a], across
        )

    for a in range(2):
        whole = part[z, lines(a)]
        for n in range(3, 7):
            piece(n, a).wait_recv()
            whole = whole + box[n, lines(a)]
        mine[lines(a)] = whole
        swap(a).start()
    for a in range(2):
        for n in range(7):
            piece(n, a).wait_send()

    def spread(n, a):
        lean = 1 - 2 * a
        source, target = ((0, 2), (0, -2), (0, 1), (0, -1), (-2, 1), (-2, 2), (2, -1))[n]
        h = chip(lean * source)
        ref = done.at[k, h, lines(a)]
        return remote(
            "seq", ref, ref, done_send.at[a, n], done_recv.at[h, a], at(y, chip(lean * target), k)
        )

    def came(d, a):
        h = chip(d)
        ref = done.at[k, h, lines(a)]
        return remote("seq", ref, ref, done_send.at[a, 0], done_recv.at[h, a], twin)

    def sum_twin(core, h):
        ref = done.at[core, h]
        return remote("seq", ref, ref, both_send.at[h], both_recv.at[h], twin)

    for a in range(2):
        swap(a).wait_recv()
        done[k, z, lines(a)] = mine[lines(a)] + far[lines(a)]
        for n in range(4):
            spread(n, a).start()
    sum_twin(k, z).start()
    for a in range(2):
        lean = 1 - 2 * a
        came(-2 * lean, a).wait_recv()
        spread(4, a).start()
        spread(5, a).start()
        came(2 * lean, a).wait_recv()
        spread(6, a).start()
    for d in (2, -2):
        sum_twin(k, chip(d)).start()
    for d in (1, -1, 3, -3, 4):
        for a in range(2):
            came(d, a).wait_recv()
        sum_twin(k, chip(d)).start()
    for copy in outgoing + [small_twin]:
        copy.wait_send()
    for a in range(2):
        swap(a).wait_send()
        for n in range(7):
            spread(n, a).wait_send()
    for h in range(8):
        sum_twin(1 - k, h).wait_recv()
    for h in order:
        sum_twin(k, h).wait_send()


def written_kernel(done, grad_query, grad_key, levels, gains):
    grad_query[...] = done[0, :, :HD]
    grad_key[...] = done[1, :, :HD]
    tile = jnp.concatenate(
        [done[0, t, HD:] for t in range(2)] + [jnp.zeros((TOK - 16, TOK), F32)], axis=0
    ).T
    levels[...] = tile[:HEADS, :LEVELS]
    gains[...] = done[0, 2, HD:]


VM = pl.BlockSpec(memory_space=pltpu.VMEM)
SM = pl.BlockSpec(memory_space=pltpu.SMEM)
ANY = pl.BlockSpec(memory_space=pl.ANY)
DMA = pltpu.SemaphoreType.DMA


def shaped(shape, dtype=F32):
    return jax.ShapeDtypeStruct(shape, dtype)


def on_device(queries, key_vectors, value_vectors, log_gate, query_map, key_map, lw, norm_gain):
    matrix = pltpu.VMEM((HEADS, TOK, HD), F32)
    small = pltpu.VMEM((SMALL, TOK), F32)
    done = pl.pallas_call(
        whole_kernel,
        out_shape=pltpu.VMEM((2, HEADS, PIECE, HD), F32),
        in_specs=[ANY] * 6 + [SM, ANY],
        out_specs=VM,
        scratch_shapes=[
            pltpu.VMEM((TOK, HD), BF),
            pltpu.VMEM((TOK, HD), BF),
            pltpu.VMEM((HEADS, TOK), F32),
            pltpu.VMEM((HEADS, HD), F32),
            pltpu.VMEM((HEADS * TOK, HD), BF),
            matrix,
            matrix,
            pltpu.VMEM((SPANS, KEY_ROWS, HD), BF),
            pltpu.VMEM((SPANS, TOK, HD), BF),
            pltpu.VMEM((SPANS // 2, HEADS * TOK, 2 * TOK), F32),
            pltpu.VMEM((HEADS * TOK, TOK), F32),
            pltpu.VMEM((HEADS * TOK, TOK), F32),
            matrix,
            pltpu.VMEM((SPANS * GATE_ROWS, 2 * TOK), F32),
            pltpu.VMEM((SPANS, HEADS, TOK), F32),
            pltpu.VMEM((CROSS, HEADS, HD, HD), F32),
            *[matrix] * 12,
            pltpu.VMEM((2, HEADS, HD, HD), F32),
            matrix,
            pltpu.VMEM((HEADS, PIECE, HD), F32),
            pltpu.VMEM((7, PIECE, HD), F32),
            pltpu.VMEM((PIECE, HD), F32),
            pltpu.VMEM((PIECE, HD), F32),
            pltpu.VMEM((HEADS, 8, TOK), F32),
            small,
            small,
            small,
            DMA((14,)),
            DMA((2, 4)),
            DMA((2, 8)),
            DMA((2, 4)),
            DMA((2, 2, 3)),
            DMA((2, SPANS)),
            DMA((2, SPANS)),
            DMA((7,)),
            DMA((HEADS,)),
            DMA((8,)),
            DMA((8,)),
            DMA((2, 7)),
            DMA((2, 7)),
            DMA((2, 7)),
            DMA((8, 2)),
            DMA((8,)),
            DMA((8,)),
            DMA((2,)),
            DMA((2,)),
            DMA((2,)),
        ],
        compiler_params=pltpu.CompilerParams(
            collective_id=0, has_side_effects=True, vmem_limit_bytes=LIMIT
        ),
        name="distill",
    )(
        queries, key_vectors, value_vectors, log_gate, query_map, key_map, lw,
        norm_gain.reshape(HEADS, HD),
    )
    grad_query, grad_key, levels, gains = pl.pallas_call(
        written_kernel,
        out_shape=(
            shaped((HEADS, HD, HD)),
            shaped((HEADS, HD, HD)),
            shaped((HEADS, LEVELS)),
            shaped((HEADS, HD)),
        ),
        in_specs=[VM],
        out_specs=(VM,) * 4,
        name="written",
    )(pltpu.with_memory_space_constraint(done, pltpu.VMEM))
    return grad_query, grad_key, levels, gains.reshape(-1)


def solution(mesh):
    return jax.shard_map(
        on_device,
        mesh=mesh,
        in_specs=(
            P("seq", "head"),
            P("seq", "head"),
            P("seq", "head"),
            P("head", "seq"),
            P("head", None, None),
            P("head", None, None),
            P("head", None),
            P("head"),
        ),
        out_specs=(P("head", None, None), P("head", None, None), P("head", None), P("head")),
        check_vma=False,
    )
```
